32 devices in a mesh: batch: 1, wide: 32 (over z, y, x, core).
Axes of the slice: x: 2, y: 2, z: 4, core: 2. Of those that a mesh axis runs over, the one named last changes fastest.
Arguments:
- features: bfloat16 [64, 64, 1, 1024], P('wide', None, 'batch'), may hold values from -6 to 6
- conv_weight: bfloat16 [3, 3, 32, 1024], replicated, may hold values from -0.375 to 0.375
- proj_weight: bfloat16 [1024, 128], replicated, may hold values from -0.1875 to 0.1875
- anchor_pixel: int32 [512, 1], P('wide', 'batch'), may hold values from 0 to 127
- positive_pixel: int32 [512, 1], P('wide', 'batch'), may hold values from 0 to 4095
Outputs:
- grad_features: bfloat16 [64, 64, 1, 1024], P('wide', None, 'batch')
- grad_conv: float32 [3, 3, 32, 1024], replicated
- grad_proj: float32 [1024, 128], replicated
- loss_value: float32 [], replicated
The draws below stay inside these ranges and needn't reach their ends.
Inputs may be any that keep to these rules, and one draw needn't show every extreme that they name: anchor_pixel[n, b] names a pixel of row tile n // 16. positive_pixel names a pixel of the same image as the anchor.
All inputs are finite; a program needn't handle non-finite values.
Results may differ from the reference program's by a relative error of at most 0.01.
Values may be sent and summed in bfloat16 or wider, within the bound.
A program may use at most 64 MiB of HBM per device.

```python
import jax
import jax.numpy as jnp
from jax import lax

CH = 1024
KEY = 128
W = 64
ANCH = 16
ROWS_DEV = 2
GW = 32
H = 64
B = 1
ANCHORS = 512


def place_ends(values, stream_key, least, top_value):
    place = [jax.random.randint(jax.random.fold_in(stream_key, axis), (), 0, length) for axis, length in enumerate(values.shape)]
    widest = values.shape.index(max(values.shape))
    neighbour = place[:widest] + [(place[widest] + 1) % values.shape[widest]] + place[widest + 1:]
    return values.at[tuple(place)].set(least).at[tuple(neighbour)].set(top_value)


def block_levels(stream_key, shape, pieces, low, largest):
    def one(dim, parts):
        draws = jax.random.uniform(jax.random.fold_in(jax.random.fold_in(stream_key, 6), dim), (parts,), jnp.float32, low / len(pieces), largest / len(pieces))
        return jnp.repeat(jnp.exp(draws), shape[dim] // parts).reshape((-1,) + (1,) * (len(shape) - dim - 1))

    loudness = one(*pieces[0])
    for cut in pieces[1:]:
        loudness = loudness * one(*cut)
    return loudness


def centred(own_key, dims, scale, limit, pieces=(), kind=jnp.bfloat16):
    result = jax.random.normal(own_key, dims, jnp.float32) * scale
    if len(pieces) > 0:
        result = block_levels(own_key, dims, pieces, -0.22, 0.18) * result
    return jnp.clip(result, min=-limit, max=limit).astype(kind)


def setup_inputs(seed: int = 0) -> dict:
    key_of = jax.random.split(jax.random.key(seed), 6)
    features = centred(key_of[0], (H, W, B, CH), 1.0, 6.0, ((0, 32),))
    conv_weight = centred(key_of[1], (3, 3, GW, CH), (9 * GW) ** -0.5, 0.375)
    proj_weight = centred(key_of[2], (CH, KEY), CH ** -0.5, 0.1875)
    anchor_pixel = place_ends(jax.random.randint(key_of[3], (ANCHORS, B), 0, ROWS_DEV * W), jax.random.fold_in(key_of[3], 1), 0, (ROWS_DEV * W) - 1).astype(jnp.int32)
    positive_pixel = place_ends(jax.random.randint(key_of[4], (ANCHORS, B), 0, H * W), jax.random.fold_in(key_of[4], 1), 0, (H * W) - 1).astype(jnp.int32)
    return {"features": features, "conv_weight": conv_weight, "proj_weight": proj_weight, "anchor_pixel": anchor_pixel, "positive_pixel": positive_pixel}


SOFTMAX_TEMPER = 0.1
EPSILON = 1e-06

def group_form(weight, groups):
    group_width = weight.shape[2]
    shaped = weight.reshape(3, 3, group_width, groups, group_width)
    return jnp.transpose(shaped, (3, 0, 1, 2, 4))

def flat_form(grad_grouped):
    groups, group_width = (grad_grouped.shape[0], grad_grouped.shape[3])
    return jnp.transpose(grad_grouped, (1, 2, 3, 0, 4)).reshape(3, 3, group_width, groups * group_width)

def conv_taps(padded, weight, height, cols_dev):
    tap_sum = None
    for row_tap in range(3):
        for col_tap in range(3):
            window = padded[row_tap:row_tap + height, col_tap:col_tap + cols_dev].astype(jnp.float32)
            tap_term = jnp.einsum('hwgc,gcd->hwgd', window, weight[:, row_tap, col_tap].astype(jnp.float32))
            tap_sum = tap_term if tap_sum is None else tap_sum + tap_term
    return tap_sum

def weight_taps(padded, grad_pre, height, cols_dev):
    row_list = []
    for row_tap in range(3):
        col_list = []
        for col_tap in range(3):
            window = padded[row_tap:row_tap + height, col_tap:col_tap + cols_dev].astype(jnp.float32)
            col_list.append(jnp.einsum('hwgc,hwgd->gcd', window, grad_pre.astype(jnp.float32)))
        row_list.append(jnp.stack(col_list, axis=1))
    return jnp.stack(row_list, axis=1)

def silu_slope(pre_value):
    sigmoid_val = jax.nn.sigmoid(pre_value)
    return sigmoid_val * (1.0 + pre_value * (1.0 - sigmoid_val))

def one_image(image_in, anchors, positives, conv_weight, proj_weight, gradient_factor):
    height, cols_dev, channels = image_in.shape
    groups, group_width = (conv_weight.shape[0], conv_weight.shape[3])
    grouped = image_in.reshape(height, cols_dev, groups, group_width)
    padded = jnp.pad(grouped, ((1, 1), (1, 1), (0, 0), (0, 0)))
    pre_act = conv_taps(padded, conv_weight, height, cols_dev)
    mixed = (grouped.astype(jnp.float32) + jax.nn.silu(pre_act)).astype(jnp.bfloat16)
    flat_mixed = mixed.reshape(height * cols_dev, channels)
    raw_key = jnp.dot(flat_mixed, proj_weight, preferred_element_type=jnp.float32)
    norm_key = jnp.sqrt(lax.optimization_barrier(jnp.sum(raw_key * raw_key, axis=1, keepdims=True)) + EPSILON)
    unit_key = raw_key / norm_key
    key_vectors = unit_key.astype(jnp.bfloat16)
    query_vectors = key_vectors[anchors]
    score_matrix = jnp.dot(query_vectors, key_vectors.T, preferred_element_type=jnp.float32) / SOFTMAX_TEMPER
    exp_scores = jnp.exp(score_matrix)
    totals = lax.optimization_barrier(jnp.sum(exp_scores, axis=1))
    weighted = jnp.dot(exp_scores.astype(jnp.bfloat16), key_vectors, preferred_element_type=jnp.float32)
    positive_key = key_vectors[positives].astype(jnp.float32)
    positive_logit = lax.optimization_barrier(jnp.sum(query_vectors.astype(jnp.float32) * positive_key, axis=1)) / SOFTMAX_TEMPER
    loss_sum = jnp.sum(jnp.log(totals) - positive_logit)
    inverse = (1.0 / totals).astype(jnp.bfloat16)
    grad_query = (weighted / totals[:, None] - positive_key) * gradient_factor
    soft_probs = (exp_scores * inverse.astype(jnp.float32)[:, None]).astype(jnp.bfloat16)
    pulled = jnp.dot(soft_probs.T, query_vectors, preferred_element_type=jnp.float32)
    pushed = jnp.zeros(raw_key.shape, jnp.float32).at[positives].add(query_vectors.astype(jnp.float32))
    grad_key = gradient_factor * (pulled - pushed) + jnp.zeros(raw_key.shape, jnp.float32).at[anchors].add(grad_query)
    along_key = lax.optimization_barrier(jnp.sum(grad_key * unit_key, axis=1, keepdims=True))
    grad_raw = ((grad_key - unit_key * along_key) / norm_key).astype(jnp.bfloat16)
    grad_proj = jnp.dot(flat_mixed.T, grad_raw, preferred_element_type=jnp.float32)
    grad_mixed = jnp.dot(grad_raw, proj_weight.T, preferred_element_type=jnp.float32).astype(jnp.bfloat16)
    grad_mixed = grad_mixed.reshape(height, cols_dev, groups, group_width)
    grad_pre = (grad_mixed.astype(jnp.float32) * silu_slope(pre_act)).astype(jnp.bfloat16)
    grad_conv = weight_taps(padded, grad_pre, height, cols_dev)
    flipped = jnp.swapaxes(conv_weight[:, ::-1, ::-1], 3, 4)
    padded_grad = jnp.pad(grad_pre, ((1, 1), (1, 1), (0, 0), (0, 0)))
    back_grad = conv_taps(padded_grad, flipped, height, cols_dev).astype(jnp.bfloat16)
    grad_image = (back_grad.astype(jnp.float32) + grad_mixed.astype(jnp.float32)).astype(jnp.bfloat16)
    return (grad_image.reshape(height, cols_dev, channels), grad_conv, grad_proj, loss_sum)

def reference(features, conv_weight, proj_weight, anchor_pixel, positive_pixel):
    images = features.shape[2]
    channels = features.shape[3]
    groups = channels // conv_weight.shape[2]
    grouped_weight = group_form(conv_weight, groups)
    anchor_rows = anchor_pixel.shape[0]
    offsets = jnp.arange(anchor_rows, dtype=jnp.int32) // ANCH * (ROWS_DEV * W)
    anchor_count = anchor_rows * images
    gradient_factor = 1.0 / (SOFTMAX_TEMPER * anchor_count)

    def per_image(image_index):
        image_in = lax.dynamic_index_in_dim(features, image_index, 2, keepdims=False)
        anchors = offsets + lax.dynamic_index_in_dim(anchor_pixel, image_index, 1, keepdims=False).astype(jnp.int32)
        positives = lax.dynamic_index_in_dim(positive_pixel, image_index, 1, keepdims=False).astype(jnp.int32)
        return one_image(image_in, anchors, positives, grouped_weight, proj_weight, gradient_factor)
    grad_images, grad_convs, grad_projs, loss_sums = lax.map(per_image, jnp.arange(images, dtype=jnp.int32))
    grad_features = jnp.moveaxis(grad_images, 0, 2)
    loss_value = jnp.sum(loss_sums) / anchor_count
    return (grad_features, flat_form(lax.optimization_barrier(jnp.sum(grad_convs, axis=0))), lax.optimization_barrier(jnp.sum(grad_projs, axis=0)), loss_value)
```

```python
import functools

import jax
import jax.numpy as jnp
from jax import lax
from jax.experimental import pallas as pl
from jax.experimental.pallas import tpu as pltpu
from jax.sharding import PartitionSpec as P

SOFTMAX_TEMPER = 0.1
EPSILON = 1e-06
LANES = 128
F32 = jnp.float32
BF16 = jnp.bfloat16
MESH = pl.DeviceIdType.MESH

NN = (((1,), (0,)), ((), ()))
NT = (((1,), (1,)), ((), ()))
TN = (((0,), (0,)), ((), ()))


def mm(a, b, dims, precision=None):
    return lax.dot_general(a, b, dims, preferred_element_type=F32, precision=precision)


def in_hbm(array):
    return pltpu.with_memory_space_constraint(array, pltpu.HBM)


def iota(shape, dim):
    return lax.broadcasted_iota(jnp.int32, shape, dim)


def store_shifted(dst, rows, start, values, cols):
    wide = values.astype(F32)
    count = wide.shape[0]
    col = iota(wide.shape, 0) % cols
    dst[1, start : start + rows] = values
    left = jnp.where(col == 0, 0.0, pltpu.roll(wide, 1, 0))
    dst[0, start : start + rows] = left.astype(BF16)
    right = jnp.where(col == cols - 1, 0.0, pltpu.roll(wide, count - 1, 0))
    dst[2, start : start + rows] = right.astype(BF16)


def kernel(
    devices,
    anchors_all,
    gradient_scale,
    geometry,
    x_hbm,
    w_hbm,
    proj_hbm,
    anchor_hbm,
    positive_hbm,
    out_ref,
    ag,
    loss_ref,
    x_ref,
    w_ref,
    proj_ref,
    anchor_ref,
    positive_ref,
    load,
    xh,
    xs,
    wn,
    wt,
    at,
    mixed,
    mixed_t,
    slope,
    posb,
    qall,
    totp,
    totx,
    totb,
    wps,
    wpx,
    wpc,
    wpr,
    gm,
    gp,
    gh,
    gs,
    gw,
    gpj,
    l1s,
    l1r,
    l2s,
    l2r,
    l3s,
    l3r,
    xh_send,
    xh_recv,
    gh_send,
    gh_recv,
    pos_send,
    pos_recv,
    q_send,
    q_recv,
    tot_send,
    tot_recv,
    wp_send,
    wp_recv,
    totx_send,
    totx_recv,
    wpx_send,
    wpx_recv,
    l1_send,
    l1_recv,
    l2_send,
    l2_recv,
    l3_send,
    l3_recv,
    ag_send,
    near_send,
    ag_recv,
    pair_send,
    pair_recv,
):
    cols, group, pieces, piece, prow, inner, anchor_count = geometry
    pixels, channels = x_ref.shape
    blocks = channels // LANES
    per_block = LANES // group
    anchors_dev = anchor_ref.shape[1]
    chips = devices // 2
    me = lax.axis_index("wide")
    core = lax.rem(me, 2)
    chip = me // 2
    partner = me + 1 - 2 * core
    place = lax.rem(chip, inner)
    layer = chip // inner
    layers = chips // inner
    barrier = pltpu.get_barrier_semaphore()

    def others(body):
        def step(k, carry):
            body(lax.rem(me + k, devices))
            return carry

        lax.fori_loop(1, devices, step, 0)

    def turn(count, start, body):
        def step(k, carry):
            body(lax.rem(start + k, count))
            return carry

        lax.fori_loop(1, count, step, 0)

    def block_loop(start, stop, body):
        def step(i, carry):
            for j in range(2):
                body(2 * i + j, carry)
            return carry

        lax.fori_loop(start // 2, stop // 2, step, 0)

    def other_chips(body):
        def step(k, carry):
            body(lax.rem(chip + k, chips))
            return carry

        lax.fori_loop(1, chips, step, 0)

    def remote(src, dst, send_sem, recv_sem, target):
        return pltpu.make_async_remote_copy(
            src_ref=src,
            dst_ref=dst,
            send_sem=send_sem,
            recv_sem=recv_sem,
            device_id={"wide": target},
            device_id_type=MESH,
        )

    def signal_entry(target):
        pl.semaphore_signal(barrier, inc=1, device_id={"wide": target}, device_id_type=MESH)

    loads = [
        pltpu.make_async_copy(src, dst, load.at[n])
        for n, (src, dst) in enumerate(
            (
                (positive_hbm, positive_ref),
                (w_hbm, w_ref),
                (x_hbm, x_ref),
                (proj_hbm, proj_ref),
                (anchor_hbm, anchor_ref),
            )
        )
    ]
    for copy in loads:
        copy.start()
    def greet(k, carry):
        signal_entry(lax.rem(me + k, devices))
        signal_entry(lax.rem(me + devices - k, devices))
        return carry

    lax.fori_loop(1, devices // 2, greet, 0)
    signal_entry(lax.rem(me + devices // 2, devices))
    pl.semaphore_wait(barrier, devices - 1)

    has_prev = me > 0
    has_next = me < devices - 1
    previous = lax.rem(me + devices - 1, devices)
    following = lax.rem(me + 1, devices)

    def halo(src, buf, send_sem, recv_sem):
        up = remote(
            src.at[pl.ds(0, cols)], buf.at[1], send_sem.at[0], recv_sem.at[1], previous
        )
        down = remote(
            src.at[pl.ds(pixels - cols, cols)],
            buf.at[0],
            send_sem.at[1],
            recv_sem.at[0],
            following,
        )
        return up, down

    def halo_start(copies):
        up, down = copies

        @pl.when(has_prev)
        def _():
            up.start()

        @pl.when(has_next)
        def _():
            down.start()

    def halo_wait(copies, buf):
        up, down = copies

        @pl.when(has_prev)
        def _():
            up.wait_send()
            down.wait_recv()

        @pl.when(jnp.logical_not(has_prev))
        def _():
            buf[0] = jnp.zeros(buf.shape[1:], buf.dtype)

        @pl.when(has_next)
        def _():
            down.wait_send()
            up.wait_recv()

        @pl.when(jnp.logical_not(has_next))
        def _():
            buf[1] = jnp.zeros(buf.shape[1:], buf.dtype)

    def to_all(buf, send_sem, recv_sem):
        def go(target):
            remote(
                buf.at[me], buf.at[me], send_sem.at[target], recv_sem.at[me], target
            ).start()

        return go

    def from_all(buf, send_sem, recv_sem):
        def done(source):
            copy = remote(
                buf.at[source], buf.at[source], send_sem.at[source], recv_sem.at[source], source
            )
            copy.wait_recv()
            copy.wait_send()

        return done

    x_halo = halo(x_hbm, xh, xh_send, xh_recv)
    halo_start(x_halo)
    for copy in loads:
        copy.wait()

    tap_count = w_ref.shape[0]
    diagonal = iota((LANES, LANES), 0) // group == iota((LANES, LANES), 1) // group

    def build(b, carry):
        lane = pl.ds(pl.multiple_of(b * LANES, LANES), LANES)
        for tap in range(tap_count):
            slab = w_ref[tap, :, lane].astype(F32)
            full = jnp.where(diagonal, jnp.concatenate([slab] * per_block, axis=0), 0.0)
            full = full.astype(BF16)
            wn[b, tap * LANES : (tap + 1) * LANES, :] = full
            wt[b, :, tap * LANES : (tap + 1) * LANES] = full
        return carry

    lax.fori_loop(0, blocks, build, 0)
    store_shifted(xs, pixels, cols, x_ref[...], cols)

    posb[me, :, :anchors_dev] = positive_ref[...].astype(F32)
    posb[me, :, anchors_dev:] = jnp.zeros((1, LANES - anchors_dev), F32)
    eye = iota((anchors_dev, anchors_dev), 0) == iota((anchors_dev, anchors_dev), 1)
    anchor_col = jnp.sum(
        jnp.where(eye, anchor_ref[...].astype(F32), 0.0), axis=1, keepdims=True
    )
    others(to_all(posb, pos_send, pos_recv))
    halo_wait(x_halo, xh)
    store_shifted(xs, cols, 0, xh[0], cols)
    store_shifted(xs, cols, cols + pixels, xh[1], cols)

    def windows(buf, lane, flip):
        parts = []
        for row in range(3):
            for col in range(3):
                r, c = (2 - row, 2 - col) if flip else (row, col)
                parts.append(buf[c, r * cols : r * cols + pixels, lane])
        return jnp.concatenate(parts, axis=1)

    def forward(b, carry):
        lane = pl.ds(pl.multiple_of(b * LANES, LANES), LANES)
        pre = mm(windows(xs, lane, False), wn[b], NN)
        sig = 1.0 / (1.0 + jnp.exp(-pre))
        mixed[:, lane] = (x_ref[:, lane].astype(F32) + pre * sig).astype(BF16)
        slope[:, lane] = sig * (1.0 + pre * (1.0 - sig))
        return carry

    block_loop(0, blocks, forward)

    raw_key = mm(mixed[...], proj_ref[...], NN)
    norm_key = jnp.sqrt(jnp.sum(raw_key * raw_key, axis=1, keepdims=True) + EPSILON)
    unit_key = raw_key / norm_key
    keys = unit_key.astype(BF16)
    pick = jnp.where(
        iota((anchors_dev, pixels), 1).astype(F32) == anchor_col, 1.0, 0.0
    )
    qall[me] = mm(pick.astype(BF16), keys, NN).astype(BF16)
    others(to_all(qall, q_send, q_recv))

    def flip_over(b, carry):
        start = pl.multiple_of(b * LANES, LANES)
        lane = pl.ds(start, LANES)
        at[b] = windows(xs, lane, False).T
        mixed_t[lane, :] = mixed[:, lane].T
        return carry

    block_loop(0, blocks, flip_over)

    others(from_all(posb, pos_send, pos_recv))
    own_lane = iota((devices, anchors_dev, LANES), 1) == iota((devices, anchors_dev, LANES), 2)
    pos_all = jnp.sum(jnp.where(own_lane, posb[...], 0.0), axis=2, keepdims=True)
    pos_local = pos_all - (me * pixels).astype(F32)
    hit3 = jnp.where(
        iota((devices, anchors_dev, pixels), 2).astype(F32) == pos_local, 1.0, 0.0
    )
    hit = hit3.reshape(anchors_all, pixels).astype(BF16)

    others(from_all(qall, q_send, q_recv))
    queries = qall[...].reshape(anchors_all, LANES)
    exp_scores = jnp.exp(mm(keys, queries, NT) / SOFTMAX_TEMPER)
    part_total = jnp.sum(exp_scores, axis=0, keepdims=True)
    part_pos = mm(hit, keys, NN)
    pos_sum = jnp.sum(
        jnp.sum(part_pos * queries.astype(F32), axis=1, keepdims=True), axis=0, keepdims=True
    )
    tot_rows = anchors_all // LANES
    rows = [part_total[:, r * LANES : (r + 1) * LANES] for r in range(tot_rows)]
    rows.append(jnp.broadcast_to(pos_sum, (1, LANES)))
    for r in range(tot_rows + 1):
        totp[r : r + 1, :] = rows[r]
    tot_pair = remote(totp, totx, totx_send, totx_recv, partner)
    tot_pair.start()
    part_weighted = mm(exp_scores.astype(BF16), keys, TN)
    by_owner = part_weighted.reshape(chips, 2, anchors_dev, LANES).astype(BF16)
    pos_owner = part_pos.reshape(chips, 2, anchors_dev, LANES).astype(BF16)
    for half in range(2):
        wps[half, :, :anchors_dev, :] = by_owner[:, half]
        wps[half, :, anchors_dev:, :] = pos_owner[:, half]
    part_pair = remote(wps.at[1 - core], wpx, wpx_send, wpx_recv, partner)
    part_pair.start()
    tot_pair.wait()
    totb[chip] = totp[...] + totx[...]

    def send_total(target):
        remote(
            totb.at[chip],
            totb.at[chip],
            tot_send.at[target],
            tot_recv.at[chip],
            target * 2 + core,
        ).start()

    other_chips(send_total)
    part_pair.wait()
    wpc[...] = (wps[core].astype(F32) + wpx[...].astype(F32)).astype(BF16)

    def send_part(target):
        remote(
            wpc.at[target], wpr.at[chip], wp_send.at[target], wp_recv.at[chip], target * 2 + core
        ).start()

    other_chips(send_part)
    wpr[chip] = wpc[chip]
    pushed = mm(hit, queries, TN)

    def total_done(source):
        copy = remote(
            totb.at[source],
            totb.at[source],
            tot_send.at[source],
            tot_recv.at[source],
            source * 2 + core,
        )
        copy.wait_recv()
        copy.wait_send()

    other_chips(total_done)
    sums = jnp.sum(totb[...], axis=0)
    total_row = jnp.concatenate([sums[r : r + 1, :] for r in range(tot_rows)], axis=1)
    loss = jnp.sum(jnp.log(total_row), axis=1, keepdims=True) - sums[
        tot_rows : tot_rows + 1, 0:1
    ] / SOFTMAX_TEMPER
    loss_ref[...] = loss / anchor_count
    inverse = (1.0 / total_row).astype(BF16).astype(F32)
    soft = (exp_scores * inverse).astype(BF16)
    pulled = mm(soft, queries, NN)
    mine = iota((anchors_dev, anchors_all), 1) == me * anchors_dev + iota(
        (anchors_dev, anchors_all), 0
    )
    own_total = jnp.sum(jnp.where(mine, total_row, 0.0), axis=1, keepdims=True)

    def part_done(source):
        copy = remote(
            wpc.at[source], wpr.at[source], wp_send.at[source], wp_recv.at[source], source * 2 + core
        )
        copy.wait_recv()
        copy.wait_send()

    other_chips(part_done)
    both = jnp.sum(wpr[...].astype(F32), axis=0)
    grad_query = (both[:anchors_dev] / own_total - both[anchors_dev:]) * gradient_scale
    grad_key = gradient_scale * (pulled - pushed)
    grad_key = grad_key + mm(pick, grad_query, TN, lax.Precision.HIGHEST)
    along = jnp.sum(grad_key * unit_key, axis=1, keepdims=True)
    grad_raw = ((grad_key - unit_key * along) / norm_key).astype(BF16)
    grad_mixed = mm(grad_raw, proj_ref[...], NT).astype(BF16)
    gm[...] = grad_mixed
    gp[...] = (grad_mixed.astype(F32) * slope[...]).astype(BF16)
    g_halo = halo(gp, gh, gh_send, gh_recv)
    halo_start(g_halo)

    gpj[...] = mm(mixed_t[...], grad_raw, NN)
    lane_group = iota((group, LANES), 1) // group

    def weight_grad(b, carry):
        lane = pl.ds(pl.multiple_of(b * LANES, LANES), LANES)
        full = mm(at[b], gp[:, lane], NN)
        for tap in range(tap_count):
            folded = jnp.zeros((group, LANES), F32)
            for g in range(per_block):
                first = tap * LANES + g * group
                folded = jnp.where(lane_group == g, full[first : first + group], folded)
            gw[b, tap * group : (tap + 1) * group, :] = folded
        return carry

    block_loop(0, blocks, weight_grad)
    if gw.shape[1] > tap_count * group:
        gw[:, tap_count * group :, :] = jnp.zeros(
            (blocks, gw.shape[1] - tap_count * group, LANES), F32
        )

    def chunk(half, i):
        b = half * (blocks // 2) + i // pieces
        first = pl.multiple_of(lax.rem(i, pieces) * piece, 8)
        first_p = pl.multiple_of((half * chips + i) * prow, 8)
        return gpj[pl.ds(first_p, prow), :], gw[b, pl.ds(first, piece), :]

    def fill(i, carry):
        proj_part, conv_part = chunk(1 - core, i)
        l1s[i, :prow, :] = proj_part.astype(BF16)
        l1s[i, prow:, :] = conv_part.astype(BF16)
        return carry

    lax.fori_loop(0, chips, fill, 0)
    l1 = remote(l1s, l1r, l1_send, l1_recv, partner)
    l1.start()
    store_shifted(gs, pixels, cols, gp[...], cols)
    l1.wait()

    def join(i, carry):
        proj_part, conv_part = chunk(core, i)
        to, at_layer = lax.rem(i, inner), i // inner
        l2s[to, at_layer, :prow, :] = (proj_part + l1r[i, :prow, :].astype(F32)).astype(BF16)
        l2s[to, at_layer, prow:, :] = (conv_part + l1r[i, prow:, :].astype(F32)).astype(BF16)
        return carry

    lax.fori_loop(0, chips, join, 0)

    def near_sum(target, slot):
        return remote(
            l2s.at[target],
            l2r.at[slot],
            l2_send.at[target],
            l2_recv.at[slot],
            (layer * inner + target) * 2 + core,
        )

    def far_sum(target, slot):
        return remote(
            l3s.at[target],
            l3r.at[slot],
            l3_send.at[target],
            l3_recv.at[slot],
            (target * inner + place) * 2 + core,
        )

    turn(inner, place, lambda target: near_sum(target, place).start())
    l2r[place] = l2s[place]

    halo_wait(g_halo, gh)
    store_shifted(gs, cols, 0, gh[0], cols)
    store_shifted(gs, cols, cols + pixels, gh[1], cols)

    def backward(b, carry):
        lane = pl.ds(pl.multiple_of(b * LANES, LANES), LANES)
        back = mm(windows(gs, lane, True), wt[b], NT).astype(BF16)
        out_ref[:, lane] = (back.astype(F32) + gm[:, lane].astype(F32)).astype(BF16)
        return carry

    block_loop(0, blocks // 2, backward)

    def near_done(source):
        copy = near_sum(source, source)
        copy.wait_recv()
        copy.wait_send()

    def far_done(source):
        copy = far_sum(source, source)
        copy.wait_recv()
        copy.wait_send()

    turn(inner, place, near_done)
    for z in range(layers):
        l3s[z] = jnp.sum(l2r[:, z].astype(F32), axis=0).astype(BF16)
    turn(layers, layer, lambda target: far_sum(target, layer).start())
    l3r[layer] = l3s[layer]
    block_loop(blocks // 2, blocks, backward)
    turn(layers, layer, far_done)
    ag[core, chip] = jnp.sum(l3r[...].astype(F32), axis=0).astype(BF16)

    def chunk_copy(index, send_sem, target):
        return remote(
            ag.at[core, index], ag.at[core, index], send_sem, ag_recv.at[index], target
        )

    def pair_copy(index, half):
        return remote(
            ag.at[half, index],
            ag.at[half, index],
            pair_send.at[index],
            pair_recv.at[index],
            partner,
        )

    def far_copy(target):
        return chunk_copy(chip, ag_send.at[target], (target * inner + place) * 2 + core)

    def near_copy(source, target):
        return chunk_copy(
            source * inner + place, near_send.at[source, target], (layer * inner + target) * 2 + core
        )

    def forward_near(source):
        turn(inner, place, lambda target: near_copy(source, target).start())
        pair_copy(source * inner + place, core).start()

    turn(layers, layer, lambda target: far_copy(target).start())
    forward_near(layer)

    def far_arrived(source):
        chunk_copy(source * inner + place, ag_send.at[source], partner).wait_recv()
        forward_near(source)

    turn(layers, layer, far_arrived)

    def near_arrived(k, carry):
        source = lax.rem(layer + k, layers)

        def one(other):
            index = source * inner + other
            chunk_copy(index, near_send.at[source, other], partner).wait_recv()
            pair_copy(index, core).start()

        turn(inner, place, one)
        return carry

    lax.fori_loop(0, layers, near_arrived, 0)

    turn(layers, layer, lambda target: far_copy(target).wait_send())

    def near_sent(source, carry):
        turn(inner, place, lambda target: near_copy(source, target).wait_send())
        return carry

    lax.fori_loop(0, layers, near_sent, 0)

    def pair_done(i, carry):
        pair_copy(i, core).wait_send()
        pair_copy(i, 1 - core).wait_recv()
        return carry

    lax.fori_loop(0, chips, pair_done, 0)


def finish(geometry, gf_ref, ag, loss_ref, gf_out, gw_out, gp_out, loss_out, gw, gp, sems):
    blocks, chips, pieces, piece, prow = geometry
    moves = [pltpu.make_async_copy(gf_ref, gf_out, sems.at[0])]
    moves[0].start()
    loss_out[...] = loss_ref[...]
    height = gw_out.shape[0]
    half_rows = chips * prow
    for half in range(2):
        for i in range(chips):
            b = half * (blocks // 2) + i // pieces
            first = i % pieces * piece
            first_p = (half * chips + i) * prow
            keep = min(piece, height - first)
            gp[first_p : first_p + prow, :] = ag[half, i, :prow, :].astype(F32)
            if keep > 0:
                gw[first : first + keep, b * LANES : (b + 1) * LANES] = ag[
                    half, i, prow : prow + keep, :
                ].astype(F32)
            if i % pieces == pieces - 1:
                lane = pl.ds(b * LANES, LANES)
                moves.append(
                    pltpu.make_async_copy(gw.at[:, lane], gw_out.at[:, lane], sems.at[3 + b])
                )
                moves[-1].start()
        rows = pl.ds(half * half_rows, half_rows)
        moves.append(pltpu.make_async_copy(gp.at[rows], gp_out.at[rows], sems.at[1 + half]))
        moves[-1].start()
    for move in moves:
        move.wait()


def per_device(devices, batches, features, conv_weight, proj_weight, anchor_pixel, positive_pixel):
    rows_dev, cols, images, channels = features.shape
    group = conv_weight.shape[2]
    key_width = proj_weight.shape[1]
    anchors_dev = anchor_pixel.shape[0]
    inner = min(4, devices // 2)
    layers = devices // 2 // inner
    pixels = rows_dev * cols
    taps = conv_weight.shape[0] * conv_weight.shape[1]
    blocks = channels // LANES
    chips = devices // 2
    pieces = chips // (blocks // 2)
    piece = -(-(taps * group) // pieces)
    piece = -(-piece // 8) * 8
    prow = channels // devices
    anchors_all = anchors_dev * devices
    anchor_count = anchors_all * images * batches
    gradient_scale = 1.0 / (SOFTMAX_TEMPER * anchor_count)
    tot_rows = anchors_all // LANES + 1
    padded = pixels + 2 * cols
    dma = pltpu.SemaphoreType.DMA
    chunk_rows = prow + piece
    vmem = pltpu.VMEM
    whole = pl.BlockSpec(memory_space=pltpu.VMEM)
    scratch = [
        vmem((pixels, channels), BF16),
        vmem((taps, group, channels), BF16),
        vmem((channels, key_width), BF16),
        vmem((1, anchors_dev), jnp.int32),
        vmem((1, anchors_dev), jnp.int32),
        dma((5,)),
        vmem((2, cols, channels), BF16),
        vmem((3, padded, channels), BF16),
        vmem((blocks, taps * LANES, LANES), BF16),
        vmem((blocks, LANES, taps * LANES), BF16),
        vmem((blocks, taps * LANES, pixels), BF16),
        vmem((pixels, channels), BF16),
        vmem((channels, pixels), BF16),
        vmem((pixels, channels), F32),
        vmem((devices, 1, LANES), F32),
        vmem((devices, anchors_dev, LANES), BF16),
        vmem((tot_rows, LANES), F32),
        vmem((tot_rows, LANES), F32),
        vmem((chips, tot_rows, LANES), F32),
        vmem((2, chips, 2 * anchors_dev, LANES), BF16),
        vmem((chips, 2 * anchors_dev, LANES), BF16),
        vmem((chips, 2 * anchors_dev, LANES), BF16),
        vmem((chips, 2 * anchors_dev, LANES), BF16),
        vmem((pixels, channels), BF16),
        vmem((pixels, channels), BF16),
        vmem((2, cols, channels), BF16),
        vmem((3, padded, channels), BF16),
        vmem((blocks, pieces * piece, LANES), F32),
        vmem((channels, LANES), F32),
        vmem((chips, chunk_rows, LANES), BF16),
        vmem((chips, chunk_rows, LANES), BF16),
        vmem((inner, layers, chunk_rows, LANES), BF16),
        vmem((inner, layers, chunk_rows, LANES), BF16),
        vmem((layers, chunk_rows, LANES), BF16),
        vmem((layers, chunk_rows, LANES), BF16),
        dma((2,)),
        dma((2,)),
        dma((2,)),
        dma((2,)),
    ]
    scratch += [dma((devices,))] * 4
    scratch += [dma((chips,))] * 4
    scratch += [dma] * 4
    scratch += [dma, dma]
    scratch += [dma((inner,))] * 2
    scratch += [dma((layers,))] * 2
    scratch += [dma((layers,)), dma((layers, inner))]
    scratch += [dma((chips,))] * 3
    sums = (
        jax.ShapeDtypeStruct((pixels, channels), BF16),
        jax.ShapeDtypeStruct((2, chips, chunk_rows, LANES), BF16),
        jax.ShapeDtypeStruct((1, 1), F32),
    )
    parts = pl.pallas_call(
        functools.partial(
            kernel,
            devices,
            anchors_all,
            gradient_scale,
            (cols, group, pieces, piece, prow, inner, anchor_count),
        ),
        out_shape=sums,
        in_specs=[pl.BlockSpec(memory_space=pltpu.HBM)] * 5,
        out_specs=(whole,) * 3,
        scratch_shapes=scratch,
        compiler_params=pltpu.CompilerParams(
            collective_id=0, has_side_effects=True, vmem_limit_bytes=26000 * 1024
        ),
    )(
        in_hbm(features.reshape(pixels, channels)),
        in_hbm(conv_weight.reshape(taps, group, channels)),
        in_hbm(proj_weight),
        in_hbm(anchor_pixel.reshape(1, anchors_dev)),
        in_hbm(positive_pixel.reshape(1, anchors_dev)),
    )
    grad_features, grad_conv, grad_proj, loss = pl.pallas_call(
        functools.partial(finish, (blocks, chips, pieces, piece, prow)),
        out_shape=(
            jax.ShapeDtypeStruct((pixels, channels), BF16),
            jax.ShapeDtypeStruct((taps * group, channels), F32),
            jax.ShapeDtypeStruct((channels, key_width), F32),
            jax.ShapeDtypeStruct((1, 1), F32),
        ),
        in_specs=[whole] * 3,
        out_specs=(pl.BlockSpec(memory_space=pltpu.HBM),) * 3 + (whole,),
        scratch_shapes=[
            vmem((taps * group, channels), F32),
            vmem((channels, key_width), F32),
            dma((3 + blocks,)),
        ],
        compiler_params=pltpu.CompilerParams(vmem_limit_bytes=16000 * 1024),
    )(*parts)
    grad_conv = grad_conv.reshape(conv_weight.shape)
    loss_value = loss.reshape(())
    if batches > 1:
        grad_conv, grad_proj, loss_value = lax.psum((grad_conv, grad_proj, loss_value), "batch")
    return (grad_features.reshape(features.shape), grad_conv, grad_proj, loss_value)


def solution(mesh):
    placed = (P("wide", None, "batch", None), P(), P(), P("wide", "batch"), P("wide", "batch"))
    return jax.shard_map(
        functools.partial(per_device, mesh.shape["wide"], mesh.shape["batch"]),
        mesh=mesh,
        in_specs=placed,
        out_specs=(P("wide", None, "batch", None), P(), P(), P()),
        check_vma=False,
    )
```

```python
import functools

import jax
import jax.numpy as jnp
from jax import lax
from jax.experimental import pallas as pl
from jax.experimental.pallas import tpu as pltpu
from jax.sharding import PartitionSpec as P

SOFTMAX_TEMPER = 0.1
EPSILON = 1e-06
LANES = 128
F32 = jnp.float32
BF16 = jnp.bfloat16
MESH = pl.DeviceIdType.MESH

NN = (((1,), (0,)), ((), ()))
NT = (((1,), (1,)), ((), ()))
TN = (((0,), (0,)), ((), ()))


def mm(a, b, dims, precision=None):
    return lax.dot_general(a, b, dims, preferred_element_type=F32, precision=precision)


def in_hbm(array):
    return pltpu.with_memory_space_constraint(array, pltpu.HBM)


def iota(shape, dim):
    return lax.broadcasted_iota(jnp.int32, shape, dim)


def store_shifted(dst, rows, start, values, cols):
    wide = values.astype(F32)
    count = wide.shape[0]
    col = iota(wide.shape, 0) % cols
    dst[1, start : start + rows] = values
    left = jnp.where(col == 0, 0.0, pltpu.roll(wide, 1, 0))
    dst[0, start : start + rows] = left.astype(BF16)
    right = jnp.where(col == cols - 1, 0.0, pltpu.roll(wide, count - 1, 0))
    dst[2, start : start + rows] = right.astype(BF16)


def kernel(names, devices, gradient_scale, geometry, *refs):
    r = dict(zip(names, refs, strict=True))
    cols, group, pieces, piece, prow, inner, anchor_count = geometry
    x_hbm, out_ref, ag_a, ag_b = r["x_hbm"], r["out"], r["ag_a"], r["ag_b"]
    pixels = x_hbm.shape[0]
    channels = x_hbm.shape[1]
    half = channels // 2
    blocks = half // LANES
    per_block = LANES // group
    anchors_dev = r["anchor"].shape[1]
    chips = devices // 2
    both = 2 * pixels
    anchors_core = chips * anchors_dev
    me = lax.axis_index("wide")
    core = lax.rem(me, 2)
    chip = me // 2
    other = 1 - core
    partner = chip * 2 + other
    place = lax.rem(chip, inner)
    layer = chip // inner
    layers = chips // inner
    span = pieces // inner
    conv_a = ag_a.shape[3] - prow
    barrier = pltpu.get_barrier_semaphore()

    def turn(count, start, body):
        def step(k, carry):
            body(lax.rem(start + k, count))
            return carry

        lax.fori_loop(1, count, step, 0)

    def other_chips(body):
        turn(chips, chip, body)

    def near_id(target):
        return (layer * inner + target) * 2 + core

    def far_id(target):
        return (target * inner + place) * 2 + core

    def remote(src, dst, name, target, at=None, sent=None):
        recv = r[name + "_recv"]
        send = r[name + "_send"]
        return pltpu.make_async_remote_copy(
            src_ref=src,
            dst_ref=dst,
            send_sem=send if sent is None else send.at[sent],
            recv_sem=recv if at is None else recv.at[at],
            device_id={"wide": target},
            device_id_type=MESH,
        )

    def to_chips(source, landing, name):
        other_chips(lambda t: remote(source(t), landing, name, t * 2 + core).start())

    def from_chips(buf, name):
        view = buf.at[pl.ds(0, chips - 1)]
        remote(view, view, name, partner).wait_recv()

    def sent_chips(buf, name):
        view = buf.at[pl.ds(0, chips - 1)]
        remote(view, view, name, partner).wait_send()

    def signal_entry(target):
        pl.semaphore_signal(barrier, inc=1, device_id={"wide": target}, device_id_type=MESH)

    has_prev = chip > 0
    has_next = chip < chips - 1
    previous = lax.rem(chip + chips - 1, chips)
    following = lax.rem(chip + 1, chips)
    my_half = pl.ds(pl.multiple_of(core * half, LANES), half)
    your_half = pl.ds(pl.multiple_of(other * half, LANES), half)
    my_pixels = pl.ds(pl.multiple_of(core * pixels, 16), pixels)

    loads = [
        pltpu.make_async_copy(src, dst, r["load"].at[n])
        for n, (src, dst) in enumerate(
            (
                (r["positive_hbm"], r["positive"]),
                (r["w_hbm"].at[:, :, my_half], r["w"]),
                (x_hbm.at[:, my_half], r["xa"].at[my_pixels]),
                (r["proj_hbm"].at[my_half], r["proj"]),
                (r["anchor_hbm"], r["anchor"]),
            )
        )
    ]
    for copy in loads:
        copy.start()

    @pl.when(has_prev)
    def _():
        signal_entry(previous * 2 + other)

    @pl.when(has_next)
    def _():
        signal_entry(following * 2 + other)

    signal_entry(partner)

    def greet(k, carry):
        signal_entry(lax.rem(chip + k, chips) * 2 + core)
        signal_entry(lax.rem(chip + chips - k, chips) * 2 + core)
        return carry

    lax.fori_loop(1, chips // 2, greet, 0)
    signal_entry(lax.rem(chip + chips // 2, chips) * 2 + core)
    pl.semaphore_wait(barrier, chips + has_prev.astype(jnp.int32) + has_next.astype(jnp.int32))

    xh, gh, xa, gp = r["xh"], r["gh"], r["xa"], r["gp"]

    def x_edge(source, slot, target):
        return [
            remote(
                x_hbm.at[pl.ds(source, cols), pl.ds(t * half, half)],
                xh.at[slot],
                "xh",
                target * 2 + t,
                at=slot,
                sent=t,
            )
            for t in range(2)
        ]

    up_edge = x_edge(0, 1, previous)
    down_edge = x_edge(pixels - cols, 0, following)
    sends_up = jnp.logical_and(core == 0, has_prev)
    sends_down = jnp.logical_and(core == 1, has_next)

    @pl.when(sends_up)
    def _():
        for copy in up_edge:
            copy.start()

    @pl.when(sends_down)
    def _():
        for copy in down_edge:
            copy.start()

    x_pair = remote(x_hbm.at[:, your_half], xa.at[my_pixels], "xp", partner)
    x_pair.start()

    def edges_wait(buf, name):
        @pl.when(has_prev)
        def _():
            remote(buf.at[0], buf.at[0], name, partner, at=0, sent=0).wait_recv()

        @pl.when(jnp.logical_not(has_prev))
        def _():
            buf[0] = jnp.zeros(buf.shape[1:], buf.dtype)

        @pl.when(has_next)
        def _():
            remote(buf.at[1], buf.at[1], name, partner, at=1, sent=1).wait_recv()

        @pl.when(jnp.logical_not(has_next))
        def _():
            buf[1] = jnp.zeros(buf.shape[1:], buf.dtype)

    for copy in loads:
        copy.wait()
    posb = r["posb"]
    posb[core, chip, :, :anchors_dev] = r["positive"][...].astype(F32)
    posb[core, chip, :, anchors_dev : 2 * anchors_dev] = r["anchor"][...].astype(F32)
    posb[core, chip, :, 2 * anchors_dev :] = jnp.zeros((1, LANES - 2 * anchors_dev), F32)
    to_chips(lambda t: posb.at[core, chip], posb.at[core, chip], "pos")

    w_ref, wn, wt, at = r["w"], r["wn"], r["wt"], r["at"]
    tap_count = w_ref.shape[0]
    diagonal = iota((LANES, LANES), 0) // group == iota((LANES, LANES), 1) // group

    def build(b, carry):
        lane = pl.ds(pl.multiple_of(b * LANES, LANES), LANES)
        for tap in range(tap_count):
            slab = w_ref[tap, :, lane].astype(F32)
            full = jnp.where(diagonal, jnp.concatenate([slab] * per_block, axis=0), 0.0)
            full = full.astype(BF16)
            wn[b, tap * LANES : (tap + 1) * LANES, :] = full
            wt[b, :, tap * LANES : (tap + 1) * LANES] = full
        return carry

    lax.fori_loop(0, blocks, build, 0)
    xs, gs = r["xs"], r["gs"]
    x_pair.wait_recv()
    store_shifted(xs, both, cols, xa[...], cols)

    def diagonal_col(row, first):
        lane = iota((anchors_dev, LANES), 1)
        hit = lane == iota((anchors_dev, LANES), 0) + first
        return jnp.sum(jnp.where(hit, row, 0.0), axis=1, keepdims=True)

    def pick_of(row, owner):
        column = diagonal_col(row, anchors_dev) + (owner * pixels).astype(F32)
        return jnp.where(iota((anchors_dev, both), 1).astype(F32) == column, 1.0, 0.0)

    pick_own = pick_of(posb[core, chip], core)
    edges_wait(xh, "xh")
    store_shifted(xs, cols, 0, xh[0], cols)
    store_shifted(xs, cols, cols + both, xh[1], cols)

    def windows(buf, lane, flip):
        parts = []
        for row in range(3):
            for col in range(3):
                rr, cc = (2 - row, 2 - col) if flip else (row, col)
                parts.append(buf[cc, rr * cols : rr * cols + both, lane])
        return jnp.concatenate(parts, axis=1)

    mixed, mixed_t, slope, proj_ref = r["mixed"], r["mixed_t"], r["slope"], r["proj"]

    def forward(b, carry):
        lane = pl.ds(pl.multiple_of(b * LANES, LANES), LANES)
        pre = mm(windows(xs, lane, False), wn[b], NN)
        sig = 1.0 / (1.0 + jnp.exp(-pre))
        mixed[:, lane] = (xa[:, lane].astype(F32) + pre * sig).astype(BF16)
        slope[:, lane] = sig * (1.0 + pre * (1.0 - sig))
        return carry

    lax.fori_loop(0, blocks, forward, 0)

    rks, rkr = r["rks"], r["rkr"]
    rks[...] = mm(mixed[...], proj_ref[...], NN)
    rk_pair = remote(rks, rkr, "rk", partner)
    rk_pair.start()
    from_chips(posb.at[core], "pos")
    pos_pair = remote(posb.at[core], posb.at[core], "posp", partner)
    pos_pair.start()
    rk_pair.wait_recv()
    raw_key = rks[...] + rkr[...]
    norm_key = jnp.sqrt(jnp.sum(raw_key * raw_key, axis=1, keepdims=True) + EPSILON)
    unit_key = raw_key / norm_key
    keys = unit_key.astype(BF16)
    qall = r["qall"]
    qall[core, chip] = mm(pick_own.astype(BF16), keys, NN).astype(BF16)
    to_chips(lambda t: qall.at[core, chip], qall.at[core, chip], "q")

    def hits(parity):
        own_lane = iota((chips, anchors_dev, LANES), 1) == iota((chips, anchors_dev, LANES), 2)
        pos_all = jnp.sum(jnp.where(own_lane, posb[parity], 0.0), axis=2, keepdims=True)
        pos_local = pos_all - (chip * both).astype(F32)
        hit3 = jnp.where(
            iota((chips, anchors_dev, both), 2).astype(F32) == pos_local, 1.0, 0.0
        )
        return hit3.reshape(anchors_core, both).astype(BF16)

    hit_own = hits(core)
    part_pos = mm(hit_own, keys, NN)
    pps, ppr = r["pps"], r["ppr"]
    pps[...] = part_pos.reshape(chips, anchors_dev, LANES).astype(BF16)
    to_chips(lambda t: pps.at[t], ppr.at[chip], "pp")
    ppr[chip] = pps[chip]

    def flip_over(b, carry):
        start = pl.multiple_of(b * LANES, LANES)
        lane = pl.ds(start, LANES)
        at[b] = windows(xs, lane, False).T
        mixed_t[lane, :] = mixed[:, lane].T
        return carry

    lax.fori_loop(0, blocks, flip_over, 0)
    pos_pair.wait_recv()
    hit_other = hits(other)
    pick_other = pick_of(posb[other, chip], other)

    from_chips(qall.at[core], "q")
    q_pair = remote(qall.at[core], qall.at[core], "qp", partner)
    q_pair.start()
    queries = qall[core].reshape(anchors_core, LANES)
    exp_own = jnp.exp(mm(keys, queries, NT) / SOFTMAX_TEMPER)
    part_total = jnp.sum(exp_own, axis=0, keepdims=True)
    pos_sum = jnp.sum(
        jnp.sum(part_pos * queries.astype(F32), axis=1, keepdims=True), axis=0, keepdims=True
    )
    totb, tfin = r["totb"], r["tfin"]
    tot_rows = anchors_core // LANES
    for n in range(tot_rows):
        totb[chip, n : n + 1, :] = part_total[:, n * LANES : (n + 1) * LANES]
    totb[chip, tot_rows : tot_rows + 1, :] = jnp.broadcast_to(pos_sum, (1, LANES))
    to_chips(lambda t: totb.at[chip], totb.at[chip], "tot")
    part_weighted = mm(exp_own.astype(BF16), keys, TN)
    ws, wr = r["ws"], r["wr"]
    ws[...] = part_weighted.reshape(chips, anchors_dev, LANES).astype(BF16)
    to_chips(lambda t: ws.at[t], wr.at[chip], "wp")
    wr[chip] = ws[chip]

    q_pair.wait_recv()
    queries_other = qall[other].reshape(anchors_core, LANES)
    exp_other = jnp.exp(mm(keys, queries_other, NT) / SOFTMAX_TEMPER)
    pushed = mm(hit_own, queries, TN) + mm(hit_other, queries_other, TN)

    def whole_row(sums):
        return jnp.concatenate([sums[n : n + 1, :] for n in range(tot_rows)], axis=1)

    def loss_of(sums, row):
        return jnp.sum(jnp.log(row), axis=1, keepdims=True) - sums[
            tot_rows : tot_rows + 1, 0:1
        ] / SOFTMAX_TEMPER

    def pulled_by(exp_scores, row, asked):
        inverse = (1.0 / row).astype(BF16).astype(F32)
        return mm((exp_scores * inverse).astype(BF16), asked, NN)

    from_chips(totb, "tot")
    sums_own = jnp.sum(totb[...], axis=0)
    tfin[core] = sums_own
    tot_pair = remote(tfin.at[core], tfin.at[core], "totp", partner)
    tot_pair.start()
    row_own = whole_row(sums_own)
    mine = iota((anchors_dev, anchors_core), 1) == chip * anchors_dev + iota(
        (anchors_dev, anchors_core), 0
    )
    own_total = jnp.sum(jnp.where(mine, row_own, 0.0), axis=1, keepdims=True)
    gq = r["gq"]
    from_chips(ppr, "pp")
    from_chips(wr, "wp")
    weighted = jnp.sum(wr[...].astype(F32), axis=0)
    pos_key = jnp.sum(ppr[...].astype(F32), axis=0)
    gq[core] = (weighted / own_total - pos_key) * gradient_scale
    gq_pair = remote(gq.at[core], gq.at[core], "gqp", partner)
    gq_pair.start()
    pulled = pulled_by(exp_own, row_own, queries)
    tot_pair.wait_recv()
    sums_other = tfin[other]
    row_other = whole_row(sums_other)
    pulled = pulled + pulled_by(exp_other, row_other, queries_other)
    r["loss"][...] = (loss_of(sums_own, row_own) + loss_of(sums_other, row_other)) / anchor_count
    grad_key = gradient_scale * (pulled - pushed)
    gq_pair.wait_recv()
    grad_key = grad_key + mm(pick_own, gq[core], TN, lax.Precision.HIGHEST)
    grad_key = grad_key + mm(pick_other, gq[other], TN, lax.Precision.HIGHEST)
    along = jnp.sum(grad_key * unit_key, axis=1, keepdims=True)
    grad_raw = ((grad_key - unit_key * along) / norm_key).astype(BF16)
    grad_mixed = mm(grad_raw, proj_ref[...], NT).astype(BF16)
    gm, gr = r["gm"], r["gr"]
    gm[...] = grad_mixed
    gr[...] = grad_raw
    gp[...] = (grad_mixed.astype(F32) * slope[...]).astype(BF16)

    g_up = remote(
        gp.at[pl.ds(0, cols)], gh.at[1], "gh", previous * 2 + core, at=1, sent=0
    )
    g_down = remote(
        gp.at[pl.ds(both - cols, cols)], gh.at[0], "gh", following * 2 + core, at=0, sent=1
    )

    @pl.when(has_prev)
    def _():
        g_up.start()

    @pl.when(has_next)
    def _():
        g_down.start()

    l2a_s, l2a_r, l2b_s, l2b_r = r["l2a_s"], r["l2a_r"], r["l2b_s"], r["l2b_r"]
    l3a_s, l3a_r, l3b_s, l3b_r = r["l3a_s"], r["l3a_r"], r["l3b_s"], r["l3b_r"]
    lane_group = iota((group, LANES), 1) // group
    first_block = layer // span + 1

    def weight_grad(k, carry):
        b = lax.rem(first_block + k, blocks)
        lane = pl.ds(pl.multiple_of(b * LANES, LANES), LANES)
        proj_part = mm(mixed_t[lane, :], gr[...], NN)
        full = mm(at[b], gp[:, lane], NN)
        taps = []
        for tap in range(tap_count):
            folded = jnp.zeros((group, LANES), F32)
            for g in range(per_block):
                first = tap * LANES + g * group
                folded = jnp.where(lane_group == g, full[first : first + group], folded)
            taps.append(folded)
        short = pieces * piece - tap_count * group
        if short:
            taps.append(jnp.zeros((short, LANES), F32))
        conv = jnp.concatenate(taps, axis=0)
        for j in range(pieces):
            z, p = b * span + j // inner, j % inner
            top = j * piece
            l2a_s[p, z, :prow, :] = proj_part[j * prow : (j + 1) * prow].astype(BF16)
            l2a_s[p, z, prow:, :] = conv[top : top + conv_a].astype(BF16)
            l2b_s[z, p] = conv[top + conv_a : top + piece].astype(BF16)
        for j in range(span):
            z = b * span + j
            turn(
                inner,
                place,
                lambda t: remote(
                    l2a_s.at[t, z], l2a_r.at[place, z], "l2a", near_id(t), at=z
                ).start(),
            )
            l2a_r[place, z] = l2a_s[place, z]

            @pl.when(z != layer)
            def _():
                remote(l2b_s.at[z], l2b_r.at[layer], "l2b", far_id(z)).start()

        return carry

    lax.fori_loop(0, blocks, weight_grad, 0)
    l2b_r[layer] = l2b_s[layer]
    store_shifted(gs, both, cols, gp[...], cols)

    def near_summed(k, carry):
        z = lax.rem(first_block * span + k, layers)
        view = l2a_r.at[pl.ds(0, inner - 1), z]
        remote(view, view, "l2a", partner, at=z).wait_recv()
        l3a_s[z] = jnp.sum(l2a_r[:, z].astype(F32), axis=0).astype(BF16)

        @pl.when(z != layer)
        def _():
            remote(l3a_s.at[z], l3a_r.at[layer], "l3a", far_id(z)).start()

        return carry

    lax.fori_loop(0, layers, near_summed, 0)
    l3a_r[layer] = l3a_s[layer]
    view = l2b_r.at[pl.ds(0, layers - 1)]
    remote(view, view, "l2b", partner).wait_recv()
    for p in range(inner):
        l3b_s[p] = jnp.sum(l2b_r[:, p].astype(F32), axis=0).astype(BF16)
    turn(
        inner,
        place,
        lambda t: remote(l3b_s.at[t], l3b_r.at[place], "l3b", near_id(t)).start(),
    )
    l3b_r[place] = l3b_s[place]

    edges_wait(gh, "gh")
    store_shifted(gs, cols, 0, gh[0], cols)
    store_shifted(gs, cols, cols + both, gh[1], cols)
    back_all = r["back"]

    def backward(b, carry):
        lane = pl.ds(pl.multiple_of(b * LANES, LANES), LANES)
        back = mm(windows(gs, lane, True), wt[b], NT).astype(BF16)
        back_all[:, lane] = (back.astype(F32) + gm[:, lane].astype(F32)).astype(BF16)
        return carry

    lax.fori_loop(0, blocks, backward, 0)
    out_pair = remote(
        back_all.at[pl.ds(pl.multiple_of(other * pixels, 16), pixels)],
        out_ref.at[:, my_half],
        "out",
        partner,
    )
    out_pair.start()
    out_ref[:, my_half] = back_all[my_pixels, :]

    view = l3a_r.at[pl.ds(0, layers - 1)]
    remote(view, view, "l3a", partner).wait_recv()
    ag_a[core, layer, place] = jnp.sum(l3a_r[...].astype(F32), axis=0).astype(BF16)

    def a_copy(z, at, name, target):
        chunk = ag_a.at[core, z, place]
        return remote(chunk, chunk, name, target, at=at)

    def b_copy(p, at, name, target):
        chunk = ag_b.at[core, p, layer]
        return remote(chunk, chunk, name, target, at=at)

    turn(layers, layer, lambda t: a_copy(layer, layer, "af", far_id(t)).start())
    turn(inner, place, lambda t: a_copy(layer, layer, "an", near_id(t)).start())

    view = l3b_r.at[pl.ds(0, inner - 1)]
    remote(view, view, "l3b", partner).wait_recv()
    ag_b[core, place, layer] = jnp.sum(l3b_r[...].astype(F32), axis=0).astype(BF16)
    turn(inner, place, lambda t: b_copy(place, place, "bn", near_id(t)).start())
    turn(layers, layer, lambda t: b_copy(place, place, "bf", far_id(t)).start())

    def a_arrived(z):
        chunk = ag_a.at[core, z, place]
        remote(chunk, chunk, "af", partner, at=z).wait_recv()
        turn(inner, place, lambda t: a_copy(z, z, "an", near_id(t)).start())

    def b_arrived(p):
        chunk = ag_b.at[core, p, layer]
        remote(chunk, chunk, "bn", partner, at=p).wait_recv()
        turn(layers, layer, lambda t: b_copy(p, p, "bf", far_id(t)).start())

    turn(layers, layer, a_arrived)
    turn(inner, place, b_arrived)

    def a_whole(k, carry):
        z = lax.rem(layer + k, layers)
        view = ag_a.at[core, z, pl.ds(0, inner - 1)]
        remote(view, view, "an", partner, at=z).wait_recv()
        remote(ag_a.at[core, z], ag_a.at[core, z], "ap", partner).start()
        return carry

    def b_whole(k, carry):
        p = lax.rem(place + k, inner)
        view = ag_b.at[core, p, pl.ds(0, layers - 1)]
        remote(view, view, "bf", partner, at=p).wait_recv()
        remote(ag_b.at[core, p], ag_b.at[core, p], "bp", partner).start()
        return carry

    lax.fori_loop(0, layers, a_whole, 0)
    lax.fori_loop(0, inner, b_whole, 0)

    @pl.when(sends_up)
    def _():
        for copy in up_edge:
            copy.wait_send()

    @pl.when(sends_down)
    def _():
        for copy in down_edge:
            copy.wait_send()

    @pl.when(has_prev)
    def _():
        g_up.wait_send()

    @pl.when(has_next)
    def _():
        g_down.wait_send()

    for copy in (x_pair, rk_pair, pos_pair, q_pair, tot_pair, gq_pair):
        copy.wait_send()
    sent_chips(posb.at[core], "pos")
    sent_chips(qall.at[core], "q")
    sent_chips(pps, "pp")
    sent_chips(totb, "tot")
    sent_chips(ws, "wp")

    def sent(view, name, at=None):
        remote(view, view, name, partner, at=at).wait_send()

    sent(l2a_s.at[pl.ds(0, inner - 1)], "l2a", 0)
    sent(l2b_s.at[pl.ds(0, layers - 1)], "l2b")
    sent(l3a_s.at[pl.ds(0, layers - 1)], "l3a")
    sent(l3b_s.at[pl.ds(0, inner - 1)], "l3b")
    sent(ag_a.at[core, pl.ds(0, layers - 1), 0], "af", 0)
    sent(ag_a.at[core, :, pl.ds(0, inner - 1)], "an", 0)
    sent(ag_b.at[core, pl.ds(0, inner - 1), 0], "bn", 0)
    sent(ag_b.at[core, :, pl.ds(0, layers - 1)], "bf", 0)
    out_pair.wait()
    sent(ag_a.at[core], "ap")
    sent(ag_b.at[core], "bp")
    remote(ag_a.at[other], ag_a.at[other], "ap", partner).wait_recv()
    remote(ag_b.at[other], ag_b.at[other], "bp", partner).wait_recv()


def finish(geometry, gf_ref, ag_a, ag_b, loss_ref, gf_out, gw_out, gp_out, loss_out, gw, gp, sems):
    blocks, inner, pieces, piece, prow = geometry
    _, layers, _, rows_a, _ = ag_a.shape
    chips = layers * inner
    moves = [pltpu.make_async_copy(gf_ref, gf_out, sems.at[0])]
    moves[0].start()
    loss_out[...] = loss_ref[...]
    height = gw_out.shape[0]
    conv_a = rows_a - prow
    for j in range(pieces):
        first = j * piece
        stop = min(height, first + piece)
        for b in range(blocks):
            side, i = b // (blocks // 2), b % (blocks // 2) * pieces + j
            lane = slice(b * LANES, (b + 1) * LANES)
            z, p = i // inner, i % inner
            first_p = (side * chips + i) * prow
            gp[first_p : first_p + prow, :] = ag_a[side, z, p, :prow, :].astype(F32)
            top = min(conv_a, max(stop - first, 0))
            if top > 0:
                gw[first : first + top, lane] = ag_a[side, z, p, prow : prow + top, :].astype(F32)
            low = stop - first - conv_a
            if low > 0:
                gw[first + conv_a : stop, lane] = ag_b[side, p, z, :low, :].astype(F32)
        if stop > first:
            rows = pl.ds(first, stop - first)
            moves.append(pltpu.make_async_copy(gw.at[rows], gw_out.at[rows], sems.at[2 + j]))
            moves[-1].start()
    moves.append(pltpu.make_async_copy(gp, gp_out, sems.at[1]))
    moves[-1].start()
    for move in moves:
        move.wait()


def per_device(devices, batches, features, conv_weight, proj_weight, anchor_pixel, positive_pixel):
    rows_dev, cols, images, channels = features.shape
    group = conv_weight.shape[2]
    key_width = proj_weight.shape[1]
    anchors_dev = anchor_pixel.shape[0]
    chips = devices // 2
    inner = min(4, chips)
    layers = chips // inner
    pixels = rows_dev * cols
    both = 2 * pixels
    half = channels // 2
    taps = conv_weight.shape[0] * conv_weight.shape[1]
    blocks = half // LANES
    pieces = chips // blocks
    piece = -(-(taps * group) // pieces)
    piece = -(-piece // 8) * 8
    prow = channels // devices
    rows_a = (prow + piece) * 5 // 8 // 16 * 16
    rows_b = prow + piece - rows_a
    anchors_core = anchors_dev * chips
    anchor_count = anchors_core * 2 * images * batches
    gradient_scale = 1.0 / (SOFTMAX_TEMPER * anchor_count)
    tot_rows = anchors_core // LANES + 1
    padded = both + 2 * cols
    dma = pltpu.SemaphoreType.DMA
    vmem = pltpu.VMEM
    whole = pl.BlockSpec(memory_space=pltpu.VMEM)
    hbm = pl.BlockSpec(memory_space=pltpu.HBM)
    part = (chips, anchors_dev, LANES)
    scratch = {
        "xa": vmem((both, half), BF16),
        "w": vmem((taps, group, half), BF16),
        "proj": vmem((half, key_width), BF16),
        "anchor": vmem((1, anchors_dev), jnp.int32),
        "positive": vmem((1, anchors_dev), jnp.int32),
        "xh": vmem((2, cols, half), BF16),
        "gh": vmem((2, cols, half), BF16),
        "xs": vmem((3, padded, half), BF16),
        "gs": vmem((3, padded, half), BF16),
        "wn": vmem((blocks, taps * LANES, LANES), BF16),
        "wt": vmem((blocks, LANES, taps * LANES), BF16),
        "at": vmem((blocks, taps * LANES, both), BF16),
        "mixed": vmem((both, half), BF16),
        "mixed_t": vmem((half, both), BF16),
        "slope": vmem((both, half), F32),
        "rks": vmem((both, key_width), F32),
        "rkr": vmem((both, key_width), F32),
        "posb": vmem((2, chips, 1, LANES), F32),
        "qall": vmem((2, *part), BF16),
        "pps": vmem(part, BF16),
        "ppr": vmem(part, BF16),
        "ws": vmem(part, BF16),
        "wr": vmem(part, BF16),
        "totb": vmem((chips, tot_rows, LANES), F32),
        "tfin": vmem((2, tot_rows, LANES), F32),
        "gq": vmem((2, anchors_dev, LANES), F32),
        "gm": vmem((both, half), BF16),
        "gp": vmem((both, half), BF16),
        "gr": vmem((both, key_width), BF16),
        "back": vmem((both, half), BF16),
        "l2a_s": vmem((inner, layers, rows_a, LANES), BF16),
        "l2a_r": vmem((inner, layers, rows_a, LANES), BF16),
        "l2b_s": vmem((layers, inner, rows_b, LANES), BF16),
        "l2b_r": vmem((layers, inner, rows_b, LANES), BF16),
        "l3a_s": vmem((layers, rows_a, LANES), BF16),
        "l3a_r": vmem((layers, rows_a, LANES), BF16),
        "l3b_s": vmem((inner, rows_b, LANES), BF16),
        "l3b_r": vmem((inner, rows_b, LANES), BF16),
        "load": dma((5,)),
    }
    singles = ("xp", "rk", "pos", "posp", "q", "qp", "pp", "tot", "totp", "wp", "gqp")
    for name in (*singles, "l2b", "l3a", "l3b", "out", "ap", "bp"):
        scratch[name + "_send"] = dma
        scratch[name + "_recv"] = dma
    for name in ("xh", "gh"):
        scratch[name + "_send"] = dma((2,))
        scratch[name + "_recv"] = dma((2,))
    for name, count in (("l2a", layers), ("af", layers), ("an", layers), ("bn", inner), ("bf", inner)):
        scratch[name + "_send"] = dma
        scratch[name + "_recv"] = dma((count,))
    names = ["x_hbm", "w_hbm", "proj_hbm", "anchor_hbm", "positive_hbm"]
    names += ["out", "ag_a", "ag_b", "loss", *scratch]
    sums = (
        jax.ShapeDtypeStruct((pixels, channels), BF16),
        jax.ShapeDtypeStruct((2, layers, inner, rows_a, LANES), BF16),
        jax.ShapeDtypeStruct((2, inner, layers, rows_b, LANES), BF16),
        jax.ShapeDtypeStruct((1, 1), F32),
    )
    parts = pl.pallas_call(
        functools.partial(
            kernel,
            names,
            devices,
            gradient_scale,
            (cols, group, pieces, piece, prow, inner, anchor_count),
        ),
        out_shape=sums,
        in_specs=[hbm] * 5,
        out_specs=(whole,) * 4,
        scratch_shapes=list(scratch.values()),
        compiler_params=pltpu.CompilerParams(
            collective_id=0, has_side_effects=True, vmem_limit_bytes=26000 * 1024
        ),
    )(
        in_hbm(features.reshape(pixels, channels)),
        in_hbm(conv_weight.reshape(taps, group, channels)),
        in_hbm(proj_weight),
        in_hbm(anchor_pixel.reshape(1, anchors_dev)),
        in_hbm(positive_pixel.reshape(1, anchors_dev)),
    )
    grad_features, grad_conv, grad_proj, loss = pl.pallas_call(
        functools.partial(finish, (2 * blocks, inner, pieces, piece, prow)),
        out_shape=(
            jax.ShapeDtypeStruct((pixels, channels), BF16),
            jax.ShapeDtypeStruct((taps * group, channels), F32),
            jax.ShapeDtypeStruct((channels, key_width), F32),
            jax.ShapeDtypeStruct((1, 1), F32),
        ),
        in_specs=[whole] * 4,
        out_specs=(hbm,) * 3 + (whole,),
        scratch_shapes=[
            vmem((taps * group, channels), F32),
            vmem((channels, key_width), F32),
            dma((2 + pieces,)),
        ],
        compiler_params=pltpu.CompilerParams(vmem_limit_bytes=16000 * 1024),
    )(*parts)
    grad_conv = grad_conv.reshape(conv_weight.shape)
    loss_value = loss.reshape(())
    if batches > 1:
        grad_conv, grad_proj, loss_value = lax.psum((grad_conv, grad_proj, loss_value), "batch")
    return (grad_features.reshape(features.shape), grad_conv, grad_proj, loss_value)


def solution(mesh):
    placed = (P("wide", None, "batch", None), P(), P(), P("wide", "batch"), P("wide", "batch"))
    return jax.shard_map(
        functools.partial(per_device, mesh.shape["wide"], mesh.shape["batch"]),
        mesh=mesh,
        in_specs=placed,
        out_specs=(P("wide", None, "batch", None), P(), P(), P()),
        check_vma=False,
    )
```

```python
import functools

import jax
import jax.numpy as jnp
from jax import lax
from jax.experimental import pallas as pl
from jax.experimental.pallas import tpu as pltpu
from jax.sharding import PartitionSpec as P

SOFTMAX_TEMPER = 0.1
EPSILON = 1e-06
LANES = 128
F32 = jnp.float32
BF16 = jnp.bfloat16
MESH = pl.DeviceIdType.MESH

NN = (((1,), (0,)), ((), ()))
NT = (((1,), (1,)), ((), ()))
TN = (((0,), (0,)), ((), ()))


def mm(a, b, dims, precision=None):
    return lax.dot_general(a, b, dims, preferred_element_type=F32, precision=precision)


def in_hbm(array):
    return pltpu.with_memory_space_constraint(array, pltpu.HBM)


def iota(shape, dim):
    return lax.broadcasted_iota(jnp.int32, shape, dim)


def store_shifted(dst, rows, start, values, cols):
    wide = values.astype(F32)
    count = wide.shape[0]
    col = iota(wide.shape, 0) % cols
    dst[1, start : start + rows] = values
    left = jnp.where(col == 0, 0.0, pltpu.roll(wide, 1, 0))
    dst[0, start : start + rows] = left.astype(BF16)
    right = jnp.where(col == cols - 1, 0.0, pltpu.roll(wide, count - 1, 0))
    dst[2, start : start + rows] = right.astype(BF16)


def kernel(names, devices, gradient_scale, geometry, *refs):
    r = dict(zip(names, refs, strict=True))
    cols, group, pieces, piece, prow, inner, anchor_count = geometry
    x_hbm, out_ref, ag_a, ag_b = r["x_hbm"], r["out"], r["ag_a"], r["ag_b"]
    pixels = x_hbm.shape[0]
    channels = x_hbm.shape[1]
    half = channels // 2
    blocks = half // LANES
    per_block = LANES // group
    anchors_dev = r["anchor"].shape[1]
    chips = devices // 2
    both = 2 * pixels
    anchors_core = chips * anchors_dev
    me = lax.axis_index("wide")
    core = lax.rem(me, 2)
    chip = me // 2
    other = 1 - core
    partner = chip * 2 + other
    place = lax.rem(chip, inner)
    layer = chip // inner
    layers = chips // inner
    span = pieces // inner
    conv_a = ag_a.shape[3] - prow
    barrier = pltpu.get_barrier_semaphore()

    def turn(count, start, body):
        def step(k, carry):
            body(lax.rem(start + k, count))
            return carry

        lax.fori_loop(1, count, step, 0)

    def other_chips(body):
        def layer_step(k, carry):
            z = jnp.where(layer < layers // 2, layers - 1 - k, k)

            def step(j, carry):
                t = z * inner + lax.rem(place + inner - 1 - j, inner)

                @pl.when(t != chip)
                def _():
                    body(t)

                return carry

            return lax.fori_loop(0, inner, step, carry, unroll=True)

        lax.fori_loop(0, layers, layer_step, 0)

    def near_id(target):
        return (layer * inner + target) * 2 + core

    def far_id(target):
        return (target * inner + place) * 2 + core

    def remote(src, dst, name, target, at=None, sent=None):
        recv = r[name + "_recv"]
        send = r[name + "_send"]
        return pltpu.make_async_remote_copy(
            src_ref=src,
            dst_ref=dst,
            send_sem=send if sent is None else send.at[sent],
            recv_sem=recv if at is None else recv.at[at],
            device_id={"wide": target},
            device_id_type=MESH,
        )

    def to_chips(source, landing, name):
        other_chips(lambda t: remote(source(t), landing, name, t * 2 + core).start())

    def from_chips(buf, name):
        view = buf.at[pl.ds(0, chips - 1)]
        remote(view, view, name, partner).wait_recv()

    def sent_chips(buf, name):
        view = buf.at[pl.ds(0, chips - 1)]
        remote(view, view, name, partner).wait_send()

    def signal_entry(target):
        pl.semaphore_signal(barrier, inc=1, device_id={"wide": target}, device_id_type=MESH)

    has_prev = chip > 0
    has_next = chip < chips - 1
    previous = lax.rem(chip + chips - 1, chips)
    following = lax.rem(chip + 1, chips)
    my_half = pl.ds(pl.multiple_of(core * half, LANES), half)
    your_half = pl.ds(pl.multiple_of(other * half, LANES), half)
    my_pixels = pl.ds(pl.multiple_of(core * pixels, 16), pixels)

    loads = [
        pltpu.make_async_copy(src, dst, r["load"].at[n])
        for n, (src, dst) in enumerate(
            (
                (r["positive_hbm"], r["positive"]),
                (r["w_hbm"].at[:, :, my_half], r["w"]),
                (x_hbm.at[:, my_half], r["xa"].at[my_pixels]),
                (r["proj_hbm"].at[my_half], r["proj"]),
                (r["anchor_hbm"], r["anchor"]),
            )
        )
    ]
    for copy in loads:
        copy.start()

    @pl.when(has_prev)
    def _():
        signal_entry(previous * 2 + other)

    @pl.when(has_next)
    def _():
        signal_entry(following * 2 + other)

    signal_entry(partner)

    def greet(k, carry):
        signal_entry(lax.rem(chip + k, chips) * 2 + core)
        signal_entry(lax.rem(chip + chips - k, chips) * 2 + core)
        return carry

    lax.fori_loop(1, chips // 2, greet, 0)
    signal_entry(lax.rem(chip + chips // 2, chips) * 2 + core)
    pl.semaphore_wait(barrier, chips + has_prev.astype(jnp.int32) + has_next.astype(jnp.int32))

    xh, gh, xa, gp = r["xh"], r["gh"], r["xa"], r["gp"]

    def x_edge(source, slot, target):
        return [
            remote(
                x_hbm.at[pl.ds(source, cols), pl.ds(t * half, half)],
                xh.at[slot],
                "xh",
                target * 2 + t,
                at=slot,
                sent=t,
            )
            for t in range(2)
        ]

    up_edge = x_edge(0, 1, previous)
    down_edge = x_edge(pixels - cols, 0, following)
    sends_up = jnp.logical_and(core == 0, has_prev)
    sends_down = jnp.logical_and(core == 1, has_next)

    @pl.when(sends_up)
    def _():
        for copy in up_edge:
            copy.start()

    @pl.when(sends_down)
    def _():
        for copy in down_edge:
            copy.start()

    x_pair = remote(x_hbm.at[:, your_half], xa.at[my_pixels], "xp", partner)
    x_pair.start()

    def edges_wait(buf, name):
        @pl.when(has_prev)
        def _():
            remote(buf.at[0], buf.at[0], name, partner, at=0, sent=0).wait_recv()

        @pl.when(jnp.logical_not(has_prev))
        def _():
            buf[0] = jnp.zeros(buf.shape[1:], buf.dtype)

        @pl.when(has_next)
        def _():
            remote(buf.at[1], buf.at[1], name, partner, at=1, sent=1).wait_recv()

        @pl.when(jnp.logical_not(has_next))
        def _():
            buf[1] = jnp.zeros(buf.shape[1:], buf.dtype)

    for copy in loads:
        copy.wait()
    posb = r["posb"]
    posb[core, chip, :, :anchors_dev] = r["positive"][...].astype(F32)
    posb[core, chip, :, anchors_dev : 2 * anchors_dev] = r["anchor"][...].astype(F32)
    posb[core, chip, :, 2 * anchors_dev :] = jnp.zeros((1, LANES - 2 * anchors_dev), F32)
    to_chips(lambda t: posb.at[core, chip], posb.at[core, chip], "pos")

    w_ref, wn, wt, at = r["w"], r["wn"], r["wt"], r["at"]
    tap_count = w_ref.shape[0]
    diagonal = iota((LANES, LANES), 0) // group == iota((LANES, LANES), 1) // group

    def build(b, carry):
        lane = pl.ds(pl.multiple_of(b * LANES, LANES), LANES)
        for tap in range(tap_count):
            slab = w_ref[tap, :, lane].astype(F32)
            full = jnp.where(diagonal, jnp.concatenate([slab] * per_block, axis=0), 0.0)
            full = full.astype(BF16)
            wn[b, tap * LANES : (tap + 1) * LANES, :] = full
            wt[b, :, tap * LANES : (tap + 1) * LANES] = full
        return carry

    lax.fori_loop(0, blocks, build, 0)
    xs, gs = r["xs"], r["gs"]
    x_pair.wait_recv()
    store_shifted(xs, both, cols, xa[...], cols)

    def diagonal_col(row, first):
        lane = iota((anchors_dev, LANES), 1)
        hit = lane == iota((anchors_dev, LANES), 0) + first
        return jnp.sum(jnp.where(hit, row, 0.0), axis=1, keepdims=True)

    def pick_of(row, owner):
        column = diagonal_col(row, anchors_dev) + (owner * pixels).astype(F32)
        return jnp.where(iota((anchors_dev, both), 1).astype(F32) == column, 1.0, 0.0)

    pick_own = pick_of(posb[core, chip], core)
    edges_wait(xh, "xh")
    store_shifted(xs, cols, 0, xh[0], cols)
    store_shifted(xs, cols, cols + both, xh[1], cols)

    def windows(buf, lane, flip):
        parts = []
        for row in range(3):
            for col in range(3):
                rr, cc = (2 - row, 2 - col) if flip else (row, col)
                parts.append(buf[cc, rr * cols : rr * cols + both, lane])
        return jnp.concatenate(parts, axis=1)

    mixed, mixed_t, slope, proj_ref = r["mixed"], r["mixed_t"], r["slope"], r["proj"]

    def forward(b, carry):
        lane = pl.ds(pl.multiple_of(b * LANES, LANES), LANES)
        pre = mm(windows(xs, lane, False), wn[b], NN)
        sig = 1.0 / (1.0 + jnp.exp(-pre))
        mixed[:, lane] = (xa[:, lane].astype(F32) + pre * sig).astype(BF16)
        slope[:, lane] = sig * (1.0 + pre * (1.0 - sig))
        return carry

    lax.fori_loop(0, blocks, forward, 0)

    rks, rkr = r["rks"], r["rkr"]
    rks[...] = mm(mixed[...], proj_ref[...], NN)
    rk_pair = remote(rks, rkr, "rk", partner)
    rk_pair.start()
    from_chips(posb.at[core], "pos")
    pos_pair = remote(posb.at[core], posb.at[core], "posp", partner)
    pos_pair.start()
    rk_pair.wait_recv()
    raw_key = rks[...] + rkr[...]
    norm_key = jnp.sqrt(jnp.sum(raw_key * raw_key, axis=1, keepdims=True) + EPSILON)
    unit_key = raw_key / norm_key
    keys = unit_key.astype(BF16)
    qall = r["qall"]
    qall[core, chip] = mm(pick_own.astype(BF16), keys, NN).astype(BF16)
    to_chips(lambda t: qall.at[core, chip], qall.at[core, chip], "q")

    def hits(parity):
        own_lane = iota((chips, anchors_dev, LANES), 1) == iota((chips, anchors_dev, LANES), 2)
        pos_all = jnp.sum(jnp.where(own_lane, posb[parity], 0.0), axis=2, keepdims=True)
        pos_local = pos_all - (chip * both).astype(F32)
        hit3 = jnp.where(
            iota((chips, anchors_dev, both), 2).astype(F32) == pos_local, 1.0, 0.0
        )
        return hit3.reshape(anchors_core, both).astype(BF16)

    hit_own = hits(core)
    part_pos = mm(hit_own, keys, NN)
    pps, ppr = r["pps"], r["ppr"]
    pps[...] = part_pos.reshape(chips, anchors_dev, LANES).astype(BF16)
    to_chips(lambda t: pps.at[t], ppr.at[chip], "pp")
    ppr[chip] = pps[chip]

    def flip_over(b, carry):
        start = pl.multiple_of(b * LANES, LANES)
        lane = pl.ds(start, LANES)
        at[b] = windows(xs, lane, False).T
        mixed_t[lane, :] = mixed[:, lane].T
        return carry

    lax.fori_loop(0, blocks, flip_over, 0)
    pos_pair.wait_recv()
    hit_other = hits(other)
    pick_other = pick_of(posb[other, chip], other)

    from_chips(qall.at[core], "q")
    q_pair = remote(qall.at[core], qall.at[core], "qp", partner)
    q_pair.start()
    queries = qall[core].reshape(anchors_core, LANES)
    exp_own = jnp.exp(mm(keys, queries, NT) / SOFTMAX_TEMPER)
    part_total = jnp.sum(exp_own, axis=0, keepdims=True)
    pos_sum = jnp.sum(
        jnp.sum(part_pos * queries.astype(F32), axis=1, keepdims=True), axis=0, keepdims=True
    )
    totb, tfin = r["totb"], r["tfin"]
    tot_rows = anchors_core // LANES
    for n in range(tot_rows):
        totb[chip, n : n + 1, :] = part_total[:, n * LANES : (n + 1) * LANES]
    totb[chip, tot_rows : tot_rows + 1, :] = jnp.broadcast_to(pos_sum, (1, LANES))
    to_chips(lambda t: totb.at[chip], totb.at[chip], "tot")
    part_weighted = mm(exp_own.astype(BF16), keys, TN)
    ws, wr = r["ws"], r["wr"]
    ws[...] = part_weighted.reshape(chips, anchors_dev, LANES).astype(BF16)
    to_chips(lambda t: ws.at[t], wr.at[chip], "wp")
    wr[chip] = ws[chip]

    q_pair.wait_recv()
    queries_other = qall[other].reshape(anchors_core, LANES)
    exp_other = jnp.exp(mm(keys, queries_other, NT) / SOFTMAX_TEMPER)
    pushed = mm(hit_own, queries, TN) + mm(hit_other, queries_other, TN)

    def whole_row(sums):
        return jnp.concatenate([sums[n : n + 1, :] for n in range(tot_rows)], axis=1)

    def loss_of(sums, row):
        return jnp.sum(jnp.log(row), axis=1, keepdims=True) - sums[
            tot_rows : tot_rows + 1, 0:1
        ] / SOFTMAX_TEMPER

    def pulled_by(exp_scores, row, asked):
        inverse = (1.0 / row).astype(BF16).astype(F32)
        return mm((exp_scores * inverse).astype(BF16), asked, NN)

    from_chips(totb, "tot")
    sums_own = jnp.sum(totb[...], axis=0)
    tfin[core] = sums_own
    tot_pair = remote(tfin.at[core], tfin.at[core], "totp", partner)
    tot_pair.start()
    row_own = whole_row(sums_own)
    mine = iota((anchors_dev, anchors_core), 1) == chip * anchors_dev + iota(
        (anchors_dev, anchors_core), 0
    )
    own_total = jnp.sum(jnp.where(mine, row_own, 0.0), axis=1, keepdims=True)
    gq = r["gq"]
    from_chips(ppr, "pp")
    from_chips(wr, "wp")
    weighted = jnp.sum(wr[...].astype(F32), axis=0)
    pos_key = jnp.sum(ppr[...].astype(F32), axis=0)
    gq[core] = (weighted / own_total - pos_key) * gradient_scale
    gq_pair = remote(gq.at[core], gq.at[core], "gqp", partner)
    gq_pair.start()
    pulled = pulled_by(exp_own, row_own, queries)
    tot_pair.wait_recv()
    sums_other = tfin[other]
    row_other = whole_row(sums_other)
    pulled = pulled + pulled_by(exp_other, row_other, queries_other)
    r["loss"][...] = (loss_of(sums_own, row_own) + loss_of(sums_other, row_other)) / anchor_count
    grad_key = gradient_scale * (pulled - pushed)
    gq_pair.wait_recv()
    grad_key = grad_key + mm(pick_own, gq[core], TN, lax.Precision.HIGHEST)
    grad_key = grad_key + mm(pick_other, gq[other], TN, lax.Precision.HIGHEST)
    along = jnp.sum(grad_key * unit_key, axis=1, keepdims=True)
    grad_raw = ((grad_key - unit_key * along) / norm_key).astype(BF16)
    grad_mixed = mm(grad_raw, proj_ref[...], NT).astype(BF16)
    gm, gr = r["gm"], r["gr"]
    gm[...] = grad_mixed
    gr[...] = grad_raw
    gp[...] = (grad_mixed.astype(F32) * slope[...]).astype(BF16)

    g_up = remote(
        gp.at[pl.ds(0, cols)], gh.at[1], "gh", previous * 2 + core, at=1, sent=0
    )
    g_down = remote(
        gp.at[pl.ds(both - cols, cols)], gh.at[0], "gh", following * 2 + core, at=0, sent=1
    )

    l2a_s, l2a_r, l2b_s, l2b_r = r["l2a_s"], r["l2a_r"], r["l2b_s"], r["l2b_r"]
    l3a_s, l3a_r, l3b_s, l3b_r = r["l3a_s"], r["l3a_r"], r["l3b_s"], r["l3b_r"]
    lane_group = iota((group, LANES), 1) // group
    first_block = layer // span + 1

    def weight_grad(k, carry):
        b = lax.rem(first_block + k, blocks)
        lane = pl.ds(pl.multiple_of(b * LANES, LANES), LANES)
        proj_part = mm(mixed_t[lane, :], gr[...], NN)
        full = mm(at[b], gp[:, lane], NN)
        taps = []
        for tap in range(tap_count):
            folded = jnp.zeros((group, LANES), F32)
            for g in range(per_block):
                first = tap * LANES + g * group
                folded = jnp.where(lane_group == g, full[first : first + group], folded)
            taps.append(folded)
        short = pieces * piece - tap_count * group
        if short:
            taps.append(jnp.zeros((short, LANES), F32))
        conv = jnp.concatenate(taps, axis=0)
        for j in range(pieces):
            z, p = b * span + j // inner, j % inner
            top = j * piece
            l2a_s[p, z, :prow, :] = proj_part[j * prow : (j + 1) * prow].astype(BF16)
            l2a_s[p, z, prow:, :] = conv[top : top + conv_a].astype(BF16)
            l2b_s[z, p] = conv[top + conv_a : top + piece].astype(BF16)
        for j in range(span):
            z = b * span + j
            turn(
                inner,
                place,
                lambda t: remote(
                    l2a_s.at[t, z], l2a_r.at[place, z], "l2a", near_id(t), at=z
                ).start(),
            )
            l2a_r[place, z] = l2a_s[place, z]

            @pl.when(z != layer)
            def _():
                remote(l2b_s.at[z], l2b_r.at[layer], "l2b", far_id(z)).start()

        return carry

    lax.fori_loop(0, blocks, weight_grad, 0)
    @pl.when(has_prev)
    def _():
        g_up.start()

    @pl.when(has_next)
    def _():
        g_down.start()

    l2b_r[layer] = l2b_s[layer]
    store_shifted(gs, both, cols, gp[...], cols)

    def near_summed(k, carry):
        z = lax.rem(first_block * span + k, layers)
        view = l2a_r.at[pl.ds(0, inner - 1), z]
        remote(view, view, "l2a", partner, at=z).wait_recv()
        l3a_s[z] = jnp.sum(l2a_r[:, z].astype(F32), axis=0).astype(BF16)

        @pl.when(z != layer)
        def _():
            remote(l3a_s.at[z], l3a_r.at[layer], "l3a", far_id(z)).start()

        return carry

    lax.fori_loop(0, layers, near_summed, 0)
    l3a_r[layer] = l3a_s[layer]
    view = l2b_r.at[pl.ds(0, layers - 1)]
    remote(view, view, "l2b", partner).wait_recv()
    for p in range(inner):
        l3b_s[p] = jnp.sum(l2b_r[:, p].astype(F32), axis=0).astype(BF16)
    turn(
        inner,
        place,
        lambda t: remote(l3b_s.at[t], l3b_r.at[place], "l3b", near_id(t)).start(),
    )
    l3b_r[place] = l3b_s[place]

    view = l3a_r.at[pl.ds(0, layers - 1)]
    remote(view, view, "l3a", partner).wait_recv()
    ag_a[core, layer, place] = jnp.sum(l3a_r[...].astype(F32), axis=0).astype(BF16)

    def a_copy(z, at, name, target):
        chunk = ag_a.at[core, z, place]
        return remote(chunk, chunk, name, target, at=at)

    def b_copy(p, at, name, target):
        chunk = ag_b.at[core, p, layer]
        return remote(chunk, chunk, name, target, at=at)

    turn(layers, layer, lambda t: a_copy(layer, layer, "af", far_id(t)).start())
    turn(inner, place, lambda t: a_copy(layer, layer, "an", near_id(t)).start())

    view = l3b_r.at[pl.ds(0, inner - 1)]
    remote(view, view, "l3b", partner).wait_recv()
    ag_b[core, place, layer] = jnp.sum(l3b_r[...].astype(F32), axis=0).astype(BF16)
    turn(inner, place, lambda t: b_copy(place, place, "bn", near_id(t)).start())
    turn(layers, layer, lambda t: b_copy(place, place, "bf", far_id(t)).start())

    edges_wait(gh, "gh")
    store_shifted(gs, cols, 0, gh[0], cols)
    store_shifted(gs, cols, cols + both, gh[1], cols)
    back_all = r["back"]

    def backward(b, carry):
        lane = pl.ds(pl.multiple_of(b * LANES, LANES), LANES)
        back = mm(windows(gs, lane, True), wt[b], NT).astype(BF16)
        back_all[:, lane] = (back.astype(F32) + gm[:, lane].astype(F32)).astype(BF16)
        return carry

    lax.fori_loop(0, blocks, backward, 0)
    out_pair = remote(
        back_all.at[pl.ds(pl.multiple_of(other * pixels, 16), pixels)],
        out_ref.at[:, my_half],
        "out",
        partner,
    )
    out_pair.start()
    out_ref[:, my_half] = back_all[my_pixels, :]

    def a_arrived(z):
        chunk = ag_a.at[core, z, place]
        remote(chunk, chunk, "af", partner, at=z).wait_recv()
        turn(inner, place, lambda t: a_copy(z, z, "an", near_id(t)).start())

    def b_arrived(p):
        chunk = ag_b.at[core, p, layer]
        remote(chunk, chunk, "bn", partner, at=p).wait_recv()
        turn(layers, layer, lambda t: b_copy(p, p, "bf", far_id(t)).start())

    turn(layers, layer, a_arrived)
    turn(inner, place, b_arrived)

    def a_whole(k, carry):
        z = lax.rem(layer + k, layers)
        view = ag_a.at[core, z, pl.ds(0, inner - 1)]
        remote(view, view, "an", partner, at=z).wait_recv()
        remote(ag_a.at[core, z], ag_a.at[core, z], "ap", partner).start()
        return carry

    def b_whole(k, carry):
        p = lax.rem(place + k, inner)
        view = ag_b.at[core, p, pl.ds(0, layers - 1)]
        remote(view, view, "bf", partner, at=p).wait_recv()
        remote(ag_b.at[core, p], ag_b.at[core, p], "bp", partner).start()
        return carry

    lax.fori_loop(0, layers, a_whole, 0)
    lax.fori_loop(0, inner, b_whole, 0)

    @pl.when(sends_up)
    def _():
        for copy in up_edge:
            copy.wait_send()

    @pl.when(sends_down)
    def _():
        for copy in down_edge:
            copy.wait_send()

    @pl.when(has_prev)
    def _():
        g_up.wait_send()

    @pl.when(has_next)
    def _():
        g_down.wait_send()

    for copy in (x_pair, rk_pair, pos_pair, q_pair, tot_pair, gq_pair):
        copy.wait_send()
    sent_chips(posb.at[core], "pos")
    sent_chips(qall.at[core], "q")
    sent_chips(pps, "pp")
    sent_chips(totb, "tot")
    sent_chips(ws, "wp")

    def sent(view, name, at=None):
        remote(view, view, name, partner, at=at).wait_send()

    sent(l2a_s.at[pl.ds(0, inner - 1)], "l2a", 0)
    sent(l2b_s.at[pl.ds(0, layers - 1)], "l2b")
    sent(l3a_s.at[pl.ds(0, layers - 1)], "l3a")
    sent(l3b_s.at[pl.ds(0, inner - 1)], "l3b")
    sent(ag_a.at[core, pl.ds(0, layers - 1), 0], "af", 0)
    sent(ag_a.at[core, :, pl.ds(0, inner - 1)], "an", 0)
    sent(ag_b.at[core, pl.ds(0, inner - 1), 0], "bn", 0)
    sent(ag_b.at[core, :, pl.ds(0, layers - 1)], "bf", 0)
    out_pair.wait()
    sent(ag_a.at[core], "ap")
    sent(ag_b.at[core], "bp")
    remote(ag_a.at[other], ag_a.at[other], "ap", partner).wait_recv()
    remote(ag_b.at[other], ag_b.at[other], "bp", partner).wait_recv()


def finish(geometry, gf_ref, ag_a, ag_b, loss_ref, gf_out, gw_out, gp_out, loss_out, gw, gp, sems):
    blocks, inner, pieces, piece, prow = geometry
    _, layers, _, rows_a, _ = ag_a.shape
    chips = layers * inner
    moves = [pltpu.make_async_copy(gf_ref, gf_out, sems.at[0])]
    moves[0].start()
    moves.append(pltpu.make_async_copy(loss_ref, loss_out, sems.at[2 + pieces]))
    moves[-1].start()
    height = gw_out.shape[0]
    conv_a = rows_a - prow
    for j in range(pieces):
        first = j * piece
        stop = min(height, first + piece)
        for b in range(blocks):
            side, i = b // (blocks // 2), b % (blocks // 2) * pieces + j
            lane = slice(b * LANES, (b + 1) * LANES)
            z, p = i // inner, i % inner
            first_p = (side * chips + i) * prow
            gp[first_p : first_p + prow, :] = ag_a[side, z, p, :prow, :].astype(F32)
            top = min(conv_a, max(stop - first, 0))
            if top > 0:
                gw[first : first + top, lane] = ag_a[side, z, p, prow : prow + top, :].astype(F32)
            low = stop - first - conv_a
            if low > 0:
                gw[first + conv_a : stop, lane] = ag_b[side, p, z, :low, :].astype(F32)
        if stop > first:
            rows = pl.ds(first, stop - first)
            moves.append(pltpu.make_async_copy(gw.at[rows], gw_out.at[rows], sems.at[2 + j]))
            moves[-1].start()
    moves.append(pltpu.make_async_copy(gp, gp_out, sems.at[1]))
    moves[-1].start()
    for move in moves:
        move.wait()


def per_device(devices, batches, features, conv_weight, proj_weight, anchor_pixel, positive_pixel):
    rows_dev, cols, images, channels = features.shape
    group = conv_weight.shape[2]
    key_width = proj_weight.shape[1]
    anchors_dev = anchor_pixel.shape[0]
    chips = devices // 2
    inner = min(4, chips)
    layers = chips // inner
    pixels = rows_dev * cols
    both = 2 * pixels
    half = channels // 2
    taps = conv_weight.shape[0] * conv_weight.shape[1]
    blocks = half // LANES
    pieces = chips // blocks
    piece = -(-(taps * group) // pieces)
    piece = -(-piece // 8) * 8
    prow = channels // devices
    rows_a = (prow + piece) * 4 // 5 // 16 * 16
    rows_b = prow + piece - rows_a
    anchors_core = anchors_dev * chips
    anchor_count = anchors_core * 2 * images * batches
    gradient_scale = 1.0 / (SOFTMAX_TEMPER * anchor_count)
    tot_rows = anchors_core // LANES + 1
    padded = both + 2 * cols
    dma = pltpu.SemaphoreType.DMA
    vmem = pltpu.VMEM
    whole = pl.BlockSpec(memory_space=pltpu.VMEM)
    hbm = pl.BlockSpec(memory_space=pltpu.HBM)
    part = (chips, anchors_dev, LANES)
    scratch = {
        "xa": vmem((both, half), BF16),
        "w": vmem((taps, group, half), BF16),
        "proj": vmem((half, key_width), BF16),
        "anchor": vmem((1, anchors_dev), jnp.int32),
        "positive": vmem((1, anchors_dev), jnp.int32),
        "xh": vmem((2, cols, half), BF16),
        "gh": vmem((2, cols, half), BF16),
        "xs": vmem((3, padded, half), BF16),
        "gs": vmem((3, padded, half), BF16),
        "wn": vmem((blocks, taps * LANES, LANES), BF16),
        "wt": vmem((blocks, LANES, taps * LANES), BF16),
        "at": vmem((blocks, taps * LANES, both), BF16),
        "mixed": vmem((both, half), BF16),
        "mixed_t": vmem((half, both), BF16),
        "slope": vmem((both, half), F32),
        "rks": vmem((both, key_width), F32),
        "rkr": vmem((both, key_width), F32),
        "posb": vmem((2, chips, 1, LANES), F32),
        "qall": vmem((2, *part), BF16),
        "pps": vmem(part, BF16),
        "ppr": vmem(part, BF16),
        "ws": vmem(part, BF16),
        "wr": vmem(part, BF16),
        "totb": vmem((chips, tot_rows, LANES), F32),
        "tfin": vmem((2, tot_rows, LANES), F32),
        "gq": vmem((2, anchors_dev, LANES), F32),
        "gm": vmem((both, half), BF16),
        "gp": vmem((both, half), BF16),
        "gr": vmem((both, key_width), BF16),
        "back": vmem((both, half), BF16),
        "l2a_s": vmem((inner, layers, rows_a, LANES), BF16),
        "l2a_r": vmem((inner, layers, rows_a, LANES), BF16),
        "l2b_s": vmem((layers, inner, rows_b, LANES), BF16),
        "l2b_r": vmem((layers, inner, rows_b, LANES), BF16),
        "l3a_s": vmem((layers, rows_a, LANES), BF16),
        "l3a_r": vmem((layers, rows_a, LANES), BF16),
        "l3b_s": vmem((inner, rows_b, LANES), BF16),
        "l3b_r": vmem((inner, rows_b, LANES), BF16),
        "load": dma((5,)),
    }
    singles = ("xp", "rk", "pos", "posp", "q", "qp", "pp", "tot", "totp", "wp", "gqp")
    for name in (*singles, "l2b", "l3a", "l3b", "out", "ap", "bp"):
        scratch[name + "_send"] = dma
        scratch[name + "_recv"] = dma
    for name in ("xh", "gh"):
        scratch[name + "_send"] = dma((2,))
        scratch[name + "_recv"] = dma((2,))
    for name, count in (("l2a", layers), ("af", layers), ("an", layers), ("bn", inner), ("bf", inner)):
        scratch[name + "_send"] = dma
        scratch[name + "_recv"] = dma((count,))
    names = ["x_hbm", "w_hbm", "proj_hbm", "anchor_hbm", "positive_hbm"]
    names += ["out", "ag_a", "ag_b", "loss", *scratch]
    sums = (
        jax.ShapeDtypeStruct((pixels, channels), BF16),
        jax.ShapeDtypeStruct((2, layers, inner, rows_a, LANES), BF16),
        jax.ShapeDtypeStruct((2, inner, layers, rows_b, LANES), BF16),
        jax.ShapeDtypeStruct((1, 1), F32),
    )
    parts = pl.pallas_call(
        functools.partial(
            kernel,
            names,
            devices,
            gradient_scale,
            (cols, group, pieces, piece, prow, inner, anchor_count),
        ),
        out_shape=sums,
        in_specs=[hbm] * 5,
        out_specs=(whole,) * 4,
        scratch_shapes=list(scratch.values()),
        compiler_params=pltpu.CompilerParams(
            collective_id=0, has_side_effects=True, vmem_limit_bytes=26000 * 1024
        ),
    )(
        in_hbm(features.reshape(pixels, channels)),
        in_hbm(conv_weight.reshape(taps, group, channels)),
        in_hbm(proj_weight),
        in_hbm(anchor_pixel.reshape(1, anchors_dev)),
        in_hbm(positive_pixel.reshape(1, anchors_dev)),
    )
    grad_features, grad_conv, grad_proj, loss = pl.pallas_call(
        functools.partial(finish, (2 * blocks, inner, pieces, piece, prow)),
        out_shape=(
            jax.ShapeDtypeStruct((pixels, channels), BF16),
            jax.ShapeDtypeStruct((taps * group, channels), F32),
            jax.ShapeDtypeStruct((channels, key_width), F32),
            jax.ShapeDtypeStruct((1, 1), F32),
        ),
        in_specs=[whole] * 4,
        out_specs=(hbm,) * 4,
        scratch_shapes=[
            vmem((taps * group, channels), F32),
            vmem((channels, key_width), F32),
            dma((3 + pieces,)),
        ],
        compiler_params=pltpu.CompilerParams(vmem_limit_bytes=16000 * 1024),
    )(*parts)
    grad_conv = grad_conv.reshape(conv_weight.shape)
    loss_value = loss.reshape(())
    if batches > 1:
        grad_conv, grad_proj, loss_value = lax.psum((grad_conv, grad_proj, loss_value), "batch")
    return (grad_features.reshape(features.shape), grad_conv, grad_proj, loss_value)


def solution(mesh):
    placed = (P("wide", None, "batch", None), P(), P(), P("wide", "batch"), P("wide", "batch"))
    return jax.shard_map(
        functools.partial(per_device, mesh.shape["wide"], mesh.shape["batch"]),
        mesh=mesh,
        in_specs=placed,
        out_specs=(P("wide", None, "batch", None), P(), P(), P()),
        check_vma=False,
    )
```

```python
import functools

import jax
import jax.numpy as jnp
from jax import lax
from jax.experimental import pallas as pl
from jax.experimental.pallas import tpu as pltpu
from jax.sharding import PartitionSpec as P

SOFTMAX_TEMPER = 0.1
EPSILON = 1e-06
LANES = 128
F32 = jnp.float32
BF16 = jnp.bfloat16
MESH = pl.DeviceIdType.MESH

NN = (((1,), (0,)), ((), ()))
NT = (((1,), (1,)), ((), ()))
TN = (((0,), (0,)), ((), ()))


def mm(a, b, dims, precision=None):
    return lax.dot_general(a, b, dims, preferred_element_type=F32, precision=precision)


def in_hbm(array):
    return pltpu.with_memory_space_constraint(array, pltpu.HBM)


def iota(shape, dim):
    return lax.broadcasted_iota(jnp.int32, shape, dim)


def store_shifted(dst, rows, start, values, cols, lane=slice(None)):
    wide = values.astype(F32)
    count = wide.shape[0]
    col = iota(wide.shape, 0) % cols
    dst[1, start : start + rows, lane] = values
    left = jnp.where(col == 0, 0.0, pltpu.roll(wide, 1, 0))
    dst[0, start : start + rows, lane] = left.astype(BF16)
    right = jnp.where(col == cols - 1, 0.0, pltpu.roll(wide, count - 1, 0))
    dst[2, start : start + rows, lane] = right.astype(BF16)


def kernel(names, devices, gradient_scale, geometry, *refs):
    r = dict(zip(names, refs, strict=True))
    cols, group, pieces, piece, prow, inner, anchor_count = geometry
    x_hbm, out_ref, ag_a, ag_b = r["x_hbm"], r["out"], r["ag_a"], r["ag_b"]
    pixels = x_hbm.shape[0]
    channels = x_hbm.shape[1]
    half = channels // 2
    blocks = half // LANES
    per_block = LANES // group
    anchors_dev = r["anchor"].shape[1]
    chips = devices // 2
    both = 2 * pixels
    anchors_core = chips * anchors_dev
    me = lax.axis_index("wide")
    core = lax.rem(me, 2)
    chip = me // 2
    other = 1 - core
    partner = chip * 2 + other
    place = lax.rem(chip, inner)
    layer = chip // inner
    layers = chips // inner
    span = pieces // inner
    conv_a = ag_a.shape[3] - prow
    barrier = pltpu.get_barrier_semaphore()

    def turn(count, start, body):
        def step(k, carry):
            body(lax.rem(start + k, count))
            return carry

        lax.fori_loop(1, count, step, 0)

    def rise(count, start, body):
        def step(k, carry):
            body(k + (k >= start).astype(jnp.int32))
            return carry

        lax.fori_loop(0, count - 1, step, 0)

    def other_chips(body):
        def layer_step(k, carry):
            z = jnp.where(layer < layers // 2, layers - 1 - k, k)

            def step(j, carry):
                t = z * inner + lax.rem(place + inner - 1 - j, inner)

                @pl.when(t != chip)
                def _():
                    body(t)

                return carry

            return lax.fori_loop(0, inner, step, carry, unroll=True)

        lax.fori_loop(0, layers, layer_step, 0)

    def near_id(target):
        return (layer * inner + target) * 2 + core

    def far_id(target):
        return (target * inner + place) * 2 + core

    def remote(src, dst, name, target, at=None, sent=None):
        recv = r[name + "_recv"]
        send = r[name + "_send"]
        return pltpu.make_async_remote_copy(
            src_ref=src,
            dst_ref=dst,
            send_sem=send if sent is None else send.at[sent],
            recv_sem=recv if at is None else recv.at[at],
            device_id={"wide": target},
            device_id_type=MESH,
        )

    def to_chips(source, landing, name):
        other_chips(lambda t: remote(source(t), landing, name, t * 2 + core).start())

    def from_chips(buf, name):
        view = buf.at[pl.ds(0, chips - 1)]
        remote(view, view, name, partner).wait_recv()

    def sent_chips(buf, name):
        view = buf.at[pl.ds(0, chips - 1)]
        remote(view, view, name, partner).wait_send()

    def signal_entry(target):
        pl.semaphore_signal(barrier, inc=1, device_id={"wide": target}, device_id_type=MESH)

    has_prev = chip > 0
    has_next = chip < chips - 1
    previous = lax.rem(chip + chips - 1, chips)
    following = lax.rem(chip + 1, chips)
    my_half = pl.ds(pl.multiple_of(core * half, LANES), half)
    your_half = pl.ds(pl.multiple_of(other * half, LANES), half)
    my_pixels = pl.ds(pl.multiple_of(core * pixels, 16), pixels)

    loads = [
        pltpu.make_async_copy(src, dst, r["load"].at[n])
        for n, (src, dst) in enumerate(
            (
                (r["positive_hbm"], r["positive"]),
                (r["w_hbm"].at[:, :, my_half], r["w"]),
                (x_hbm.at[:, my_half], r["xa"].at[my_pixels]),
                (r["proj_hbm"].at[my_half], r["proj"]),
                (r["anchor_hbm"], r["anchor"]),
            )
        )
    ]
    for copy in loads:
        copy.start()

    @pl.when(has_prev)
    def _():
        signal_entry(previous * 2 + other)

    @pl.when(has_next)
    def _():
        signal_entry(following * 2 + other)

    signal_entry(partner)

    def greet(k, carry):
        signal_entry(lax.rem(chip + k, chips) * 2 + core)
        signal_entry(lax.rem(chip + chips - k, chips) * 2 + core)
        return carry

    lax.fori_loop(1, chips // 2, greet, 0)
    signal_entry(lax.rem(chip + chips // 2, chips) * 2 + core)
    pl.semaphore_wait(barrier, chips + has_prev.astype(jnp.int32) + has_next.astype(jnp.int32))

    xh, gh, xa, gp = r["xh"], r["gh"], r["xa"], r["gp"]

    wide = half // 2

    def x_edge(source, slot, target):
        return [
            remote(
                x_hbm.at[pl.ds(source, cols), pl.ds(t * half + q * wide, wide)],
                xh.at[slot, :, pl.ds(q * wide, wide)],
                "xh",
                target * 2 + t,
                at=slot * 2 + q,
                sent=q * 2 + t,
            )
            for q in range(2)
            for t in range(2)
        ]

    up_edge = x_edge(0, 1, previous)
    down_edge = x_edge(pixels - cols, 0, following)
    sends_up = jnp.logical_and(core == 0, has_prev)
    sends_down = jnp.logical_and(core == 1, has_next)

    @pl.when(sends_up)
    def _():
        for copy in up_edge:
            copy.start()

    @pl.when(sends_down)
    def _():
        for copy in down_edge:
            copy.start()

    x_pair = remote(x_hbm.at[:, your_half], xa.at[my_pixels], "xp", partner)
    x_pair.start()

    def edges_wait(buf, name):
        @pl.when(has_prev)
        def _():
            remote(buf.at[0], buf.at[0], name, partner, at=0, sent=0).wait_recv()

        @pl.when(jnp.logical_not(has_prev))
        def _():
            buf[0] = jnp.zeros(buf.shape[1:], buf.dtype)

        @pl.when(has_next)
        def _():
            remote(buf.at[1], buf.at[1], name, partner, at=1, sent=1).wait_recv()

        @pl.when(jnp.logical_not(has_next))
        def _():
            buf[1] = jnp.zeros(buf.shape[1:], buf.dtype)

    for copy in loads:
        copy.wait()
    posb = r["posb"]
    posb[core, chip, :, :anchors_dev] = r["positive"][...].astype(F32)
    posb[core, chip, :, anchors_dev : 2 * anchors_dev] = r["anchor"][...].astype(F32)
    posb[core, chip, :, 2 * anchors_dev :] = jnp.zeros((1, LANES - 2 * anchors_dev), F32)
    to_chips(lambda t: posb.at[core, chip], posb.at[core, chip], "pos")

    w_ref, wn, wt, at = r["w"], r["wn"], r["wt"], r["at"]
    tap_count = w_ref.shape[0]
    diagonal = iota((LANES, LANES), 0) // group == iota((LANES, LANES), 1) // group

    def build(b, carry):
        lane = pl.ds(pl.multiple_of(b * LANES, LANES), LANES)
        for tap in range(tap_count):
            slab = w_ref[tap, :, lane].astype(F32)
            full = jnp.where(diagonal, jnp.concatenate([slab] * per_block, axis=0), 0.0)
            full = full.astype(BF16)
            wn[b, tap * LANES : (tap + 1) * LANES, :] = full
            wt[b, :, tap * LANES : (tap + 1) * LANES] = full
        return carry

    lax.fori_loop(0, blocks, build, 0)
    xs, gs = r["xs"], r["gs"]
    x_pair.wait_recv()
    store_shifted(xs, both, cols, xa[...], cols)

    def diagonal_col(row, first):
        lane = iota((anchors_dev, LANES), 1)
        hit = lane == iota((anchors_dev, LANES), 0) + first
        return jnp.sum(jnp.where(hit, row, 0.0), axis=1, keepdims=True)

    def pick_of(row, owner):
        column = diagonal_col(row, anchors_dev) + (owner * pixels).astype(F32)
        return jnp.where(iota((anchors_dev, both), 1).astype(F32) == column, 1.0, 0.0)

    pick_own = pick_of(posb[core, chip], core)

    @pl.when(jnp.logical_not(has_prev))
    def _():
        xh[0] = jnp.zeros(xh.shape[1:], xh.dtype)

    @pl.when(jnp.logical_not(has_next))
    def _():
        xh[1] = jnp.zeros(xh.shape[1:], xh.dtype)

    def x_edges_wait(q):
        lane = slice(q * wide, (q + 1) * wide)
        for slot, present in ((0, has_prev), (1, has_next)):
            view = xh.at[slot, :, pl.ds(q * wide, wide)]
            copy = remote(view, view, "xh", partner, at=slot * 2 + q, sent=0)

            @pl.when(present)
            def _():
                copy.wait_recv()

        store_shifted(xs, cols, 0, xh[0, :, lane], cols, lane)
        store_shifted(xs, cols, cols + both, xh[1, :, lane], cols, lane)

    def windows(buf, lane, flip):
        parts = []
        for row in range(3):
            for col in range(3):
                rr, cc = (2 - row, 2 - col) if flip else (row, col)
                parts.append(buf[cc, rr * cols : rr * cols + both, lane])
        return jnp.concatenate(parts, axis=1)

    mixed, mixed_t, slope, proj_ref = r["mixed"], r["mixed_t"], r["slope"], r["proj"]

    def forward(b, carry):
        lane = pl.ds(pl.multiple_of(b * LANES, LANES), LANES)
        pre = mm(windows(xs, lane, False), wn[b], NN)
        sig = 1.0 / (1.0 + jnp.exp(-pre))
        mixed[:, lane] = (xa[:, lane].astype(F32) + pre * sig).astype(BF16)
        slope[:, lane] = sig * (1.0 + pre * (1.0 - sig))
        return carry

    for q in range(2):
        x_edges_wait(q)
        lax.fori_loop(q * blocks // 2, (q + 1) * blocks // 2, forward, 0, unroll=True)

    rks, rkr = r["rks"], r["rkr"]
    rks[...] = mm(mixed[...], proj_ref[...], NN)
    rk_pair = remote(rks, rkr, "rk", partner)
    rk_pair.start()
    from_chips(posb.at[core], "pos")
    pos_pair = remote(posb.at[core], posb.at[core], "posp", partner)
    pos_pair.start()
    rk_pair.wait_recv()
    raw_key = rks[...] + rkr[...]
    norm_key = jnp.sqrt(jnp.sum(raw_key * raw_key, axis=1, keepdims=True) + EPSILON)
    unit_key = raw_key / norm_key
    keys = unit_key.astype(BF16)
    qall = r["qall"]
    qall[core, chip] = mm(pick_own.astype(BF16), keys, NN).astype(BF16)
    to_chips(lambda t: qall.at[core, chip], qall.at[core, chip], "q")

    def hits(parity):
        own_lane = iota((chips, anchors_dev, LANES), 1) == iota((chips, anchors_dev, LANES), 2)
        pos_all = jnp.sum(jnp.where(own_lane, posb[parity], 0.0), axis=2, keepdims=True)
        pos_local = pos_all - (chip * both).astype(F32)
        hit3 = jnp.where(
            iota((chips, anchors_dev, both), 2).astype(F32) == pos_local, 1.0, 0.0
        )
        return hit3.reshape(anchors_core, both).astype(BF16)

    hit_own = hits(core)
    part_pos = mm(hit_own, keys, NN)
    pps, ppr = r["pps"], r["ppr"]
    pps[...] = part_pos.reshape(chips, anchors_dev, LANES).astype(BF16)
    to_chips(lambda t: pps.at[t], ppr.at[chip], "pp")
    ppr[chip] = pps[chip]

    def flip_over(b, carry):
        start = pl.multiple_of(b * LANES, LANES)
        lane = pl.ds(start, LANES)
        at[b] = windows(xs, lane, False).T
        mixed_t[lane, :] = mixed[:, lane].T
        return carry

    lax.fori_loop(0, blocks, flip_over, 0, unroll=True)
    pos_pair.wait_recv()
    hit_other = hits(other)
    pick_other = pick_of(posb[other, chip], other)

    from_chips(qall.at[core], "q")
    q_pair = remote(qall.at[core], qall.at[core], "qp", partner)
    q_pair.start()
    queries = qall[core].reshape(anchors_core, LANES)
    exp_own = jnp.exp(mm(keys, queries, NT) / SOFTMAX_TEMPER)
    part_total = jnp.sum(exp_own, axis=0, keepdims=True)
    pos_sum = jnp.sum(
        jnp.sum(part_pos * queries.astype(F32), axis=1, keepdims=True), axis=0, keepdims=True
    )
    totb, tfin = r["totb"], r["tfin"]
    tot_rows = anchors_core // LANES
    for n in range(tot_rows):
        totb[chip, n : n + 1, :] = part_total[:, n * LANES : (n + 1) * LANES]
    totb[chip, tot_rows : tot_rows + 1, :] = jnp.broadcast_to(pos_sum, (1, LANES))
    to_chips(lambda t: totb.at[chip], totb.at[chip], "tot")
    part_weighted = mm(exp_own.astype(BF16), keys, TN)
    ws, wr = r["ws"], r["wr"]
    ws[...] = part_weighted.reshape(chips, anchors_dev, LANES).astype(BF16)
    to_chips(lambda t: ws.at[t], wr.at[chip], "wp")
    wr[chip] = ws[chip]

    q_pair.wait_recv()
    queries_other = qall[other].reshape(anchors_core, LANES)
    exp_other = jnp.exp(mm(keys, queries_other, NT) / SOFTMAX_TEMPER)
    pushed = mm(hit_own, queries, TN) + mm(hit_other, queries_other, TN)

    def whole_row(sums):
        return jnp.concatenate([sums[n : n + 1, :] for n in range(tot_rows)], axis=1)

    def loss_of(sums, row):
        return jnp.sum(jnp.log(row), axis=1, keepdims=True) - sums[
            tot_rows : tot_rows + 1, 0:1
        ] / SOFTMAX_TEMPER

    def pulled_by(exp_scores, row, asked):
        inverse = (1.0 / row).astype(BF16).astype(F32)
        return mm((exp_scores * inverse).astype(BF16), asked, NN)

    from_chips(totb, "tot")
    sums_own = jnp.sum(totb[...], axis=0)
    tfin[core] = sums_own
    tot_pair = remote(tfin.at[core], tfin.at[core], "totp", partner)
    tot_pair.start()
    row_own = whole_row(sums_own)
    mine = iota((anchors_dev, anchors_core), 1) == chip * anchors_dev + iota(
        (anchors_dev, anchors_core), 0
    )
    own_total = jnp.sum(jnp.where(mine, row_own, 0.0), axis=1, keepdims=True)
    gq = r["gq"]
    from_chips(ppr, "pp")
    from_chips(wr, "wp")
    weighted = jnp.sum(wr[...].astype(F32), axis=0)
    pos_key = jnp.sum(ppr[...].astype(F32), axis=0)
    gq[core] = (weighted / own_total - pos_key) * gradient_scale
    gq_pair = remote(gq.at[core], gq.at[core], "gqp", partner)
    gq_pair.start()
    pulled = pulled_by(exp_own, row_own, queries)
    tot_pair.wait_recv()
    sums_other = tfin[other]
    row_other = whole_row(sums_other)
    pulled = pulled + pulled_by(exp_other, row_other, queries_other)
    r["loss"][...] = (loss_of(sums_own, row_own) + loss_of(sums_other, row_other)) / anchor_count
    grad_key = gradient_scale * (pulled - pushed)
    gq_pair.wait_recv()
    grad_key = grad_key + mm(pick_own, gq[core], TN, lax.Precision.HIGHEST)
    grad_key = grad_key + mm(pick_other, gq[other], TN, lax.Precision.HIGHEST)
    along = jnp.sum(grad_key * unit_key, axis=1, keepdims=True)
    grad_raw = ((grad_key - unit_key * along) / norm_key).astype(BF16)
    grad_mixed = mm(grad_raw, proj_ref[...], NT).astype(BF16)
    gm, gr = r["gm"], r["gr"]
    gm[...] = grad_mixed
    gr[...] = grad_raw
    gp[...] = (grad_mixed.astype(F32) * slope[...]).astype(BF16)

    g_up = remote(
        gp.at[pl.ds(0, cols)], gh.at[1], "gh", previous * 2 + core, at=1, sent=0
    )
    g_down = remote(
        gp.at[pl.ds(both - cols, cols)], gh.at[0], "gh", following * 2 + core, at=0, sent=1
    )

    l2a_s, l2a_r, l2b_s, l2b_r = r["l2a_s"], r["l2a_r"], r["l2b_s"], r["l2b_r"]
    l3a_s, l3a_r, l3b_s, l3b_r = r["l3a_s"], r["l3a_r"], r["l3b_s"], r["l3b_r"]
    lane_group = iota((group, LANES), 1) // group
    first_block = layer // span + 1

    def weight_grad(k, carry):
        b = lax.rem(first_block + k, blocks)
        lane = pl.ds(pl.multiple_of(b * LANES, LANES), LANES)
        proj_part = mm(mixed_t[lane, :], gr[...], NN)
        full = mm(at[b], gp[:, lane], NN)
        taps = []
        for tap in range(tap_count):
            folded = jnp.zeros((group, LANES), F32)
            for g in range(per_block):
                first = tap * LANES + g * group
                folded = jnp.where(lane_group == g, full[first : first + group], folded)
            taps.append(folded)
        short = pieces * piece - tap_count * group
        if short:
            taps.append(jnp.zeros((short, LANES), F32))
        conv = jnp.concatenate(taps, axis=0)
        for j in range(pieces):
            z, p = b * span + j // inner, j % inner
            top = j * piece
            l2a_s[p, z, :prow, :] = proj_part[j * prow : (j + 1) * prow].astype(BF16)
            l2a_s[p, z, prow:, :] = conv[top : top + conv_a].astype(BF16)
            l2b_s[z, p] = conv[top + conv_a : top + piece].astype(BF16)
        for j in range(span):
            z = b * span + j
            turn(
                inner,
                place,
                lambda t: remote(
                    l2a_s.at[t, z], l2a_r.at[place, z], "l2a", near_id(t), at=z
                ).start(),
            )
            l2a_r[place, z] = l2a_s[place, z]

            @pl.when(z != layer)
            def _():
                remote(l2b_s.at[z], l2b_r.at[layer], "l2b", far_id(z)).start()

        return carry

    lax.fori_loop(0, blocks, weight_grad, 0)
    @pl.when(has_prev)
    def _():
        g_up.start()

    @pl.when(has_next)
    def _():
        g_down.start()

    l2b_r[layer] = l2b_s[layer]
    store_shifted(gs, both, cols, gp[...], cols)

    def near_summed(k, carry):
        z = lax.rem(first_block * span + k, layers)
        view = l2a_r.at[pl.ds(0, inner - 1), z]
        remote(view, view, "l2a", partner, at=z).wait_recv()
        l3a_s[z] = jnp.sum(l2a_r[:, z].astype(F32), axis=0).astype(BF16)

        @pl.when(z != layer)
        def _():
            remote(l3a_s.at[z], l3a_r.at[layer], "l3a", far_id(z)).start()

        return carry

    lax.fori_loop(0, layers, near_summed, 0)
    l3a_r[layer] = l3a_s[layer]
    view = l2b_r.at[pl.ds(0, layers - 1)]
    remote(view, view, "l2b", partner).wait_recv()
    for p in range(inner):
        l3b_s[p] = jnp.sum(l2b_r[:, p].astype(F32), axis=0).astype(BF16)
    turn(
        inner,
        place,
        lambda t: remote(l3b_s.at[t], l3b_r.at[place], "l3b", near_id(t)).start(),
    )
    l3b_r[place] = l3b_s[place]

    view = l3a_r.at[pl.ds(0, layers - 1)]
    remote(view, view, "l3a", partner).wait_recv()
    ag_a[core, layer, place] = jnp.sum(l3a_r[...].astype(F32), axis=0).astype(BF16)

    def a_copy(z, at, name, target):
        chunk = ag_a.at[core, z, place]
        return remote(chunk, chunk, name, target, at=at)

    def b_copy(p, at, name, target):
        chunk = ag_b.at[core, p, layer]
        return remote(chunk, chunk, name, target, at=at)

    rise(layers, layer, lambda t: a_copy(layer, layer, "af", far_id(t)).start())
    rise(inner, place, lambda t: a_copy(layer, layer, "an", near_id(t)).start())

    view = l3b_r.at[pl.ds(0, inner - 1)]
    remote(view, view, "l3b", partner).wait_recv()
    ag_b[core, place, layer] = jnp.sum(l3b_r[...].astype(F32), axis=0).astype(BF16)
    rise(inner, place, lambda t: b_copy(place, place, "bn", near_id(t)).start())
    rise(layers, layer, lambda t: b_copy(place, place, "bf", far_id(t)).start())

    edges_wait(gh, "gh")
    store_shifted(gs, cols, 0, gh[0], cols)
    store_shifted(gs, cols, cols + both, gh[1], cols)
    back_all = r["back"]

    def backward(b, carry):
        lane = pl.ds(pl.multiple_of(b * LANES, LANES), LANES)
        back = mm(windows(gs, lane, True), wt[b], NT).astype(BF16)
        back_all[:, lane] = (back.astype(F32) + gm[:, lane].astype(F32)).astype(BF16)
        return carry

    lax.fori_loop(0, blocks, backward, 0, unroll=True)
    out_pair = remote(
        back_all.at[pl.ds(pl.multiple_of(other * pixels, 16), pixels)],
        out_ref.at[:, my_half],
        "out",
        partner,
    )
    out_pair.start()
    out_ref[:, my_half] = back_all[my_pixels, :]

    def a_arrived(z):
        chunk = ag_a.at[core, z, place]
        remote(chunk, chunk, "af", partner, at=z).wait_recv()
        rise(inner, place, lambda t: a_copy(z, z, "an", near_id(t)).start())

    def b_arrived(p):
        chunk = ag_b.at[core, p, layer]
        remote(chunk, chunk, "bn", partner, at=p).wait_recv()
        rise(layers, layer, lambda t: b_copy(p, p, "bf", far_id(t)).start())

    rise(layers, layer, a_arrived)
    rise(inner, place, b_arrived)

    def a_whole(k, carry):
        z = lax.rem(layer + k, layers)
        view = ag_a.at[core, z, pl.ds(0, inner - 1)]
        remote(view, view, "an", partner, at=z).wait_recv()
        remote(ag_a.at[core, z], ag_a.at[core, z], "ap", partner).start()
        return carry

    def b_whole(k, carry):
        p = lax.rem(place + k, inner)
        view = ag_b.at[core, p, pl.ds(0, layers - 1)]
        remote(view, view, "bf", partner, at=p).wait_recv()
        remote(ag_b.at[core, p], ag_b.at[core, p], "bp", partner).start()
        return carry

    lax.fori_loop(0, layers, a_whole, 0)
    lax.fori_loop(0, inner, b_whole, 0)

    @pl.when(sends_up)
    def _():
        for copy in up_edge:
            copy.wait_send()

    @pl.when(sends_down)
    def _():
        for copy in down_edge:
            copy.wait_send()

    @pl.when(has_prev)
    def _():
        g_up.wait_send()

    @pl.when(has_next)
    def _():
        g_down.wait_send()

    for copy in (x_pair, rk_pair, pos_pair, q_pair, tot_pair, gq_pair):
        copy.wait_send()
    sent_chips(posb.at[core], "pos")
    sent_chips(qall.at[core], "q")
    sent_chips(pps, "pp")
    sent_chips(totb, "tot")
    sent_chips(ws, "wp")

    def sent(view, name, at=None):
        remote(view, view, name, partner, at=at).wait_send()

    sent(l2a_s.at[pl.ds(0, inner - 1)], "l2a", 0)
    sent(l2b_s.at[pl.ds(0, layers - 1)], "l2b")
    sent(l3a_s.at[pl.ds(0, layers - 1)], "l3a")
    sent(l3b_s.at[pl.ds(0, inner - 1)], "l3b")
    sent(ag_a.at[core, pl.ds(0, layers - 1), 0], "af", 0)
    sent(ag_a.at[core, :, pl.ds(0, inner - 1)], "an", 0)
    sent(ag_b.at[core, pl.ds(0, inner - 1), 0], "bn", 0)
    sent(ag_b.at[core, :, pl.ds(0, layers - 1)], "bf", 0)
    out_pair.wait()
    sent(ag_a.at[core], "ap")
    sent(ag_b.at[core], "bp")
    remote(ag_a.at[other], ag_a.at[other], "ap", partner).wait_recv()
    remote(ag_b.at[other], ag_b.at[other], "bp", partner).wait_recv()


def finish(geometry, gf_ref, ag_a, ag_b, loss_ref, gf_out, gw_out, gp_out, loss_out, gw, gp, sems):
    blocks, inner, pieces, piece, prow = geometry
    _, layers, _, rows_a, _ = ag_a.shape
    chips = layers * inner
    moves = [pltpu.make_async_copy(gf_ref, gf_out, sems.at[0])]
    moves[0].start()
    moves.append(pltpu.make_async_copy(loss_ref, loss_out, sems.at[2 + pieces]))
    moves[-1].start()
    height = gw_out.shape[0]
    conv_a = rows_a - prow
    for j in range(pieces):
        first = j * piece
        stop = min(height, first + piece)
        for b in range(blocks):
            side, i = b // (blocks // 2), b % (blocks // 2) * pieces + j
            lane = slice(b * LANES, (b + 1) * LANES)
            z, p = i // inner, i % inner
            first_p = (side * chips + i) * prow
            gp[first_p : first_p + prow, :] = ag_a[side, z, p, :prow, :].astype(F32)
            top = min(conv_a, max(stop - first, 0))
            if top > 0:
                gw[first : first + top, lane] = ag_a[side, z, p, prow : prow + top, :].astype(F32)
            low = stop - first - conv_a
            if low > 0:
                gw[first + conv_a : stop, lane] = ag_b[side, p, z, :low, :].astype(F32)
        if stop > first:
            rows = pl.ds(first, stop - first)
            moves.append(pltpu.make_async_copy(gw.at[rows], gw_out.at[rows], sems.at[2 + j]))
            moves[-1].start()
    moves.append(pltpu.make_async_copy(gp, gp_out, sems.at[1]))
    moves[-1].start()
    for move in moves:
        move.wait()


def per_device(devices, batches, features, conv_weight, proj_weight, anchor_pixel, positive_pixel):
    rows_dev, cols, images, channels = features.shape
    group = conv_weight.shape[2]
    key_width = proj_weight.shape[1]
    anchors_dev = anchor_pixel.shape[0]
    chips = devices // 2
    inner = min(4, chips)
    layers = chips // inner
    pixels = rows_dev * cols
    both = 2 * pixels
    half = channels // 2
    taps = conv_weight.shape[0] * conv_weight.shape[1]
    blocks = half // LANES
    pieces = chips // blocks
    piece = -(-(taps * group) // pieces)
    piece = -(-piece // 8) * 8
    prow = channels // devices
    rows_a = (prow + piece) * 4 // 5 // 16 * 16
    rows_b = prow + piece - rows_a
    anchors_core = anchors_dev * chips
    anchor_count = anchors_core * 2 * images * batches
    gradient_scale = 1.0 / (SOFTMAX_TEMPER * anchor_count)
    tot_rows = anchors_core // LANES + 1
    padded = both + 2 * cols
    dma = pltpu.SemaphoreType.DMA
    vmem = pltpu.VMEM
    whole = pl.BlockSpec(memory_space=pltpu.VMEM)
    hbm = pl.BlockSpec(memory_space=pltpu.HBM)
    part = (chips, anchors_dev, LANES)
    scratch = {
        "xa": vmem((both, half), BF16),
        "w": vmem((taps, group, half), BF16),
        "proj": vmem((half, key_width), BF16),
        "anchor": vmem((1, anchors_dev), jnp.int32),
        "positive": vmem((1, anchors_dev), jnp.int32),
        "xh": vmem((2, cols, half), BF16),
        "gh": vmem((2, cols, half), BF16),
        "xs": vmem((3, padded, half), BF16),
        "gs": vmem((3, padded, half), BF16),
        "wn": vmem((blocks, taps * LANES, LANES), BF16),
        "wt": vmem((blocks, LANES, taps * LANES), BF16),
        "at": vmem((blocks, taps * LANES, both), BF16),
        "mixed": vmem((both, half), BF16),
        "mixed_t": vmem((half, both), BF16),
        "slope": vmem((both, half), F32),
        "rks": vmem((both, key_width), F32),
        "rkr": vmem((both, key_width), F32),
        "posb": vmem((2, chips, 1, LANES), F32),
        "qall": vmem((2, *part), BF16),
        "pps": vmem(part, BF16),
        "ppr": vmem(part, BF16),
        "ws": vmem(part, BF16),
        "wr": vmem(part, BF16),
        "totb": vmem((chips, tot_rows, LANES), F32),
        "tfin": vmem((2, tot_rows, LANES), F32),
        "gq": vmem((2, anchors_dev, LANES), F32),
        "gm": vmem((both, half), BF16),
        "gp": vmem((both, half), BF16),
        "gr": vmem((both, key_width), BF16),
        "back": vmem((both, half), BF16),
        "l2a_s": vmem((inner, layers, rows_a, LANES), BF16),
        "l2a_r": vmem((inner, layers, rows_a, LANES), BF16),
        "l2b_s": vmem((layers, inner, rows_b, LANES), BF16),
        "l2b_r": vmem((layers, inner, rows_b, LANES), BF16),
        "l3a_s": vmem((layers, rows_a, LANES), BF16),
        "l3a_r": vmem((layers, rows_a, LANES), BF16),
        "l3b_s": vmem((inner, rows_b, LANES), BF16),
        "l3b_r": vmem((inner, rows_b, LANES), BF16),
        "load": dma((5,)),
    }
    singles = ("xp", "rk", "pos", "posp", "q", "qp", "pp", "tot", "totp", "wp", "gqp")
    for name in (*singles, "l2b", "l3a", "l3b", "out", "ap", "bp"):
        scratch[name + "_send"] = dma
        scratch[name + "_recv"] = dma
    for name, count in (("xh", 4), ("gh", 2)):
        scratch[name + "_send"] = dma((count,))
        scratch[name + "_recv"] = dma((count,))
    for name, count in (("l2a", layers), ("af", layers), ("an", layers), ("bn", inner), ("bf", inner)):
        scratch[name + "_send"] = dma
        scratch[name + "_recv"] = dma((count,))
    names = ["x_hbm", "w_hbm", "proj_hbm", "anchor_hbm", "positive_hbm"]
    names += ["out", "ag_a", "ag_b", "loss", *scratch]
    sums = (
        jax.ShapeDtypeStruct((pixels, channels), BF16),
        jax.ShapeDtypeStruct((2, layers, inner, rows_a, LANES), BF16),
        jax.ShapeDtypeStruct((2, inner, layers, rows_b, LANES), BF16),
        jax.ShapeDtypeStruct((1, 1), F32),
    )
    parts = pl.pallas_call(
        functools.partial(
            kernel,
            names,
            devices,
            gradient_scale,
            (cols, group, pieces, piece, prow, inner, anchor_count),
        ),
        out_shape=sums,
        in_specs=[hbm] * 5,
        out_specs=(whole,) * 4,
        scratch_shapes=list(scratch.values()),
        compiler_params=pltpu.CompilerParams(
            collective_id=0, has_side_effects=True, vmem_limit_bytes=26000 * 1024
        ),
    )(
        in_hbm(features.reshape(pixels, channels)),
        in_hbm(conv_weight.reshape(taps, group, channels)),
        in_hbm(proj_weight),
        in_hbm(anchor_pixel.reshape(1, anchors_dev)),
        in_hbm(positive_pixel.reshape(1, anchors_dev)),
    )
    grad_features, grad_conv, grad_proj, loss = pl.pallas_call(
        functools.partial(finish, (2 * blocks, inner, pieces, piece, prow)),
        out_shape=(
            jax.ShapeDtypeStruct((pixels, channels), BF16),
            jax.ShapeDtypeStruct((taps * group, channels), F32),
            jax.ShapeDtypeStruct((channels, key_width), F32),
            jax.ShapeDtypeStruct((1, 1), F32),
        ),
        in_specs=[whole] * 4,
        out_specs=(hbm,) * 4,
        scratch_shapes=[
            vmem((taps * group, channels), F32),
            vmem((channels, key_width), F32),
            dma((3 + pieces,)),
        ],
        compiler_params=pltpu.CompilerParams(vmem_limit_bytes=16000 * 1024),
    )(*parts)
    grad_conv = grad_conv.reshape(conv_weight.shape)
    loss_value = loss.reshape(())
    if batches > 1:
        grad_conv, grad_proj, loss_value = lax.psum((grad_conv, grad_proj, loss_value), "batch")
    return (grad_features.reshape(features.shape), grad_conv, grad_proj, loss_value)


def solution(mesh):
    placed = (P("wide", None, "batch", None), P(), P(), P("wide", "batch"), P("wide", "batch"))
    return jax.shard_map(
        functools.partial(per_device, mesh.shape["wide"], mesh.shape["batch"]),
        mesh=mesh,
        in_specs=placed,
        out_specs=(P("wide", None, "batch", None), P(), P(), P()),
        check_vma=False,
    )
```

```python
import functools

import jax
import jax.numpy as jnp
from jax import lax
from jax.experimental import pallas as pl
from jax.experimental.pallas import tpu as pltpu
from jax.sharding import PartitionSpec as P

SOFTMAX_TEMPER = 0.1
EPSILON = 1e-06
LANES = 128
F32 = jnp.float32
BF16 = jnp.bfloat16
MESH = pl.DeviceIdType.MESH

NN = (((1,), (0,)), ((), ()))
NT = (((1,), (1,)), ((), ()))
TN = (((0,), (0,)), ((), ()))


def mm(a, b, dims, precision=None):
    return lax.dot_general(a, b, dims, preferred_element_type=F32, precision=precision)


def in_hbm(array):
    return pltpu.with_memory_space_constraint(array, pltpu.HBM)


def iota(shape, dim):
    return lax.broadcasted_iota(jnp.int32, shape, dim)


def store_shifted(dst, rows, start, values, cols, lane=slice(None)):
    wide = values.astype(F32)
    count = wide.shape[0]
    col = iota(wide.shape, 0) % cols
    dst[1, start : start + rows, lane] = values
    left = jnp.where(col == 0, 0.0, pltpu.roll(wide, 1, 0))
    dst[0, start : start + rows, lane] = left.astype(BF16)
    right = jnp.where(col == cols - 1, 0.0, pltpu.roll(wide, count - 1, 0))
    dst[2, start : start + rows, lane] = right.astype(BF16)


def kernel(names, devices, gradient_scale, geometry, *refs):
    r = dict(zip(names, refs, strict=True))
    cols, group, pieces, piece, prow, inner, anchor_count = geometry
    x_hbm, out_ref, ag_a, ag_b = r["x_hbm"], r["out"], r["ag_a"], r["ag_b"]
    pixels = x_hbm.shape[0]
    channels = x_hbm.shape[1]
    half = channels // 2
    blocks = half // LANES
    per_block = LANES // group
    anchors_dev = r["anchor"].shape[1]
    chips = devices // 2
    both = 2 * pixels
    anchors_core = chips * anchors_dev
    me = lax.axis_index("wide")
    core = lax.rem(me, 2)
    chip = me // 2
    other = 1 - core
    partner = chip * 2 + other
    place = lax.rem(chip, inner)
    layer = chip // inner
    layers = chips // inner
    span = pieces // inner
    conv_a = ag_a.shape[3] - prow
    barrier = pltpu.get_barrier_semaphore()

    def turn(count, start, body):
        def step(k, carry):
            body(lax.rem(start + k, count))
            return carry

        lax.fori_loop(1, count, step, 0)

    def away(k, count, own):
        down = count - 1 - k
        down = down - (down <= own).astype(jnp.int32)
        up = k + (k >= own).astype(jnp.int32)
        return jnp.where(2 * own < count, down, up)

    def farthest(count, own, body):
        def step(k, carry):
            body(away(k, count, own))
            return carry

        lax.fori_loop(0, count - 1, step, 0)

    def nearest(count, own, body):
        farthest_last = count - 2

        def step(k, carry):
            body(away(farthest_last - k, count, own))
            return carry

        lax.fori_loop(0, count - 1, step, 0)

    def across(body):
        body(inner - 1 - place)
        body(place + 1 - 2 * lax.rem(place, 2))
        body(place + 2 - 4 * (place // 2))

    def rise(count, start, body):
        def step(k, carry):
            body(k + (k >= start).astype(jnp.int32))
            return carry

        lax.fori_loop(0, count - 1, step, 0)

    def other_chips(body):
        def layer_step(k, carry):
            z = jnp.where(layer < layers // 2, layers - 1 - k, k)

            def step(j, carry):
                t = z * inner + lax.rem(place + inner - 1 - j, inner)

                @pl.when(t != chip)
                def _():
                    body(t)

                return carry

            return lax.fori_loop(0, inner, step, carry, unroll=True)

        lax.fori_loop(0, layers, layer_step, 0)

    def near_id(target):
        return (layer * inner + target) * 2 + core

    def far_id(target):
        return (target * inner + place) * 2 + core

    def remote(src, dst, name, target, at=None, sent=None):
        recv = r[name + "_recv"]
        send = r[name + "_send"]
        return pltpu.make_async_remote_copy(
            src_ref=src,
            dst_ref=dst,
            send_sem=send if sent is None else send.at[sent],
            recv_sem=recv if at is None else recv.at[at],
            device_id={"wide": target},
            device_id_type=MESH,
        )

    def to_chips(source, landing, name):
        other_chips(lambda t: remote(source(t), landing, name, t * 2 + core).start())

    def from_chips(buf, name):
        view = buf.at[pl.ds(0, chips - 1)]
        remote(view, view, name, partner).wait_recv()

    def sent_chips(buf, name):
        view = buf.at[pl.ds(0, chips - 1)]
        remote(view, view, name, partner).wait_send()

    def signal_entry(target):
        pl.semaphore_signal(barrier, inc=1, device_id={"wide": target}, device_id_type=MESH)

    has_prev = chip > 0
    has_next = chip < chips - 1
    previous = lax.rem(chip + chips - 1, chips)
    following = lax.rem(chip + 1, chips)
    my_half = pl.ds(pl.multiple_of(core * half, LANES), half)
    your_half = pl.ds(pl.multiple_of(other * half, LANES), half)
    my_pixels = pl.ds(pl.multiple_of(core * pixels, 16), pixels)

    loads = [
        pltpu.make_async_copy(src, dst, r["load"].at[n])
        for n, (src, dst) in enumerate(
            (
                (x_hbm, r["xf"]),
                (r["positive_hbm"], r["positive"]),
                (r["w_hbm"].at[:, :, my_half], r["w"]),
                (x_hbm.at[:, my_half], r["xa"].at[my_pixels]),
                (r["proj_hbm"].at[my_half], r["proj"]),
                (r["anchor_hbm"], r["anchor"]),
            )
        )
    ]
    for copy in loads:
        copy.start()

    @pl.when(has_prev)
    def _():
        signal_entry(previous * 2 + other)

    @pl.when(has_next)
    def _():
        signal_entry(following * 2 + other)

    signal_entry(partner)

    def greet(k, carry):
        signal_entry(lax.rem(chip + k, chips) * 2 + core)
        signal_entry(lax.rem(chip + chips - k, chips) * 2 + core)
        return carry

    lax.fori_loop(1, chips // 2, greet, 0)
    signal_entry(lax.rem(chip + chips // 2, chips) * 2 + core)
    loads[0].wait()
    xf = r["xf"]
    pl.semaphore_wait(barrier, chips + has_prev.astype(jnp.int32) + has_next.astype(jnp.int32))

    xh, xa, gp = r["xh"], r["xa"], r["gp"]

    wide = half // 2

    def x_edge(source, slot, target):
        return [
            remote(
                xf.at[pl.ds(source, cols), pl.ds(t * half + q * wide, wide)],
                xh.at[slot, :, pl.ds(q * wide, wide)],
                "xh",
                target * 2 + t,
                at=slot * 2 + q,
                sent=q * 2 + t,
            )
            for q in range(2)
            for t in range(2)
        ]

    up_edge = x_edge(0, 1, previous)
    down_edge = x_edge(pixels - cols, 0, following)
    sends_up = jnp.logical_and(core == 0, has_prev)
    sends_down = jnp.logical_and(core == 1, has_next)

    @pl.when(sends_up)
    def _():
        for copy in up_edge:
            copy.start()

    @pl.when(sends_down)
    def _():
        for copy in down_edge:
            copy.start()

    x_pair = remote(xf.at[:, your_half], xa.at[my_pixels], "xp", partner)
    x_pair.start()

    def edges(src, buf, name):
        up = remote(src.at[0], buf.at[1], name, previous * 2 + core, at=1, sent=0)
        down = remote(src.at[1], buf.at[0], name, following * 2 + core, at=0, sent=1)
        return up, down

    def edges_start(copies):
        for copy, present in zip(copies, (has_prev, has_next), strict=True):
            pl.when(present)(copy.start)

    def edges_sent(copies):
        for copy, present in zip(copies, (has_prev, has_next), strict=True):
            pl.when(present)(copy.wait_send)

    def edges_wait(copies, buf):
        up, down = copies

        @pl.when(has_prev)
        def _():
            down.wait_recv()

        @pl.when(jnp.logical_not(has_prev))
        def _():
            buf[0] = jnp.zeros(buf.shape[1:], buf.dtype)

        @pl.when(has_next)
        def _():
            up.wait_recv()

        @pl.when(jnp.logical_not(has_next))
        def _():
            buf[1] = jnp.zeros(buf.shape[1:], buf.dtype)

    for copy in loads[1:]:
        copy.wait()
    posb = r["posb"]
    posb[core, chip, :, :anchors_dev] = r["positive"][...].astype(F32)
    posb[core, chip, :, anchors_dev : 2 * anchors_dev] = r["anchor"][...].astype(F32)
    posb[core, chip, :, 2 * anchors_dev :] = jnp.zeros((1, LANES - 2 * anchors_dev), F32)
    to_chips(lambda t: posb.at[core, chip], posb.at[core, chip], "pos")

    w_ref, wn, wt, at = r["w"], r["wn"], r["wt"], r["at"]
    tap_count = w_ref.shape[0]
    diagonal = iota((LANES, LANES), 0) // group == iota((LANES, LANES), 1) // group

    def build(b, carry):
        lane = pl.ds(pl.multiple_of(b * LANES, LANES), LANES)
        for tap in range(tap_count):
            slab = w_ref[tap, :, lane].astype(F32)
            full = jnp.where(diagonal, jnp.concatenate([slab] * per_block, axis=0), 0.0)
            full = full.astype(BF16)
            wn[b, tap * LANES : (tap + 1) * LANES, :] = full
            wt[b, :, tap * LANES : (tap + 1) * LANES] = full
        return carry

    lax.fori_loop(0, blocks, build, 0)
    xs, gs = r["xs"], r["gs"]
    x_pair.wait_recv()
    store_shifted(xs, both, cols, xa[...], cols)

    def diagonal_col(row, first):
        lane = iota((anchors_dev, LANES), 1)
        hit = lane == iota((anchors_dev, LANES), 0) + first
        return jnp.sum(jnp.where(hit, row, 0.0), axis=1, keepdims=True)

    def pick_of(row, owner):
        column = diagonal_col(row, anchors_dev) + (owner * pixels).astype(F32)
        return jnp.where(iota((anchors_dev, both), 1).astype(F32) == column, 1.0, 0.0)

    pick_own = pick_of(posb[core, chip], core)

    @pl.when(jnp.logical_not(has_prev))
    def _():
        xh[0] = jnp.zeros(xh.shape[1:], xh.dtype)

    @pl.when(jnp.logical_not(has_next))
    def _():
        xh[1] = jnp.zeros(xh.shape[1:], xh.dtype)

    def x_edges_wait(q):
        lane = slice(q * wide, (q + 1) * wide)
        for slot, present in ((0, has_prev), (1, has_next)):
            view = xh.at[slot, :, pl.ds(q * wide, wide)]
            copy = remote(view, view, "xh", partner, at=slot * 2 + q, sent=0)

            @pl.when(present)
            def _():
                copy.wait_recv()

        store_shifted(xs, cols, 0, xh[0, :, lane], cols, lane)
        store_shifted(xs, cols, cols + both, xh[1, :, lane], cols, lane)

    def windows(buf, lane, flip):
        parts = []
        for row in range(3):
            for col in range(3):
                rr, cc = (2 - row, 2 - col) if flip else (row, col)
                parts.append(buf[cc, rr * cols : rr * cols + both, lane])
        return jnp.concatenate(parts, axis=1)

    mixed, mixed_t, slope, proj_ref = r["mixed"], r["mixed_t"], r["slope"], r["proj"]

    def forward(b, carry):
        lane = pl.ds(pl.multiple_of(b * LANES, LANES), LANES)
        pre = mm(windows(xs, lane, False), wn[b], NN)
        sig = 1.0 / (1.0 + jnp.exp(-pre))
        mixed[:, lane] = (xa[:, lane].astype(F32) + pre * sig).astype(BF16)
        slope[:, lane] = sig * (1.0 + pre * (1.0 - sig))
        return carry

    for q in range(2):
        x_edges_wait(q)
        lax.fori_loop(q * blocks // 2, (q + 1) * blocks // 2, forward, 0, unroll=True)

    rks, rkr = r["rks"], r["rkr"]
    rks[...] = mm(mixed[...], proj_ref[...], NN)
    rk_pair = remote(rks, rkr, "rk", partner)
    rk_pair.start()
    from_chips(posb.at[core], "pos")
    pos_pair = remote(posb.at[core], posb.at[core], "posp", partner)
    pos_pair.start()
    rk_pair.wait_recv()
    raw_key = rks[...] + rkr[...]
    norm_key = jnp.sqrt(jnp.sum(raw_key * raw_key, axis=1, keepdims=True) + EPSILON)
    unit_key = raw_key / norm_key
    keys = unit_key.astype(BF16)
    qall = r["qall"]
    qall[core, chip] = mm(pick_own.astype(BF16), keys, NN).astype(BF16)
    to_chips(lambda t: qall.at[core, chip], qall.at[core, chip], "q")

    slope_edge, slope_far = r["slope_edge"], r["slope_far"]
    slope_edge[0] = slope[:cols, :].astype(BF16)
    slope_edge[1] = slope[both - cols :, :].astype(BF16)
    slope_edges = edges(slope_edge, slope_far, "sh")
    edges_start(slope_edges)

    def hits(parity):
        own_lane = iota((chips, anchors_dev, LANES), 1) == iota((chips, anchors_dev, LANES), 2)
        pos_all = jnp.sum(jnp.where(own_lane, posb[parity], 0.0), axis=2, keepdims=True)
        pos_local = pos_all - (chip * both).astype(F32)
        hit3 = jnp.where(
            iota((chips, anchors_dev, both), 2).astype(F32) == pos_local, 1.0, 0.0
        )
        return hit3.reshape(anchors_core, both).astype(BF16)

    hit_own = hits(core)
    part_pos = mm(hit_own, keys, NN)
    pps, ppr = r["pps"], r["ppr"]
    pps[...] = part_pos.reshape(chips, anchors_dev, LANES).astype(BF16)
    ppr[chip] = pps[chip]

    def flip_over(b, carry):
        start = pl.multiple_of(b * LANES, LANES)
        lane = pl.ds(start, LANES)
        at[b] = windows(xs, lane, False).T
        mixed_t[lane, :] = mixed[:, lane].T
        return carry

    lax.fori_loop(0, blocks, flip_over, 0, unroll=True)
    to_chips(lambda t: pps.at[t], ppr.at[chip], "pp")
    pos_pair.wait_recv()
    hit_other = hits(other)
    pick_other = pick_of(posb[other, chip], other)

    from_chips(qall.at[core], "q")
    q_pair = remote(qall.at[core], qall.at[core], "qp", partner)
    q_pair.start()
    queries = qall[core].reshape(anchors_core, LANES)
    exp_own = jnp.exp(mm(keys, queries, NT) / SOFTMAX_TEMPER)
    part_total = jnp.sum(exp_own, axis=0, keepdims=True)
    pos_sum = jnp.sum(
        jnp.sum(part_pos * queries.astype(F32), axis=1, keepdims=True), axis=0, keepdims=True
    )
    totb, tfin = r["totb"], r["tfin"]
    tot_rows = anchors_core // LANES
    for n in range(tot_rows):
        totb[chip, n : n + 1, :] = part_total[:, n * LANES : (n + 1) * LANES]
    totb[chip, tot_rows : tot_rows + 1, :] = jnp.broadcast_to(pos_sum, (1, LANES))
    to_chips(lambda t: totb.at[chip], totb.at[chip], "tot")
    part_weighted = mm(exp_own.astype(BF16), keys, TN)
    ws, wr = r["ws"], r["wr"]
    ws[...] = part_weighted.reshape(chips, anchors_dev, LANES).astype(BF16)
    to_chips(lambda t: ws.at[t], wr.at[chip], "wp")
    wr[chip] = ws[chip]

    q_pair.wait_recv()
    queries_other = qall[other].reshape(anchors_core, LANES)
    exp_other = jnp.exp(mm(keys, queries_other, NT) / SOFTMAX_TEMPER)
    pushed = mm(hit_own, queries, TN) + mm(hit_other, queries_other, TN)

    def whole_row(sums):
        return jnp.concatenate([sums[n : n + 1, :] for n in range(tot_rows)], axis=1)

    def loss_of(sums, row):
        return jnp.sum(jnp.log(row), axis=1, keepdims=True) - sums[
            tot_rows : tot_rows + 1, 0:1
        ] / SOFTMAX_TEMPER

    def pulled_by(exp_scores, row, asked):
        inverse = (1.0 / row).astype(BF16).astype(F32)
        return mm((exp_scores * inverse).astype(BF16), asked, NN)

    from_chips(totb, "tot")
    sums_own = jnp.sum(totb[...], axis=0)
    tfin[core] = sums_own
    tot_pair = remote(tfin.at[core], tfin.at[core], "totp", partner)
    tot_pair.start()
    row_own = whole_row(sums_own)
    mine = iota((anchors_dev, anchors_core), 1) == chip * anchors_dev + iota(
        (anchors_dev, anchors_core), 0
    )
    own_total = jnp.sum(jnp.where(mine, row_own, 0.0), axis=1, keepdims=True)
    gq = r["gq"]
    from_chips(ppr, "pp")
    from_chips(wr, "wp")
    weighted = jnp.sum(wr[...].astype(F32), axis=0)
    pos_key = jnp.sum(ppr[...].astype(F32), axis=0)
    gq[core] = (weighted / own_total - pos_key) * gradient_scale
    gq_pair = remote(gq.at[core], gq.at[core], "gqp", partner)
    gq_pair.start()
    pulled = pulled_by(exp_own, row_own, queries)
    tot_pair.wait_recv()
    sums_other = tfin[other]
    row_other = whole_row(sums_other)
    pulled = pulled + pulled_by(exp_other, row_other, queries_other)
    r["loss"][...] = (loss_of(sums_own, row_own) + loss_of(sums_other, row_other)) / anchor_count
    grad_key = gradient_scale * (pulled - pushed)
    gq_pair.wait_recv()
    grad_key = grad_key + mm(pick_own, gq[core], TN, lax.Precision.HIGHEST)
    grad_key = grad_key + mm(pick_other, gq[other], TN, lax.Precision.HIGHEST)
    along = jnp.sum(grad_key * unit_key, axis=1, keepdims=True)
    grad_raw = ((grad_key - unit_key * along) / norm_key).astype(BF16)
    grad_mixed = mm(grad_raw, proj_ref[...], NT).astype(BF16)
    gm, gr = r["gm"], r["gr"]
    gm[...] = grad_mixed
    gr[...] = grad_raw
    gp[...] = (grad_mixed.astype(F32) * slope[...]).astype(BF16)

    raw_edge, raw_far = r["raw_edge"], r["raw_far"]
    raw_edge[0] = grad_raw[:cols]
    raw_edge[1] = grad_raw[both - cols :]
    raw_edges = edges(raw_edge, raw_far, "gh")
    l2a_s, l2a_r, l2b_s, l2b_r = r["l2a_s"], r["l2a_r"], r["l2b_s"], r["l2b_r"]
    l3a_s, l3a_r, l3b_s, l3b_r = r["l3a_s"], r["l3a_r"], r["l3b_s"], r["l3b_r"]
    lane_group = iota((group, LANES), 1) // group
    own_block = layer // span

    def block_at(k):
        return jnp.where(k == blocks - 1, own_block, away(k, blocks, own_block))


    def weight_grad(k, carry):
        b = block_at(k)
        lane = pl.ds(pl.multiple_of(b * LANES, LANES), LANES)
        proj_part = mm(mixed_t[lane, :], gr[...], NN)
        full = mm(at[b], gp[:, lane], NN)
        taps = []
        for tap in range(tap_count):
            folded = jnp.zeros((group, LANES), F32)
            for g in range(per_block):
                first = tap * LANES + g * group
                folded = jnp.where(lane_group == g, full[first : first + group], folded)
            taps.append(folded)
        short = pieces * piece - tap_count * group
        if short:
            taps.append(jnp.zeros((short, LANES), F32))
        conv = jnp.concatenate(taps, axis=0)
        for j in range(pieces):
            z, p = b * span + j // inner, j % inner
            top = j * piece
            l2a_s[p, z, :prow, :] = proj_part[j * prow : (j + 1) * prow].astype(BF16)
            l2a_s[p, z, prow:, :] = conv[top : top + conv_a].astype(BF16)
            l2b_s[z, p] = conv[top + conv_a : top + piece].astype(BF16)
        for j in range(span):
            z = b * span + j
            across(
                lambda t: remote(
                    l2a_s.at[t, z], l2a_r.at[place, z], "l2a", near_id(t), at=z
                ).start(),
            )
            l2a_r[place, z] = l2a_s[place, z]

            @pl.when(z != layer)
            def _():
                remote(l2b_s.at[z], l2b_r.at[layer], "l2b", far_id(z)).start()

        return carry

    lax.fori_loop(0, blocks, weight_grad, 0)
    edges_start(raw_edges)
    l2b_r[layer] = l2b_s[layer]
    store_shifted(gs, both, cols, gp[...], cols)

    def near_summed(k, carry):
        z = block_at(k // span) * span + lax.rem(k, span)
        view = l2a_r.at[pl.ds(0, inner - 1), z]
        remote(view, view, "l2a", partner, at=z).wait_recv()
        l3a_s[z] = jnp.sum(l2a_r[:, z].astype(F32), axis=0).astype(BF16)

        @pl.when(z != layer)
        def _():
            remote(l3a_s.at[z], l3a_r.at[layer], "l3a", far_id(z)).start()

        return carry

    lax.fori_loop(0, layers, near_summed, 0)
    l3a_r[layer] = l3a_s[layer]
    view = l2b_r.at[pl.ds(0, layers - 1)]
    remote(view, view, "l2b", partner).wait_recv()
    for p in range(inner):
        l3b_s[p] = jnp.sum(l2b_r[:, p].astype(F32), axis=0).astype(BF16)
    turn(
        inner,
        place,
        lambda t: remote(l3b_s.at[t], l3b_r.at[place], "l3b", near_id(t)).start(),
    )
    l3b_r[place] = l3b_s[place]

    view = l3a_r.at[pl.ds(0, layers - 1)]
    remote(view, view, "l3a", partner).wait_recv()
    ag_a[core, layer, place] = jnp.sum(l3a_r[...].astype(F32), axis=0).astype(BF16)

    def a_copy(z, at, name, target):
        chunk = ag_a.at[core, z, place]
        return remote(chunk, chunk, name, target, at=at)

    def b_copy(p, at, name, target):
        chunk = ag_b.at[core, p, layer]
        return remote(chunk, chunk, name, target, at=at)

    farthest(layers, layer, lambda t: a_copy(layer, layer, "af", far_id(t)).start())
    rise(inner, place, lambda t: a_copy(layer, layer, "an", near_id(t)).start())

    view = l3b_r.at[pl.ds(0, inner - 1)]
    remote(view, view, "l3b", partner).wait_recv()
    ag_b[core, place, layer] = jnp.sum(l3b_r[...].astype(F32), axis=0).astype(BF16)
    rise(inner, place, lambda t: b_copy(place, place, "bn", near_id(t)).start())
    farthest(layers, layer, lambda t: b_copy(place, place, "bf", far_id(t)).start())

    edges_wait(slope_edges, slope_far)
    edges_wait(raw_edges, raw_far)
    for slot in range(2):
        edge = mm(raw_far[slot], proj_ref[...], NT).astype(BF16).astype(F32)
        edge = (edge * slope_far[slot].astype(F32)).astype(BF16)
        store_shifted(gs, cols, slot * (cols + both), edge, cols)
    back_all = r["back"]

    def backward(b, carry):
        lane = pl.ds(pl.multiple_of(b * LANES, LANES), LANES)
        back = mm(windows(gs, lane, True), wt[b], NT).astype(BF16)
        back_all[:, lane] = (back.astype(F32) + gm[:, lane].astype(F32)).astype(BF16)
        return carry

    lax.fori_loop(0, blocks, backward, 0, unroll=True)
    out_pair = remote(
        back_all.at[pl.ds(pl.multiple_of(other * pixels, 16), pixels)],
        out_ref.at[:, my_half],
        "out",
        partner,
    )
    out_pair.start()
    out_ref[:, my_half] = back_all[my_pixels, :]

    def a_arrived(z):
        chunk = ag_a.at[core, z, place]
        remote(chunk, chunk, "af", partner, at=z).wait_recv()
        rise(inner, place, lambda t: a_copy(z, z, "an", near_id(t)).start())

    def b_arrived(p):
        chunk = ag_b.at[core, p, layer]
        remote(chunk, chunk, "bn", partner, at=p).wait_recv()
        farthest(layers, layer, lambda t: b_copy(p, p, "bf", far_id(t)).start())

    nearest(layers, layer, a_arrived)
    rise(inner, place, b_arrived)

    def a_whole(k, carry):
        z = jnp.where(k == 0, layer, away(layers - 1 - k, layers, layer))
        view = ag_a.at[core, z, pl.ds(0, inner - 1)]
        remote(view, view, "an", partner, at=z).wait_recv()
        remote(ag_a.at[core, z], ag_a.at[core, z], "ap", partner).start()
        return carry

    def b_whole(k, carry):
        p = lax.rem(place + k, inner)
        view = ag_b.at[core, p, pl.ds(0, layers - 1)]
        remote(view, view, "bf", partner, at=p).wait_recv()
        remote(ag_b.at[core, p], ag_b.at[core, p], "bp", partner).start()
        return carry

    lax.fori_loop(0, layers, a_whole, 0)
    lax.fori_loop(0, inner, b_whole, 0)

    @pl.when(sends_up)
    def _():
        for copy in up_edge:
            copy.wait_send()

    @pl.when(sends_down)
    def _():
        for copy in down_edge:
            copy.wait_send()

    edges_sent(slope_edges)
    edges_sent(raw_edges)

    for copy in (x_pair, rk_pair, pos_pair, q_pair, tot_pair, gq_pair):
        copy.wait_send()
    sent_chips(posb.at[core], "pos")
    sent_chips(qall.at[core], "q")
    sent_chips(pps, "pp")
    sent_chips(totb, "tot")
    sent_chips(ws, "wp")

    def sent(view, name, at=None):
        remote(view, view, name, partner, at=at).wait_send()

    sent(l2a_s.at[pl.ds(0, inner - 1)], "l2a", 0)
    sent(l2b_s.at[pl.ds(0, layers - 1)], "l2b")
    sent(l3a_s.at[pl.ds(0, layers - 1)], "l3a")
    sent(l3b_s.at[pl.ds(0, inner - 1)], "l3b")
    sent(ag_a.at[core, pl.ds(0, layers - 1), 0], "af", 0)
    sent(ag_a.at[core, :, pl.ds(0, inner - 1)], "an", 0)
    sent(ag_b.at[core, pl.ds(0, inner - 1), 0], "bn", 0)
    sent(ag_b.at[core, :, pl.ds(0, layers - 1)], "bf", 0)
    out_pair.wait()
    sent(ag_a.at[core], "ap")
    sent(ag_b.at[core], "bp")
    remote(ag_a.at[other], ag_a.at[other], "ap", partner).wait_recv()
    remote(ag_b.at[other], ag_b.at[other], "bp", partner).wait_recv()


def finish(geometry, gf_ref, ag_a, ag_b, loss_ref, gf_out, gw_out, gp_out, loss_out, gw, gp, sems):
    blocks, inner, pieces, piece, prow = geometry
    _, layers, _, rows_a, _ = ag_a.shape
    chips = layers * inner
    moves = [pltpu.make_async_copy(gf_ref, gf_out, sems.at[0])]
    moves[0].start()
    moves.append(pltpu.make_async_copy(loss_ref, loss_out, sems.at[2 + pieces]))
    moves[-1].start()
    height = gw_out.shape[0]
    conv_a = rows_a - prow
    for j in range(pieces):
        first = j * piece
        stop = min(height, first + piece)
        for b in range(blocks):
            side, i = b // (blocks // 2), b % (blocks // 2) * pieces + j
            lane = slice(b * LANES, (b + 1) * LANES)
            z, p = i // inner, i % inner
            first_p = (side * chips + i) * prow
            gp[first_p : first_p + prow, :] = ag_a[side, z, p, :prow, :].astype(F32)
            top = min(conv_a, max(stop - first, 0))
            if top > 0:
                gw[first : first + top, lane] = ag_a[side, z, p, prow : prow + top, :].astype(F32)
            low = stop - first - conv_a
            if low > 0:
                gw[first + conv_a : stop, lane] = ag_b[side, p, z, :low, :].astype(F32)
        if stop > first:
            rows = pl.ds(first, stop - first)
            moves.append(pltpu.make_async_copy(gw.at[rows], gw_out.at[rows], sems.at[2 + j]))
            moves[-1].start()
    moves.append(pltpu.make_async_copy(gp, gp_out, sems.at[1]))
    moves[-1].start()
    for move in moves:
        move.wait()


def per_device(devices, batches, features, conv_weight, proj_weight, anchor_pixel, positive_pixel):
    rows_dev, cols, images, channels = features.shape
    group = conv_weight.shape[2]
    key_width = proj_weight.shape[1]
    anchors_dev = anchor_pixel.shape[0]
    chips = devices // 2
    inner = min(4, chips)
    layers = chips // inner
    pixels = rows_dev * cols
    both = 2 * pixels
    half = channels // 2
    taps = conv_weight.shape[0] * conv_weight.shape[1]
    blocks = half // LANES
    pieces = chips // blocks
    piece = -(-(taps * group) // pieces)
    piece = -(-piece // 8) * 8
    prow = channels // devices
    rows_a = (prow + piece) * 5 // 8 // 16 * 16
    rows_b = prow + piece - rows_a
    anchors_core = anchors_dev * chips
    anchor_count = anchors_core * 2 * images * batches
    gradient_scale = 1.0 / (SOFTMAX_TEMPER * anchor_count)
    tot_rows = anchors_core // LANES + 1
    padded = both + 2 * cols
    dma = pltpu.SemaphoreType.DMA
    vmem = pltpu.VMEM
    whole = pl.BlockSpec(memory_space=pltpu.VMEM)
    hbm = pl.BlockSpec(memory_space=pltpu.HBM)
    part = (chips, anchors_dev, LANES)
    scratch = {
        "xa": vmem((both, half), BF16),
        "w": vmem((taps, group, half), BF16),
        "proj": vmem((half, key_width), BF16),
        "anchor": vmem((1, anchors_dev), jnp.int32),
        "positive": vmem((1, anchors_dev), jnp.int32),
        "xh": vmem((2, cols, half), BF16),
        "slope_edge": vmem((2, cols, half), BF16),
        "slope_far": vmem((2, cols, half), BF16),
        "raw_edge": vmem((2, cols, key_width), BF16),
        "raw_far": vmem((2, cols, key_width), BF16),
        "xs": vmem((3, padded, half), BF16),
        "gs": vmem((3, padded, half), BF16),
        "wn": vmem((blocks, taps * LANES, LANES), BF16),
        "wt": vmem((blocks, LANES, taps * LANES), BF16),
        "at": vmem((blocks, taps * LANES, both), BF16),
        "mixed": vmem((both, half), BF16),
        "mixed_t": vmem((half, both), BF16),
        "slope": vmem((both, half), F32),
        "rks": vmem((both, key_width), F32),
        "rkr": vmem((both, key_width), F32),
        "posb": vmem((2, chips, 1, LANES), F32),
        "qall": vmem((2, *part), BF16),
        "pps": vmem(part, BF16),
        "ppr": vmem(part, BF16),
        "ws": vmem(part, BF16),
        "wr": vmem(part, BF16),
        "totb": vmem((chips, tot_rows, LANES), F32),
        "tfin": vmem((2, tot_rows, LANES), F32),
        "gq": vmem((2, anchors_dev, LANES), F32),
        "gm": vmem((both, half), BF16),
        "gp": vmem((both, half), BF16),
        "gr": vmem((both, key_width), BF16),
        "back": vmem((both, half), BF16),
        "l2a_s": vmem((inner, layers, rows_a, LANES), BF16),
        "l2a_r": vmem((inner, layers, rows_a, LANES), BF16),
        "l2b_s": vmem((layers, inner, rows_b, LANES), BF16),
        "l2b_r": vmem((layers, inner, rows_b, LANES), BF16),
        "l3a_s": vmem((layers, rows_a, LANES), BF16),
        "l3a_r": vmem((layers, rows_a, LANES), BF16),
        "l3b_s": vmem((inner, rows_b, LANES), BF16),
        "l3b_r": vmem((inner, rows_b, LANES), BF16),
        "xf": vmem((pixels, channels), BF16),
        "load": dma((6,)),
    }
    singles = ("xp", "rk", "pos", "posp", "q", "qp", "pp", "tot", "totp", "wp", "gqp")
    for name in (*singles, "l2b", "l3a", "l3b", "out", "ap", "bp"):
        scratch[name + "_send"] = dma
        scratch[name + "_recv"] = dma
    for name, count in (("xh", 4), ("sh", 2), ("gh", 2)):
        scratch[name + "_send"] = dma((count,))
        scratch[name + "_recv"] = dma((count,))
    for name, count in (("l2a", layers), ("af", layers), ("an", layers), ("bn", inner), ("bf", inner)):
        scratch[name + "_send"] = dma
        scratch[name + "_recv"] = dma((count,))
    names = ["x_hbm", "w_hbm", "proj_hbm", "anchor_hbm", "positive_hbm"]
    names += ["out", "ag_a", "ag_b", "loss", *scratch]
    sums = (
        jax.ShapeDtypeStruct((pixels, channels), BF16),
        jax.ShapeDtypeStruct((2, layers, inner, rows_a, LANES), BF16),
        jax.ShapeDtypeStruct((2, inner, layers, rows_b, LANES), BF16),
        jax.ShapeDtypeStruct((1, 1), F32),
    )
    parts = pl.pallas_call(
        functools.partial(
            kernel,
            names,
            devices,
            gradient_scale,
            (cols, group, pieces, piece, prow, inner, anchor_count),
        ),
        out_shape=sums,
        in_specs=[hbm] * 5,
        out_specs=(whole,) * 4,
        scratch_shapes=list(scratch.values()),
        compiler_params=pltpu.CompilerParams(
            collective_id=0, has_side_effects=True, vmem_limit_bytes=26000 * 1024
        ),
    )(
        in_hbm(features.reshape(pixels, channels)),
        in_hbm(conv_weight.reshape(taps, group, channels)),
        in_hbm(proj_weight),
        in_hbm(anchor_pixel.reshape(1, anchors_dev)),
        in_hbm(positive_pixel.reshape(1, anchors_dev)),
    )
    grad_features, grad_conv, grad_proj, loss = pl.pallas_call(
        functools.partial(finish, (2 * blocks, inner, pieces, piece, prow)),
        out_shape=(
            jax.ShapeDtypeStruct((pixels, channels), BF16),
            jax.ShapeDtypeStruct((taps * group, channels), F32),
            jax.ShapeDtypeStruct((channels, key_width), F32),
            jax.ShapeDtypeStruct((1, 1), F32),
        ),
        in_specs=[whole] * 4,
        out_specs=(hbm,) * 4,
        scratch_shapes=[
            vmem((taps * group, channels), F32),
            vmem((channels, key_width), F32),
            dma((3 + pieces,)),
        ],
        compiler_params=pltpu.CompilerParams(vmem_limit_bytes=16000 * 1024),
    )(*parts)
    grad_conv = grad_conv.reshape(conv_weight.shape)
    loss_value = loss.reshape(())
    if batches > 1:
        grad_conv, grad_proj, loss_value = lax.psum((grad_conv, grad_proj, loss_value), "batch")
    return (grad_features.reshape(features.shape), grad_conv, grad_proj, loss_value)


def solution(mesh):
    placed = (P("wide", None, "batch", None), P(), P(), P("wide", "batch"), P("wide", "batch"))
    return jax.shard_map(
        functools.partial(per_device, mesh.shape["wide"], mesh.shape["batch"]),
        mesh=mesh,
        in_specs=placed,
        out_specs=(P("wide", None, "batch", None), P(), P(), P()),
        check_vma=False,
    )
```

```python
import functools

import jax
import jax.numpy as jnp
from jax import lax
from jax.experimental import pallas as pl
from jax.experimental.pallas import tpu as pltpu
from jax.sharding import PartitionSpec as P

SOFTMAX_TEMPER = 0.1
EPSILON = 1e-06
LANES = 128
F32 = jnp.float32
BF16 = jnp.bfloat16
MESH = pl.DeviceIdType.MESH

NN = (((1,), (0,)), ((), ()))
NT = (((1,), (1,)), ((), ()))
TN = (((0,), (0,)), ((), ()))


def mm(a, b, dims, precision=None):
    return lax.dot_general(a, b, dims, preferred_element_type=F32, precision=precision)


def in_hbm(array):
    return pltpu.with_memory_space_constraint(array, pltpu.HBM)


def iota(shape, dim):
    return lax.broadcasted_iota(jnp.int32, shape, dim)


def store_shifted(dst, rows, start, values, cols, lane=slice(None)):
    wide = values.astype(F32)
    count = wide.shape[0]
    col = iota(wide.shape, 0) % cols
    dst[1, start : start + rows, lane] = values
    left = jnp.where(col == 0, 0.0, pltpu.roll(wide, 1, 0))
    dst[0, start : start + rows, lane] = left.astype(BF16)
    right = jnp.where(col == cols - 1, 0.0, pltpu.roll(wide, count - 1, 0))
    dst[2, start : start + rows, lane] = right.astype(BF16)


def kernel(names, devices, gradient_scale, geometry, *refs):
    r = dict(zip(names, refs, strict=True))
    cols, group, pieces, piece, prow, inner, anchor_count = geometry
    x_hbm, out_ref, ag_a, ag_b = r["x_hbm"], r["out"], r["ag_a"], r["ag_b"]
    pixels = x_hbm.shape[0]
    channels = x_hbm.shape[1]
    half = channels // 2
    blocks = half // LANES
    per_block = LANES // group
    anchors_dev = r["anchor"].shape[1]
    chips = devices // 2
    both = 2 * pixels
    anchors_core = chips * anchors_dev
    me = lax.axis_index("wide")
    core = lax.rem(me, 2)
    chip = me // 2
    other = 1 - core
    partner = chip * 2 + other
    place = lax.rem(chip, inner)
    layer = chip // inner
    layers = chips // inner
    span = pieces // inner
    conv_a = ag_a.shape[3] - prow
    barrier = pltpu.get_barrier_semaphore()

    def turn(count, start, body):
        def step(k, carry):
            body(lax.rem(start + k, count))
            return carry

        lax.fori_loop(1, count, step, 0)

    def away(k, count, own):
        down = count - 1 - k
        down = down - (down <= own).astype(jnp.int32)
        up = k + (k >= own).astype(jnp.int32)
        return jnp.where(2 * own < count, down, up)

    def farthest(count, own, body):
        def step(k, carry):
            body(away(k, count, own))
            return carry

        lax.fori_loop(0, count - 1, step, 0)

    def nearest(count, own, body):
        farthest_last = count - 2

        def step(k, carry):
            body(away(farthest_last - k, count, own))
            return carry

        lax.fori_loop(0, count - 1, step, 0)

    def across(body):
        body(inner - 1 - place)
        body(place + 1 - 2 * lax.rem(place, 2))
        body(place + 2 - 4 * (place // 2))

    def rise(count, start, body):
        def step(k, carry):
            body(k + (k >= start).astype(jnp.int32))
            return carry

        lax.fori_loop(0, count - 1, step, 0)

    def other_chips(body):
        def layer_step(k, carry):
            z = jnp.where(layer < layers // 2, layers - 1 - k, k)

            def step(j, carry):
                t = z * inner + lax.rem(place + inner - 1 - j, inner)

                @pl.when(t != chip)
                def _():
                    body(t)

                return carry

            return lax.fori_loop(0, inner, step, carry, unroll=True)

        lax.fori_loop(0, layers, layer_step, 0)

    def near_id(target):
        return (layer * inner + target) * 2 + core

    def far_id(target):
        return (target * inner + place) * 2 + core

    def remote(src, dst, name, target, at=None, sent=None):
        recv = r[name + "_recv"]
        send = r[name + "_send"]
        return pltpu.make_async_remote_copy(
            src_ref=src,
            dst_ref=dst,
            send_sem=send if sent is None else send.at[sent],
            recv_sem=recv if at is None else recv.at[at],
            device_id={"wide": target},
            device_id_type=MESH,
        )

    def to_chips(source, landing, name):
        other_chips(lambda t: remote(source(t), landing, name, t * 2 + core).start())

    def from_chips(buf, name):
        view = buf.at[pl.ds(0, chips - 1)]
        remote(view, view, name, partner).wait_recv()

    def sent_chips(buf, name):
        view = buf.at[pl.ds(0, chips - 1)]
        remote(view, view, name, partner).wait_send()

    def signal_entry(target):
        pl.semaphore_signal(barrier, inc=1, device_id={"wide": target}, device_id_type=MESH)

    has_prev = chip > 0
    has_next = chip < chips - 1
    previous = lax.rem(chip + chips - 1, chips)
    following = lax.rem(chip + 1, chips)
    my_half = pl.ds(pl.multiple_of(core * half, LANES), half)
    your_half = pl.ds(pl.multiple_of(other * half, LANES), half)
    my_pixels = pl.ds(pl.multiple_of(core * pixels, 16), pixels)

    loads = [
        pltpu.make_async_copy(src, dst, r["load"].at[n])
        for n, (src, dst) in enumerate(
            (
                (x_hbm, r["xf"]),
                (r["positive_hbm"], r["positive"]),
                (r["w_hbm"].at[:, :, my_half], r["w"]),
                (x_hbm.at[:, my_half], r["xa"].at[my_pixels]),
                (r["proj_hbm"].at[my_half], r["proj"]),
                (r["anchor_hbm"], r["anchor"]),
            )
        )
    ]
    for copy in loads:
        copy.start()

    @pl.when(has_prev)
    def _():
        signal_entry(previous * 2 + other)

    @pl.when(has_next)
    def _():
        signal_entry(following * 2 + other)

    signal_entry(partner)

    def greet(k, carry):
        signal_entry(lax.rem(chip + k, chips) * 2 + core)
        signal_entry(lax.rem(chip + chips - k, chips) * 2 + core)
        return carry

    lax.fori_loop(1, chips // 2, greet, 0)
    signal_entry(lax.rem(chip + chips // 2, chips) * 2 + core)
    loads[0].wait()
    xf = r["xf"]
    pl.semaphore_wait(barrier, chips + has_prev.astype(jnp.int32) + has_next.astype(jnp.int32))

    xh, xa, gp = r["xh"], r["xa"], r["gp"]

    wide = half // 2

    def x_edge(source, slot, target):
        return [
            remote(
                xf.at[pl.ds(source, cols), pl.ds(t * half + q * wide, wide)],
                xh.at[slot, :, pl.ds(q * wide, wide)],
                "xh",
                target * 2 + t,
                at=slot * 2 + q,
                sent=q * 2 + t,
            )
            for q in range(2)
            for t in range(2)
        ]

    up_edge = x_edge(0, 1, previous)
    down_edge = x_edge(pixels - cols, 0, following)
    sends_up = jnp.logical_and(core == 0, has_prev)
    sends_down = jnp.logical_and(core == 1, has_next)

    @pl.when(sends_up)
    def _():
        for copy in up_edge:
            copy.start()

    @pl.when(sends_down)
    def _():
        for copy in down_edge:
            copy.start()

    x_pair = remote(xf.at[:, your_half], xa.at[my_pixels], "xp", partner)
    x_pair.start()

    def edges(src, buf, name):
        up = remote(src.at[0], buf.at[1], name, previous * 2 + core, at=1, sent=0)
        down = remote(src.at[1], buf.at[0], name, following * 2 + core, at=0, sent=1)
        return up, down

    def edges_start(copies):
        for copy, present in zip(copies, (has_prev, has_next), strict=True):
            pl.when(present)(copy.start)

    def edges_sent(copies):
        for copy, present in zip(copies, (has_prev, has_next), strict=True):
            pl.when(present)(copy.wait_send)

    def edges_wait(copies, buf):
        up, down = copies

        @pl.when(has_prev)
        def _():
            down.wait_recv()

        @pl.when(jnp.logical_not(has_prev))
        def _():
            buf[0] = jnp.zeros(buf.shape[1:], buf.dtype)

        @pl.when(has_next)
        def _():
            up.wait_recv()

        @pl.when(jnp.logical_not(has_next))
        def _():
            buf[1] = jnp.zeros(buf.shape[1:], buf.dtype)

    for copy in loads[1:]:
        copy.wait()
    posb = r["posb"]
    posb[core, chip, :, :anchors_dev] = r["positive"][...].astype(F32)
    posb[core, chip, :, anchors_dev : 2 * anchors_dev] = r["anchor"][...].astype(F32)
    posb[core, chip, :, 2 * anchors_dev :] = jnp.zeros((1, LANES - 2 * anchors_dev), F32)
    to_chips(lambda t: posb.at[core, chip], posb.at[core, chip], "pos")

    w_ref, wn, wt, at = r["w"], r["wn"], r["wt"], r["at"]
    tap_count = w_ref.shape[0]
    diagonal = iota((LANES, LANES), 0) // group == iota((LANES, LANES), 1) // group

    def build(b, carry):
        lane = pl.ds(pl.multiple_of(b * LANES, LANES), LANES)
        for tap in range(tap_count):
            slab = w_ref[tap, :, lane].astype(F32)
            full = jnp.where(diagonal, jnp.concatenate([slab] * per_block, axis=0), 0.0)
            full = full.astype(BF16)
            wn[b, tap * LANES : (tap + 1) * LANES, :] = full
            wt[b, :, tap * LANES : (tap + 1) * LANES] = full
        return carry

    lax.fori_loop(0, blocks, build, 0)
    xs, gs = r["xs"], r["gs"]
    x_pair.wait_recv()
    store_shifted(xs, both, cols, xa[...], cols)

    def diagonal_col(row, first):
        lane = iota((anchors_dev, LANES), 1)
        hit = lane == iota((anchors_dev, LANES), 0) + first
        return jnp.sum(jnp.where(hit, row, 0.0), axis=1, keepdims=True)

    def pick_of(row, owner):
        column = diagonal_col(row, anchors_dev) + (owner * pixels).astype(F32)
        return jnp.where(iota((anchors_dev, both), 1).astype(F32) == column, 1.0, 0.0)

    pick_own = pick_of(posb[core, chip], core)

    @pl.when(jnp.logical_not(has_prev))
    def _():
        xh[0] = jnp.zeros(xh.shape[1:], xh.dtype)

    @pl.when(jnp.logical_not(has_next))
    def _():
        xh[1] = jnp.zeros(xh.shape[1:], xh.dtype)

    def x_edges_wait(q):
        lane = slice(q * wide, (q + 1) * wide)
        for slot, present in ((0, has_prev), (1, has_next)):
            view = xh.at[slot, :, pl.ds(q * wide, wide)]
            copy = remote(view, view, "xh", partner, at=slot * 2 + q, sent=0)

            @pl.when(present)
            def _():
                copy.wait_recv()

        store_shifted(xs, cols, 0, xh[0, :, lane], cols, lane)
        store_shifted(xs, cols, cols + both, xh[1, :, lane], cols, lane)

    def windows(buf, lane, flip):
        parts = []
        for row in range(3):
            for col in range(3):
                rr, cc = (2 - row, 2 - col) if flip else (row, col)
                parts.append(buf[cc, rr * cols : rr * cols + both, lane])
        return jnp.concatenate(parts, axis=1)

    mixed, mixed_t, slope, proj_ref = r["mixed"], r["mixed_t"], r["slope"], r["proj"]

    def forward(b, carry):
        lane = pl.ds(pl.multiple_of(b * LANES, LANES), LANES)
        pre = mm(windows(xs, lane, False), wn[b], NN)
        sig = 1.0 / (1.0 + jnp.exp(-pre))
        mixed[:, lane] = (xa[:, lane].astype(F32) + pre * sig).astype(BF16)
        slope[:, lane] = sig * (1.0 + pre * (1.0 - sig))
        return carry

    for q in range(2):
        x_edges_wait(q)
        lax.fori_loop(q * blocks // 2, (q + 1) * blocks // 2, forward, 0, unroll=True)

    rks, rkr = r["rks"], r["rkr"]
    rks[...] = mm(mixed[...], proj_ref[...], NN)
    rk_pair = remote(rks, rkr, "rk", partner)
    rk_pair.start()
    from_chips(posb.at[core], "pos")
    pos_pair = remote(posb.at[core], posb.at[core], "posp", partner)
    pos_pair.start()
    rk_pair.wait_recv()
    raw_key = rks[...] + rkr[...]
    norm_key = jnp.sqrt(jnp.sum(raw_key * raw_key, axis=1, keepdims=True) + EPSILON)
    unit_key = raw_key / norm_key
    keys = unit_key.astype(BF16)
    qall = r["qall"]
    qall[core, chip] = mm(pick_own.astype(BF16), keys, NN).astype(BF16)
    to_chips(lambda t: qall.at[core, chip], qall.at[core, chip], "q")

    slope_edge, slope_far = r["slope_edge"], r["slope_far"]
    slope_edge[0] = slope[:cols, :].astype(BF16)
    slope_edge[1] = slope[both - cols :, :].astype(BF16)
    slope_edges = edges(slope_edge, slope_far, "sh")
    edges_start(slope_edges)

    def hits(parity):
        own_lane = iota((chips, anchors_dev, LANES), 1) == iota((chips, anchors_dev, LANES), 2)
        pos_all = jnp.sum(jnp.where(own_lane, posb[parity], 0.0), axis=2, keepdims=True)
        pos_local = pos_all - (chip * both).astype(F32)
        hit3 = jnp.where(
            iota((chips, anchors_dev, both), 2).astype(F32) == pos_local, 1.0, 0.0
        )
        return hit3.reshape(anchors_core, both).astype(BF16)

    hit_own = hits(core)
    part_pos = mm(hit_own, keys, NN)
    pps, ppr = r["pps"], r["ppr"]
    pps[...] = part_pos.reshape(chips, anchors_dev, LANES).astype(BF16)
    ppr[chip] = pps[chip]

    def flip_over(b, carry):
        start = pl.multiple_of(b * LANES, LANES)
        lane = pl.ds(start, LANES)
        at[b] = windows(xs, lane, False).T
        mixed_t[lane, :] = mixed[:, lane].T
        return carry

    lax.fori_loop(0, blocks, flip_over, 0, unroll=True)
    to_chips(lambda t: pps.at[t], ppr.at[chip], "pp")

    from_chips(qall.at[core], "q")
    q_pair = remote(qall.at[core], qall.at[core], "qp", partner)
    q_pair.start()
    queries = qall[core].reshape(anchors_core, LANES)
    exp_own = jnp.exp(mm(keys, queries, NT) / SOFTMAX_TEMPER)
    part_total = jnp.sum(exp_own, axis=0, keepdims=True)
    pos_sum = jnp.sum(
        jnp.sum(part_pos * queries.astype(F32), axis=1, keepdims=True), axis=0, keepdims=True
    )
    totb, tfin = r["totb"], r["tfin"]
    tot_rows = anchors_core // LANES
    for n in range(tot_rows):
        totb[chip, n : n + 1, :] = part_total[:, n * LANES : (n + 1) * LANES]
    totb[chip, tot_rows : tot_rows + 1, :] = jnp.broadcast_to(pos_sum, (1, LANES))
    to_chips(lambda t: totb.at[chip], totb.at[chip], "tot")
    part_weighted = mm(exp_own.astype(BF16), keys, TN)
    ws, wr = r["ws"], r["wr"]
    ws[...] = part_weighted.reshape(chips, anchors_dev, LANES).astype(BF16)
    to_chips(lambda t: ws.at[t], wr.at[chip], "wp")
    wr[chip] = ws[chip]
    pos_pair.wait_recv()
    hit_other = hits(other)
    pick_other = pick_of(posb[other, chip], other)

    q_pair.wait_recv()
    queries_other = qall[other].reshape(anchors_core, LANES)
    exp_other = jnp.exp(mm(keys, queries_other, NT) / SOFTMAX_TEMPER)
    pushed = mm(hit_own, queries, TN) + mm(hit_other, queries_other, TN)

    def whole_row(sums):
        return jnp.concatenate([sums[n : n + 1, :] for n in range(tot_rows)], axis=1)

    def loss_of(sums, row):
        return jnp.sum(jnp.log(row), axis=1, keepdims=True) - sums[
            tot_rows : tot_rows + 1, 0:1
        ] / SOFTMAX_TEMPER

    def pulled_by(exp_scores, row, asked):
        inverse = (1.0 / row).astype(BF16).astype(F32)
        return mm((exp_scores * inverse).astype(BF16), asked, NN)

    from_chips(totb, "tot")
    sums_own = jnp.sum(totb[...], axis=0)
    tfin[core] = sums_own
    tot_pair = remote(tfin.at[core], tfin.at[core], "totp", partner)
    tot_pair.start()
    row_own = whole_row(sums_own)
    mine = iota((anchors_dev, anchors_core), 1) == chip * anchors_dev + iota(
        (anchors_dev, anchors_core), 0
    )
    own_total = jnp.sum(jnp.where(mine, row_own, 0.0), axis=1, keepdims=True)
    gq = r["gq"]
    from_chips(ppr, "pp")
    from_chips(wr, "wp")
    weighted = jnp.sum(wr[...].astype(F32), axis=0)
    pos_key = jnp.sum(ppr[...].astype(F32), axis=0)
    gq[core] = (weighted / own_total - pos_key) * gradient_scale
    gq_pair = remote(gq.at[core], gq.at[core], "gqp", partner)
    gq_pair.start()
    pulled = pulled_by(exp_own, row_own, queries)
    tot_pair.wait_recv()
    sums_other = tfin[other]
    row_other = whole_row(sums_other)
    pulled = pulled + pulled_by(exp_other, row_other, queries_other)
    grad_key = gradient_scale * (pulled - pushed)
    gq_pair.wait_recv()
    grad_key = grad_key + mm(pick_own, gq[core], TN, lax.Precision.HIGHEST)
    grad_key = grad_key + mm(pick_other, gq[other], TN, lax.Precision.HIGHEST)
    along = jnp.sum(grad_key * unit_key, axis=1, keepdims=True)
    grad_raw = ((grad_key - unit_key * along) / norm_key).astype(BF16)
    grad_mixed = mm(grad_raw, proj_ref[...], NT).astype(BF16)
    gm, gr = r["gm"], r["gr"]
    gm[...] = grad_mixed
    gr[...] = grad_raw
    gp[...] = (grad_mixed.astype(F32) * slope[...]).astype(BF16)

    raw_edge, raw_far = r["raw_edge"], r["raw_far"]
    raw_edge[0] = grad_raw[:cols]
    raw_edge[1] = grad_raw[both - cols :]
    raw_edges = edges(raw_edge, raw_far, "gh")
    l2a_s, l2a_r, l2b_s, l2b_r = r["l2a_s"], r["l2a_r"], r["l2b_s"], r["l2b_r"]
    l3a_s, l3a_r, l3b_s, l3b_r = r["l3a_s"], r["l3a_r"], r["l3b_s"], r["l3b_r"]
    lane_group = iota((group, LANES), 1) // group
    own_block = layer // span

    def block_at(k):
        return jnp.where(k == blocks - 1, own_block, away(k, blocks, own_block))


    def weight_grad(k, carry):
        b = block_at(k)
        lane = pl.ds(pl.multiple_of(b * LANES, LANES), LANES)
        proj_part = mm(mixed_t[lane, :], gr[...], NN)
        full = mm(at[b], gp[:, lane], NN)
        taps = []
        for tap in range(tap_count):
            folded = jnp.zeros((group, LANES), F32)
            for g in range(per_block):
                first = tap * LANES + g * group
                folded = jnp.where(lane_group == g, full[first : first + group], folded)
            taps.append(folded)
        short = pieces * piece - tap_count * group
        if short:
            taps.append(jnp.zeros((short, LANES), F32))
        conv = jnp.concatenate(taps, axis=0)
        for j in range(pieces):
            z, p = b * span + j // inner, j % inner
            top = j * piece
            l2a_s[p, z, :prow, :] = proj_part[j * prow : (j + 1) * prow].astype(BF16)
            l2a_s[p, z, prow:, :] = conv[top : top + conv_a].astype(BF16)
            l2b_s[z, p] = conv[top + conv_a : top + piece].astype(BF16)
        for j in range(span):
            z = b * span + j
            across(
                lambda t: remote(
                    l2a_s.at[t, z], l2a_r.at[place, z], "l2a", near_id(t), at=z
                ).start(),
            )
            l2a_r[place, z] = l2a_s[place, z]

            @pl.when(z != layer)
            def _():
                remote(l2b_s.at[z], l2b_r.at[layer], "l2b", far_id(z)).start()

        return carry

    lax.fori_loop(0, blocks, weight_grad, 0)
    edges_start(raw_edges)
    r["loss"][...] = (loss_of(sums_own, row_own) + loss_of(sums_other, row_other)) / anchor_count
    l2b_r[layer] = l2b_s[layer]
    store_shifted(gs, both, cols, gp[...], cols)

    def near_summed(k, carry):
        z = block_at(k // span) * span + lax.rem(k, span)
        view = l2a_r.at[pl.ds(0, inner - 1), z]
        remote(view, view, "l2a", partner, at=z).wait_recv()
        l3a_s[z] = jnp.sum(l2a_r[:, z].astype(F32), axis=0).astype(BF16)

        @pl.when(z != layer)
        def _():
            remote(l3a_s.at[z], l3a_r.at[layer], "l3a", far_id(z)).start()

        return carry

    lax.fori_loop(0, layers, near_summed, 0)
    l3a_r[layer] = l3a_s[layer]
    view = l2b_r.at[pl.ds(0, layers - 1)]
    remote(view, view, "l2b", partner).wait_recv()
    for p in range(inner):
        l3b_s[p] = jnp.sum(l2b_r[:, p].astype(F32), axis=0).astype(BF16)
    turn(
        inner,
        place,
        lambda t: remote(l3b_s.at[t], l3b_r.at[place], "l3b", near_id(t)).start(),
    )
    l3b_r[place] = l3b_s[place]

    view = l3a_r.at[pl.ds(0, layers - 1)]
    remote(view, view, "l3a", partner).wait_recv()
    ag_a[core, layer, place] = jnp.sum(l3a_r[...].astype(F32), axis=0).astype(BF16)

    def a_copy(z, at, name, target):
        chunk = ag_a.at[core, z, place]
        return remote(chunk, chunk, name, target, at=at)

    def b_copy(p, at, name, target):
        chunk = ag_b.at[core, p, layer]
        return remote(chunk, chunk, name, target, at=at)

    farthest(layers, layer, lambda t: a_copy(layer, layer, "af", far_id(t)).start())

    view = l3b_r.at[pl.ds(0, inner - 1)]
    remote(view, view, "l3b", partner).wait_recv()
    ag_b[core, place, layer] = jnp.sum(l3b_r[...].astype(F32), axis=0).astype(BF16)
    rise(inner, place, lambda t: b_copy(place, place, "bn", near_id(t)).start())
    rise(inner, place, lambda t: a_copy(layer, layer, "an", near_id(t)).start())
    farthest(layers, layer, lambda t: b_copy(place, place, "bf", far_id(t)).start())

    edges_wait(slope_edges, slope_far)
    edges_wait(raw_edges, raw_far)
    for slot in range(2):
        edge = mm(raw_far[slot], proj_ref[...], NT).astype(BF16).astype(F32)
        edge = (edge * slope_far[slot].astype(F32)).astype(BF16)
        store_shifted(gs, cols, slot * (cols + both), edge, cols)
    back_all = r["back"]

    def backward(b, carry):
        lane = pl.ds(pl.multiple_of(b * LANES, LANES), LANES)
        back = mm(windows(gs, lane, True), wt[b], NT).astype(BF16)
        back_all[:, lane] = (back.astype(F32) + gm[:, lane].astype(F32)).astype(BF16)
        return carry

    lax.fori_loop(0, blocks, backward, 0, unroll=True)
    out_pair = remote(
        back_all.at[pl.ds(pl.multiple_of(other * pixels, 16), pixels)],
        out_ref.at[:, my_half],
        "out",
        partner,
    )
    out_pair.start()
    out_ref[:, my_half] = back_all[my_pixels, :]

    def a_arrived(z):
        chunk = ag_a.at[core, z, place]
        remote(chunk, chunk, "af", partner, at=z).wait_recv()
        rise(inner, place, lambda t: a_copy(z, z, "an", near_id(t)).start())

    def b_arrived(p):
        chunk = ag_b.at[core, p, layer]
        remote(chunk, chunk, "bn", partner, at=p).wait_recv()
        farthest(layers, layer, lambda t: b_copy(p, p, "bf", far_id(t)).start())

    nearest(layers, layer, a_arrived)
    rise(inner, place, b_arrived)

    def a_whole(k, carry):
        z = jnp.where(k == 0, layer, away(layers - 1 - k, layers, layer))
        view = ag_a.at[core, z, pl.ds(0, inner - 1)]
        remote(view, view, "an", partner, at=z).wait_recv()
        remote(ag_a.at[core, z], ag_a.at[core, z], "ap", partner).start()
        return carry

    def b_whole(k, carry):
        p = lax.rem(place + k, inner)
        view = ag_b.at[core, p, pl.ds(0, layers - 1)]
        remote(view, view, "bf", partner, at=p).wait_recv()
        remote(ag_b.at[core, p], ag_b.at[core, p], "bp", partner).start()
        return carry

    lax.fori_loop(0, layers, a_whole, 0)
    lax.fori_loop(0, inner, b_whole, 0)

    @pl.when(sends_up)
    def _():
        for copy in up_edge:
            copy.wait_send()

    @pl.when(sends_down)
    def _():
        for copy in down_edge:
            copy.wait_send()

    edges_sent(slope_edges)
    edges_sent(raw_edges)

    for copy in (x_pair, rk_pair, pos_pair, q_pair, tot_pair, gq_pair):
        copy.wait_send()
    sent_chips(posb.at[core], "pos")
    sent_chips(qall.at[core], "q")
    sent_chips(pps, "pp")
    sent_chips(totb, "tot")
    sent_chips(ws, "wp")

    def sent(view, name, at=None):
        remote(view, view, name, partner, at=at).wait_send()

    sent(l2a_s.at[pl.ds(0, inner - 1)], "l2a", 0)
    sent(l2b_s.at[pl.ds(0, layers - 1)], "l2b")
    sent(l3a_s.at[pl.ds(0, layers - 1)], "l3a")
    sent(l3b_s.at[pl.ds(0, inner - 1)], "l3b")
    sent(ag_a.at[core, pl.ds(0, layers - 1), 0], "af", 0)
    sent(ag_a.at[core, :, pl.ds(0, inner - 1)], "an", 0)
    sent(ag_b.at[core, pl.ds(0, inner - 1), 0], "bn", 0)
    sent(ag_b.at[core, :, pl.ds(0, layers - 1)], "bf", 0)
    out_pair.wait()
    sent(ag_a.at[core], "ap")
    sent(ag_b.at[core], "bp")
    remote(ag_a.at[other], ag_a.at[other], "ap", partner).wait_recv()
    remote(ag_b.at[other], ag_b.at[other], "bp", partner).wait_recv()


def finish(geometry, gf_ref, ag_a, ag_b, loss_ref, gf_out, gw_out, gp_out, loss_out, gw, gp, sems):
    blocks, inner, pieces, piece, prow = geometry
    _, layers, _, rows_a, _ = ag_a.shape
    chips = layers * inner
    moves = [pltpu.make_async_copy(gf_ref, gf_out, sems.at[0])]
    moves[0].start()
    moves.append(pltpu.make_async_copy(loss_ref, loss_out, sems.at[2 + pieces]))
    moves[-1].start()
    height = gw_out.shape[0]
    conv_a = rows_a - prow
    for j in range(pieces):
        first = j * piece
        stop = min(height, first + piece)
        for b in range(blocks):
            side, i = b // (blocks // 2), b % (blocks // 2) * pieces + j
            lane = slice(b * LANES, (b + 1) * LANES)
            z, p = i // inner, i % inner
            first_p = (side * chips + i) * prow
            gp[first_p : first_p + prow, :] = ag_a[side, z, p, :prow, :].astype(F32)
            top = min(conv_a, max(stop - first, 0))
            if top > 0:
                gw[first : first + top, lane] = ag_a[side, z, p, prow : prow + top, :].astype(F32)
            low = stop - first - conv_a
            if low > 0:
                gw[first + conv_a : stop, lane] = ag_b[side, p, z, :low, :].astype(F32)
        if stop > first:
            rows = pl.ds(first, stop - first)
            moves.append(pltpu.make_async_copy(gw.at[rows], gw_out.at[rows], sems.at[2 + j]))
            moves[-1].start()
    moves.append(pltpu.make_async_copy(gp, gp_out, sems.at[1]))
    moves[-1].start()
    for move in moves:
        move.wait()


def per_device(devices, batches, features, conv_weight, proj_weight, anchor_pixel, positive_pixel):
    rows_dev, cols, images, channels = features.shape
    group = conv_weight.shape[2]
    key_width = proj_weight.shape[1]
    anchors_dev = anchor_pixel.shape[0]
    chips = devices // 2
    inner = min(4, chips)
    layers = chips // inner
    pixels = rows_dev * cols
    both = 2 * pixels
    half = channels // 2
    taps = conv_weight.shape[0] * conv_weight.shape[1]
    blocks = half // LANES
    pieces = chips // blocks
    piece = -(-(taps * group) // pieces)
    piece = -(-piece // 8) * 8
    prow = channels // devices
    rows_a = (prow + piece) * 5 // 8 // 16 * 16
    rows_b = prow + piece - rows_a
    anchors_core = anchors_dev * chips
    anchor_count = anchors_core * 2 * images * batches
    gradient_scale = 1.0 / (SOFTMAX_TEMPER * anchor_count)
    tot_rows = anchors_core // LANES + 1
    padded = both + 2 * cols
    dma = pltpu.SemaphoreType.DMA
    vmem = pltpu.VMEM
    whole = pl.BlockSpec(memory_space=pltpu.VMEM)
    hbm = pl.BlockSpec(memory_space=pltpu.HBM)
    part = (chips, anchors_dev, LANES)
    scratch = {
        "xa": vmem((both, half), BF16),
        "w": vmem((taps, group, half), BF16),
        "proj": vmem((half, key_width), BF16),
        "anchor": vmem((1, anchors_dev), jnp.int32),
        "positive": vmem((1, anchors_dev), jnp.int32),
        "xh": vmem((2, cols, half), BF16),
        "slope_edge": vmem((2, cols, half), BF16),
        "slope_far": vmem((2, cols, half), BF16),
        "raw_edge": vmem((2, cols, key_width), BF16),
        "raw_far": vmem((2, cols, key_width), BF16),
        "xs": vmem((3, padded, half), BF16),
        "gs": vmem((3, padded, half), BF16),
        "wn": vmem((blocks, taps * LANES, LANES), BF16),
        "wt": vmem((blocks, LANES, taps * LANES), BF16),
        "at": vmem((blocks, taps * LANES, both), BF16),
        "mixed": vmem((both, half), BF16),
        "mixed_t": vmem((half, both), BF16),
        "slope": vmem((both, half), F32),
        "rks": vmem((both, key_width), F32),
        "rkr": vmem((both, key_width), F32),
        "posb": vmem((2, chips, 1, LANES), F32),
        "qall": vmem((2, *part), BF16),
        "pps": vmem(part, BF16),
        "ppr": vmem(part, BF16),
        "ws": vmem(part, BF16),
        "wr": vmem(part, BF16),
        "totb": vmem((chips, tot_rows, LANES), F32),
        "tfin": vmem((2, tot_rows, LANES), F32),
        "gq": vmem((2, anchors_dev, LANES), F32),
        "gm": vmem((both, half), BF16),
        "gp": vmem((both, half), BF16),
        "gr": vmem((both, key_width), BF16),
        "back": vmem((both, half), BF16),
        "l2a_s": vmem((inner, layers, rows_a, LANES), BF16),
        "l2a_r": vmem((inner, layers, rows_a, LANES), BF16),
        "l2b_s": vmem((layers, inner, rows_b, LANES), BF16),
        "l2b_r": vmem((layers, inner, rows_b, LANES), BF16),
        "l3a_s": vmem((layers, rows_a, LANES), BF16),
        "l3a_r": vmem((layers, rows_a, LANES), BF16),
        "l3b_s": vmem((inner, rows_b, LANES), BF16),
        "l3b_r": vmem((inner, rows_b, LANES), BF16),
        "xf": vmem((pixels, channels), BF16),
        "load": dma((6,)),
    }
    singles = ("xp", "rk", "pos", "posp", "q", "qp", "pp", "tot", "totp", "wp", "gqp")
    for name in (*singles, "l2b", "l3a", "l3b", "out", "ap", "bp"):
        scratch[name + "_send"] = dma
        scratch[name + "_recv"] = dma
    for name, count in (("xh", 4), ("sh", 2), ("gh", 2)):
        scratch[name + "_send"] = dma((count,))
        scratch[name + "_recv"] = dma((count,))
    for name, count in (("l2a", layers), ("af", layers), ("an", layers), ("bn", inner), ("bf", inner)):
        scratch[name + "_send"] = dma
        scratch[name + "_recv"] = dma((count,))
    names = ["x_hbm", "w_hbm", "proj_hbm", "anchor_hbm", "positive_hbm"]
    names += ["out", "ag_a", "ag_b", "loss", *scratch]
    sums = (
        jax.ShapeDtypeStruct((pixels, channels), BF16),
        jax.ShapeDtypeStruct((2, layers, inner, rows_a, LANES), BF16),
        jax.ShapeDtypeStruct((2, inner, layers, rows_b, LANES), BF16),
        jax.ShapeDtypeStruct((1, 1), F32),
    )
    parts = pl.pallas_call(
        functools.partial(
            kernel,
            names,
            devices,
            gradient_scale,
            (cols, group, pieces, piece, prow, inner, anchor_count),
        ),
        out_shape=sums,
        in_specs=[hbm] * 5,
        out_specs=(whole,) * 4,
        scratch_shapes=list(scratch.values()),
        compiler_params=pltpu.CompilerParams(
            collective_id=0, has_side_effects=True, vmem_limit_bytes=26000 * 1024
        ),
    )(
        in_hbm(features.reshape(pixels, channels)),
        in_hbm(conv_weight.reshape(taps, group, channels)),
        in_hbm(proj_weight),
        in_hbm(anchor_pixel.reshape(1, anchors_dev)),
        in_hbm(positive_pixel.reshape(1, anchors_dev)),
    )
    grad_features, grad_conv, grad_proj, loss = pl.pallas_call(
        functools.partial(finish, (2 * blocks, inner, pieces, piece, prow)),
        out_shape=(
            jax.ShapeDtypeStruct((pixels, channels), BF16),
            jax.ShapeDtypeStruct((taps * group, channels), F32),
            jax.ShapeDtypeStruct((channels, key_width), F32),
            jax.ShapeDtypeStruct((1, 1), F32),
        ),
        in_specs=[whole] * 4,
        out_specs=(hbm,) * 4,
        scratch_shapes=[
            vmem((taps * group, channels), F32),
            vmem((channels, key_width), F32),
            dma((3 + pieces,)),
        ],
        compiler_params=pltpu.CompilerParams(vmem_limit_bytes=16000 * 1024),
    )(*parts)
    grad_conv = grad_conv.reshape(conv_weight.shape)
    loss_value = loss.reshape(())
    if batches > 1:
        grad_conv, grad_proj, loss_value = lax.psum((grad_conv, grad_proj, loss_value), "batch")
    return (grad_features.reshape(features.shape), grad_conv, grad_proj, loss_value)


def solution(mesh):
    placed = (P("wide", None, "batch", None), P(), P(), P("wide", "batch"), P("wide", "batch"))
    return jax.shard_map(
        functools.partial(per_device, mesh.shape["wide"], mesh.shape["batch"]),
        mesh=mesh,
        in_specs=placed,
        out_specs=(P("wide", None, "batch", None), P(), P(), P()),
        check_vma=False,
    )
```

```python
import functools

import jax
import jax.numpy as jnp
from jax import lax
from jax.experimental import pallas as pl
from jax.experimental.pallas import tpu as pltpu
from jax.sharding import PartitionSpec as P

SOFTMAX_TEMPER = 0.1
EPSILON = 1e-06
LANES = 128
F32 = jnp.float32
BF16 = jnp.bfloat16
MESH = pl.DeviceIdType.MESH

NN = (((1,), (0,)), ((), ()))
NT = (((1,), (1,)), ((), ()))
TN = (((0,), (0,)), ((), ()))


def mm(a, b, dims, precision=None):
    return lax.dot_general(a, b, dims, preferred_element_type=F32, precision=precision)


def in_hbm(array):
    return pltpu.with_memory_space_constraint(array, pltpu.HBM)


def iota(shape, dim):
    return lax.broadcasted_iota(jnp.int32, shape, dim)


def store_shifted(dst, rows, start, values, cols, lane=slice(None)):
    wide = values.astype(F32)
    count = wide.shape[0]
    col = iota(wide.shape, 0) % cols
    dst[1, start : start + rows, lane] = values
    left = jnp.where(col == 0, 0.0, pltpu.roll(wide, 1, 0))
    dst[0, start : start + rows, lane] = left.astype(BF16)
    right = jnp.where(col == cols - 1, 0.0, pltpu.roll(wide, count - 1, 0))
    dst[2, start : start + rows, lane] = right.astype(BF16)


def kernel(names, devices, gradient_scale, geometry, *refs):
    r = dict(zip(names, refs, strict=True))
    cols, group, pieces, piece, prow, inner, anchor_count = geometry
    x_hbm, out_ref, ag_a, ag_b = r["x_hbm"], r["out"], r["ag_a"], r["ag_b"]
    pixels = x_hbm.shape[0]
    channels = x_hbm.shape[1]
    half = channels // 2
    blocks = half // LANES
    per_block = LANES // group
    anchors_dev = r["anchor"].shape[1]
    chips = devices // 2
    both = 2 * pixels
    anchors_core = chips * anchors_dev
    me = lax.axis_index("wide")
    core = lax.rem(me, 2)
    chip = me // 2
    other = 1 - core
    partner = chip * 2 + other
    place = lax.rem(chip, inner)
    layer = chip // inner
    layers = chips // inner
    span = pieces // inner
    conv_a = ag_a.shape[3] - prow
    barrier = pltpu.get_barrier_semaphore()

    def turn(count, start, body):
        def step(k, carry):
            body(lax.rem(start + k, count))
            return carry

        lax.fori_loop(1, count, step, 0)

    def away(k, count, own):
        down = count - 1 - k
        down = down - (down <= own).astype(jnp.int32)
        up = k + (k >= own).astype(jnp.int32)
        return jnp.where(2 * own < count, down, up)

    def farthest(count, own, body):
        def step(k, carry):
            body(away(k, count, own))
            return carry

        lax.fori_loop(0, count - 1, step, 0)

    def nearest(count, own, body):
        farthest_last = count - 2

        def step(k, carry):
            body(away(farthest_last - k, count, own))
            return carry

        lax.fori_loop(0, count - 1, step, 0)

    def across(body):
        body(inner - 1 - place)
        body(place + 1 - 2 * lax.rem(place, 2))
        body(place + 2 - 4 * (place // 2))

    def rise(count, start, body):
        def step(k, carry):
            body(k + (k >= start).astype(jnp.int32))
            return carry

        lax.fori_loop(0, count - 1, step, 0)

    def other_chips(body):
        def layer_step(k, carry):
            z = jnp.where(layer < layers // 2, layers - 1 - k, k)

            def step(j, carry):
                t = z * inner + lax.rem(place + inner - 1 - j, inner)

                @pl.when(t != chip)
                def _():
                    body(t)

                return carry

            return lax.fori_loop(0, inner, step, carry, unroll=True)

        lax.fori_loop(0, layers, layer_step, 0)

    def near_id(target):
        return (layer * inner + target) * 2 + core

    def far_id(target):
        return (target * inner + place) * 2 + core

    main = ("xp", "rk", "q", "qp", "pp", "wp", "gqp", "l2a", "l3a", "af", "an", "out", "ap")
    rest = ("l2b", "l3b", "bn", "bf", "bp")
    sender = {name: "main" for name in main} | {name: "rest" for name in rest}

    def remote(src, dst, name, target, at=None, sent=None):
        recv = r[name + "_recv"]
        send = r[sender.get(name, name) + "_send"]
        return pltpu.make_async_remote_copy(
            src_ref=src,
            dst_ref=dst,
            send_sem=send if sent is None else send.at[sent],
            recv_sem=recv if at is None else recv.at[at],
            device_id={"wide": target},
            device_id_type=MESH,
        )

    def to_chips(source, landing, name):
        other_chips(lambda t: remote(source(t), landing, name, t * 2 + core).start())

    def from_chips(buf, name):
        view = buf.at[pl.ds(0, chips - 1)]
        remote(view, view, name, partner).wait_recv()

    def sent_chips(buf, name):
        view = buf.at[pl.ds(0, chips - 1)]
        remote(view, view, name, partner).wait_send()

    def signal_entry(target):
        pl.semaphore_signal(barrier, inc=1, device_id={"wide": target}, device_id_type=MESH)

    has_prev = chip > 0
    has_next = chip < chips - 1
    previous = lax.rem(chip + chips - 1, chips)
    following = lax.rem(chip + 1, chips)
    my_half = pl.ds(pl.multiple_of(core * half, LANES), half)
    your_half = pl.ds(pl.multiple_of(other * half, LANES), half)
    my_pixels = pl.ds(pl.multiple_of(core * pixels, 16), pixels)

    loads = [
        pltpu.make_async_copy(src, dst, r["load"].at[n])
        for n, (src, dst) in enumerate(
            (
                (x_hbm, r["xf"]),
                (r["positive_hbm"], r["positive"]),
                (r["w_hbm"].at[:, :, my_half], r["w"]),
                (x_hbm.at[:, my_half], r["xa"].at[my_pixels]),
                (r["proj_hbm"].at[my_half], r["proj"]),
                (r["anchor_hbm"], r["anchor"]),
            )
        )
    ]
    for copy in loads:
        copy.start()

    @pl.when(has_prev)
    def _():
        signal_entry(previous * 2 + other)

    @pl.when(has_next)
    def _():
        signal_entry(following * 2 + other)

    signal_entry(partner)

    def greet(k, carry):
        signal_entry(lax.rem(chip + k, chips) * 2 + core)
        signal_entry(lax.rem(chip + chips - k, chips) * 2 + core)
        return carry

    lax.fori_loop(1, chips // 2, greet, 0)
    signal_entry(lax.rem(chip + chips // 2, chips) * 2 + core)
    loads[0].wait()
    xf = r["xf"]
    pl.semaphore_wait(barrier, chips + has_prev.astype(jnp.int32) + has_next.astype(jnp.int32))

    xh, xa, gp = r["xh"], r["xa"], r["gp"]

    wide = half // 2

    def x_edge(source, slot, target):
        return [
            remote(
                xf.at[pl.ds(source, cols), pl.ds(t * half + q * wide, wide)],
                xh.at[slot, :, pl.ds(q * wide, wide)],
                "xh",
                target * 2 + t,
                at=slot * 2 + q,
                sent=q * 2 + t,
            )
            for q in range(2)
            for t in range(2)
        ]

    up_edge = x_edge(0, 1, previous)
    down_edge = x_edge(pixels - cols, 0, following)
    sends_up = jnp.logical_and(core == 0, has_prev)
    sends_down = jnp.logical_and(core == 1, has_next)

    @pl.when(sends_up)
    def _():
        for copy in up_edge:
            copy.start()

    @pl.when(sends_down)
    def _():
        for copy in down_edge:
            copy.start()

    x_pair = remote(xf.at[:, your_half], xa.at[my_pixels], "xp", partner)
    x_pair.start()

    def edges(src, buf, name):
        up = remote(src.at[0], buf.at[1], name, previous * 2 + core, at=1, sent=0)
        down = remote(src.at[1], buf.at[0], name, following * 2 + core, at=0, sent=1)
        return up, down

    def edges_start(copies):
        for copy, present in zip(copies, (has_prev, has_next), strict=True):
            pl.when(present)(copy.start)

    def edges_sent(copies):
        for copy, present in zip(copies, (has_prev, has_next), strict=True):
            pl.when(present)(copy.wait_send)

    def edges_wait(copies, buf):
        up, down = copies

        @pl.when(has_prev)
        def _():
            down.wait_recv()

        @pl.when(jnp.logical_not(has_prev))
        def _():
            buf[0] = jnp.zeros(buf.shape[1:], buf.dtype)

        @pl.when(has_next)
        def _():
            up.wait_recv()

        @pl.when(jnp.logical_not(has_next))
        def _():
            buf[1] = jnp.zeros(buf.shape[1:], buf.dtype)

    for copy in loads[1:]:
        copy.wait()
    posb = r["posb"]
    posb[core, chip, :, :anchors_dev] = r["positive"][...].astype(F32)
    posb[core, chip, :, anchors_dev : 2 * anchors_dev] = r["anchor"][...].astype(F32)
    posb[core, chip, :, 2 * anchors_dev :] = jnp.zeros((1, LANES - 2 * anchors_dev), F32)
    to_chips(lambda t: posb.at[core, chip], posb.at[core, chip], "pos")

    w_ref, wn, wt, at = r["w"], r["wn"], r["wt"], r["at"]
    tap_count = w_ref.shape[0]
    diagonal = iota((LANES, LANES), 0) // group == iota((LANES, LANES), 1) // group

    def build(b, carry):
        lane = pl.ds(pl.multiple_of(b * LANES, LANES), LANES)
        for tap in range(tap_count):
            slab = w_ref[tap, :, lane].astype(F32)
            full = jnp.where(diagonal, jnp.concatenate([slab] * per_block, axis=0), 0.0)
            full = full.astype(BF16)
            wn[b, tap * LANES : (tap + 1) * LANES, :] = full
            wt[b, :, tap * LANES : (tap + 1) * LANES] = full
        return carry

    lax.fori_loop(0, blocks, build, 0)
    xs, gs = r["xs"], r["gs"]
    x_pair.wait_recv()
    store_shifted(xs, both, cols, xa[...], cols)

    def diagonal_col(row, first):
        lane = iota((anchors_dev, LANES), 1)
        hit = lane == iota((anchors_dev, LANES), 0) + first
        return jnp.sum(jnp.where(hit, row, 0.0), axis=1, keepdims=True)

    def pick_of(row, owner):
        column = diagonal_col(row, anchors_dev) + (owner * pixels).astype(F32)
        return jnp.where(iota((anchors_dev, both), 1).astype(F32) == column, 1.0, 0.0)

    pick_own = pick_of(posb[core, chip], core)

    @pl.when(jnp.logical_not(has_prev))
    def _():
        xh[0] = jnp.zeros(xh.shape[1:], xh.dtype)

    @pl.when(jnp.logical_not(has_next))
    def _():
        xh[1] = jnp.zeros(xh.shape[1:], xh.dtype)

    def x_edges_wait(q):
        lane = slice(q * wide, (q + 1) * wide)
        for slot, present in ((0, has_prev), (1, has_next)):
            view = xh.at[slot, :, pl.ds(q * wide, wide)]
            copy = remote(view, view, "xh", partner, at=slot * 2 + q, sent=0)

            @pl.when(present)
            def _():
                copy.wait_recv()

        store_shifted(xs, cols, 0, xh[0, :, lane], cols, lane)
        store_shifted(xs, cols, cols + both, xh[1, :, lane], cols, lane)

    def windows(buf, lane, flip):
        parts = []
        for row in range(3):
            for col in range(3):
                rr, cc = (2 - row, 2 - col) if flip else (row, col)
                parts.append(buf[cc, rr * cols : rr * cols + both, lane])
        return jnp.concatenate(parts, axis=1)

    mixed, mixed_t, slope, proj_ref = r["mixed"], r["mixed_t"], r["slope"], r["proj"]

    def forward(b, carry):
        lane = pl.ds(pl.multiple_of(b * LANES, LANES), LANES)
        pre = mm(windows(xs, lane, False), wn[b], NN)
        sig = 1.0 / (1.0 + jnp.exp(-pre))
        mixed[:, lane] = (xa[:, lane].astype(F32) + pre * sig).astype(BF16)
        slope[:, lane] = sig * (1.0 + pre * (1.0 - sig))
        return carry

    for q in range(2):
        x_edges_wait(q)
        lax.fori_loop(q * blocks // 2, (q + 1) * blocks // 2, forward, 0, unroll=True)

    rks, rkr = r["rks"], r["rkr"]
    rks[...] = mm(mixed[...], proj_ref[...], NN)
    rk_pair = remote(rks, rkr, "rk", partner)
    rk_pair.start()
    from_chips(posb.at[core], "pos")
    pos_pair = remote(posb.at[core], posb.at[core], "posp", partner)
    pos_pair.start()
    rk_pair.wait_recv()
    raw_key = rks[...] + rkr[...]
    norm_key = jnp.sqrt(jnp.sum(raw_key * raw_key, axis=1, keepdims=True) + EPSILON)
    unit_key = raw_key / norm_key
    keys = unit_key.astype(BF16)
    qall = r["qall"]
    qall[core, chip] = mm(pick_own.astype(BF16), keys, NN).astype(BF16)
    to_chips(lambda t: qall.at[core, chip], qall.at[core, chip], "q")

    slope_edge, slope_far = r["slope_edge"], r["slope_far"]
    slope_edge[0] = slope[:cols, :].astype(BF16)
    slope_edge[1] = slope[both - cols :, :].astype(BF16)
    slope_edges = edges(slope_edge, slope_far, "sh")
    edges_start(slope_edges)

    def hits(parity):
        own_lane = iota((chips, anchors_dev, LANES), 1) == iota((chips, anchors_dev, LANES), 2)
        pos_all = jnp.sum(jnp.where(own_lane, posb[parity], 0.0), axis=2, keepdims=True)
        pos_local = pos_all - (chip * both).astype(F32)
        hit3 = jnp.where(
            iota((chips, anchors_dev, both), 2).astype(F32) == pos_local, 1.0, 0.0
        )
        return hit3.reshape(anchors_core, both).astype(BF16)

    hit_own = hits(core)
    part_pos = mm(hit_own, keys, NN)
    pps, ppr = r["pps"], r["ppr"]
    pps[...] = part_pos.reshape(chips, anchors_dev, LANES).astype(BF16)
    ppr[chip] = pps[chip]

    def flip_over(b, carry):
        start = pl.multiple_of(b * LANES, LANES)
        lane = pl.ds(start, LANES)
        at[b] = windows(xs, lane, False).T
        mixed_t[lane, :] = mixed[:, lane].T
        return carry

    lax.fori_loop(0, blocks, flip_over, 0, unroll=True)
    to_chips(lambda t: pps.at[t], ppr.at[chip], "pp")

    from_chips(qall.at[core], "q")
    q_pair = remote(qall.at[core], qall.at[core], "qp", partner)
    q_pair.start()
    queries = qall[core].reshape(anchors_core, LANES)
    exp_own = jnp.exp(mm(keys, queries, NT) / SOFTMAX_TEMPER)
    part_total = jnp.sum(exp_own, axis=0, keepdims=True)
    pos_sum = jnp.sum(
        jnp.sum(part_pos * queries.astype(F32), axis=1, keepdims=True), axis=0, keepdims=True
    )
    totb, tfin = r["totb"], r["tfin"]
    tot_rows = anchors_core // LANES
    for n in range(tot_rows):
        totb[chip, n : n + 1, :] = part_total[:, n * LANES : (n + 1) * LANES]
    totb[chip, tot_rows : tot_rows + 1, :] = jnp.broadcast_to(pos_sum, (1, LANES))
    to_chips(lambda t: totb.at[chip], totb.at[chip], "tot")
    part_weighted = mm(exp_own.astype(BF16), keys, TN)
    ws, wr = r["ws"], r["wr"]
    ws[...] = part_weighted.reshape(chips, anchors_dev, LANES).astype(BF16)
    to_chips(lambda t: ws.at[t], wr.at[chip], "wp")
    wr[chip] = ws[chip]
    pos_pair.wait_recv()
    hit_other = hits(other)
    pick_other = pick_of(posb[other, chip], other)

    q_pair.wait_recv()
    queries_other = qall[other].reshape(anchors_core, LANES)
    exp_other = jnp.exp(mm(keys, queries_other, NT) / SOFTMAX_TEMPER)
    pushed = mm(hit_own, queries, TN) + mm(hit_other, queries_other, TN)

    def whole_row(sums):
        return jnp.concatenate([sums[n : n + 1, :] for n in range(tot_rows)], axis=1)

    def loss_of(sums, row):
        return jnp.sum(jnp.log(row), axis=1, keepdims=True) - sums[
            tot_rows : tot_rows + 1, 0:1
        ] / SOFTMAX_TEMPER

    def pulled_by(exp_scores, row, asked):
        inverse = (1.0 / row).astype(BF16).astype(F32)
        return mm((exp_scores * inverse).astype(BF16), asked, NN)

    from_chips(totb, "tot")
    sums_own = jnp.sum(totb[...], axis=0)
    tfin[core] = sums_own
    tot_pair = remote(tfin.at[core], tfin.at[core], "totp", partner)
    tot_pair.start()
    row_own = whole_row(sums_own)
    mine = iota((anchors_dev, anchors_core), 1) == chip * anchors_dev + iota(
        (anchors_dev, anchors_core), 0
    )
    own_total = jnp.sum(jnp.where(mine, row_own, 0.0), axis=1, keepdims=True)
    gq = r["gq"]
    from_chips(ppr, "pp")
    from_chips(wr, "wp")
    weighted = jnp.sum(wr[...].astype(F32), axis=0)
    pos_key = jnp.sum(ppr[...].astype(F32), axis=0)
    gq[core] = (weighted / own_total - pos_key) * gradient_scale
    gq_pair = remote(gq.at[core], gq.at[core], "gqp", partner)
    gq_pair.start()
    pulled = pulled_by(exp_own, row_own, queries)
    tot_pair.wait_recv()
    sums_other = tfin[other]
    row_other = whole_row(sums_other)
    pulled = pulled + pulled_by(exp_other, row_other, queries_other)
    grad_key = gradient_scale * (pulled - pushed)
    gq_pair.wait_recv()
    grad_key = grad_key + mm(pick_own, gq[core], TN, lax.Precision.HIGHEST)
    grad_key = grad_key + mm(pick_other, gq[other], TN, lax.Precision.HIGHEST)
    along = jnp.sum(grad_key * unit_key, axis=1, keepdims=True)
    grad_raw = ((grad_key - unit_key * along) / norm_key).astype(BF16)
    grad_mixed = mm(grad_raw, proj_ref[...], NT).astype(BF16)
    gm, gr = r["gm"], r["gr"]
    gm[...] = grad_mixed
    gr[...] = grad_raw
    gp[...] = (grad_mixed.astype(F32) * slope[...]).astype(BF16)

    raw_edge, raw_far = r["raw_edge"], r["raw_far"]
    raw_edge[0] = grad_raw[:cols]
    raw_edge[1] = grad_raw[both - cols :]
    raw_edges = edges(raw_edge, raw_far, "gh")
    l2a_s, l2a_r, l2b_s, l2b_r = r["l2a_s"], r["l2a_r"], r["l2b_s"], r["l2b_r"]
    l3a_s, l3a_r, l3b_s, l3b_r = r["l3a_s"], r["l3a_r"], r["l3b_s"], r["l3b_r"]
    lane_group = iota((group, LANES), 1) // group
    own_block = layer // span

    def block_at(k):
        return jnp.where(k == blocks - 1, own_block, away(k, blocks, own_block))


    def weight_grad(k, carry):
        b = block_at(k)
        lane = pl.ds(pl.multiple_of(b * LANES, LANES), LANES)
        proj_part = mm(mixed_t[lane, :], gr[...], NN)
        full = mm(at[b], gp[:, lane], NN)
        taps = []
        for tap in range(tap_count):
            folded = jnp.zeros((group, LANES), F32)
            for g in range(per_block):
                first = tap * LANES + g * group
                folded = jnp.where(lane_group == g, full[first : first + group], folded)
            taps.append(folded)
        short = pieces * piece - tap_count * group
        if short:
            taps.append(jnp.zeros((short, LANES), F32))
        conv = jnp.concatenate(taps, axis=0)
        for j in range(pieces):
            z, p = b * span + j // inner, j % inner
            top = j * piece
            l2a_s[p, z, :prow, :] = proj_part[j * prow : (j + 1) * prow].astype(BF16)
            l2a_s[p, z, prow:, :] = conv[top : top + conv_a].astype(BF16)
            l2b_s[z, p] = conv[top + conv_a : top + piece].astype(BF16)
        for j in range(span):
            z = b * span + j
            across(
                lambda t: remote(
                    l2a_s.at[t, z], l2a_r.at[place, z], "l2a", near_id(t), at=z
                ).start(),
            )
            l2a_r[place, z] = l2a_s[place, z]

            @pl.when(z != layer)
            def _():
                remote(l2b_s.at[z], l2b_r.at[layer], "l2b", far_id(z)).start()

        return carry

    lax.fori_loop(0, blocks, weight_grad, 0)
    edges_start(raw_edges)
    r["loss"][...] = (loss_of(sums_own, row_own) + loss_of(sums_other, row_other)) / anchor_count
    l2b_r[layer] = l2b_s[layer]
    store_shifted(gs, both, cols, gp[...], cols)

    def near_summed(k, carry):
        z = block_at(k // span) * span + lax.rem(k, span)
        view = l2a_r.at[pl.ds(0, inner - 1), z]
        remote(view, view, "l2a", partner, at=z).wait_recv()
        l3a_s[z] = jnp.sum(l2a_r[:, z].astype(F32), axis=0).astype(BF16)

        @pl.when(z != layer)
        def _():
            remote(l3a_s.at[z], l3a_r.at[layer], "l3a", far_id(z)).start()

        return carry

    lax.fori_loop(0, layers, near_summed, 0)
    l3a_r[layer] = l3a_s[layer]
    view = l2b_r.at[pl.ds(0, layers - 1)]
    remote(view, view, "l2b", partner).wait_recv()
    for p in range(inner):
        l3b_s[p] = jnp.sum(l2b_r[:, p].astype(F32), axis=0).astype(BF16)
    turn(
        inner,
        place,
        lambda t: remote(l3b_s.at[t], l3b_r.at[place], "l3b", near_id(t)).start(),
    )
    l3b_r[place] = l3b_s[place]

    view = l3a_r.at[pl.ds(0, layers - 1)]
    remote(view, view, "l3a", partner).wait_recv()
    ag_a[core, layer, place] = jnp.sum(l3a_r[...].astype(F32), axis=0).astype(BF16)

    def a_copy(z, at, name, target):
        chunk = ag_a.at[core, z, place]
        return remote(chunk, chunk, name, target, at=at)

    def b_copy(p, at, name, target):
        chunk = ag_b.at[core, p, layer]
        return remote(chunk, chunk, name, target, at=at)

    farthest(layers, layer, lambda t: a_copy(layer, layer, "af", far_id(t)).start())

    view = l3b_r.at[pl.ds(0, inner - 1)]
    remote(view, view, "l3b", partner).wait_recv()
    ag_b[core, place, layer] = jnp.sum(l3b_r[...].astype(F32), axis=0).astype(BF16)
    rise(inner, place, lambda t: b_copy(place, place, "bn", near_id(t)).start())
    rise(inner, place, lambda t: a_copy(layer, layer, "an", near_id(t)).start())
    farthest(layers, layer, lambda t: b_copy(place, place, "bf", far_id(t)).start())

    edges_wait(slope_edges, slope_far)
    edges_wait(raw_edges, raw_far)
    for slot in range(2):
        edge = mm(raw_far[slot], proj_ref[...], NT).astype(BF16).astype(F32)
        edge = (edge * slope_far[slot].astype(F32)).astype(BF16)
        store_shifted(gs, cols, slot * (cols + both), edge, cols)
    back_all = r["back"]

    def backward(b, carry):
        lane = pl.ds(pl.multiple_of(b * LANES, LANES), LANES)
        back = mm(windows(gs, lane, True), wt[b], NT).astype(BF16)
        back_all[:, lane] = (back.astype(F32) + gm[:, lane].astype(F32)).astype(BF16)
        return carry

    lax.fori_loop(0, blocks, backward, 0, unroll=True)
    out_pair = remote(
        back_all.at[pl.ds(pl.multiple_of(other * pixels, 16), pixels)],
        out_ref.at[:, my_half],
        "out",
        partner,
    )
    out_pair.start()
    out_ref[:, my_half] = back_all[my_pixels, :]

    def a_arrived(z):
        chunk = ag_a.at[core, z, place]
        remote(chunk, chunk, "af", partner, at=z).wait_recv()
        rise(inner, place, lambda t: a_copy(z, z, "an", near_id(t)).start())

    def b_arrived(p):
        chunk = ag_b.at[core, p, layer]
        remote(chunk, chunk, "bn", partner, at=p).wait_recv()
        farthest(layers, layer, lambda t: b_copy(p, p, "bf", far_id(t)).start())

    nearest(layers, layer, a_arrived)
    rise(inner, place, b_arrived)

    def a_whole(k, carry):
        z = jnp.where(k == 0, layer, away(layers - 1 - k, layers, layer))
        view = ag_a.at[core, z, pl.ds(0, inner - 1)]
        remote(view, view, "an", partner, at=z).wait_recv()
        remote(ag_a.at[core, z], ag_a.at[core, z], "ap", partner).start()
        return carry

    def b_whole(k, carry):
        p = lax.rem(place + k, inner)
        view = ag_b.at[core, p, pl.ds(0, layers - 1)]
        remote(view, view, "bf", partner, at=p).wait_recv()
        remote(ag_b.at[core, p], ag_b.at[core, p], "bp", partner).start()
        return carry

    lax.fori_loop(0, layers, a_whole, 0)
    lax.fori_loop(0, inner, b_whole, 0)

    @pl.when(sends_up)
    def _():
        for copy in up_edge:
            copy.wait_send()

    @pl.when(sends_down)
    def _():
        for copy in down_edge:
            copy.wait_send()

    edges_sent(slope_edges)
    edges_sent(raw_edges)

    for copy in (pos_pair, tot_pair):
        copy.wait_send()
    sent_chips(posb.at[core], "pos")
    sent_chips(totb, "tot")

    def sent(view, name, at=None):
        remote(view, view, name, partner, at=at).wait_send()

    sent(r["main_all"], "out")
    sent(r["rest_all"], "bp")
    out_pair.wait_recv()
    remote(ag_a.at[other], ag_a.at[other], "ap", partner).wait_recv()
    remote(ag_b.at[other], ag_b.at[other], "bp", partner).wait_recv()


def finish(geometry, gf_ref, ag_a, ag_b, loss_ref, gf_out, gw_out, gp_out, loss_out, gw, gp, sems):
    blocks, inner, pieces, piece, prow = geometry
    _, layers, _, rows_a, _ = ag_a.shape
    chips = layers * inner
    moves = [pltpu.make_async_copy(gf_ref, gf_out, sems.at[0])]
    moves[0].start()
    moves.append(pltpu.make_async_copy(loss_ref, loss_out, sems.at[2 + pieces]))
    moves[-1].start()
    height = gw_out.shape[0]
    conv_a = rows_a - prow
    for j in range(pieces):
        first = j * piece
        stop = min(height, first + piece)
        for b in range(blocks):
            side, i = b // (blocks // 2), b % (blocks // 2) * pieces + j
            lane = slice(b * LANES, (b + 1) * LANES)
            z, p = i // inner, i % inner
            first_p = (side * chips + i) * prow
            gp[first_p : first_p + prow, :] = ag_a[side, z, p, :prow, :].astype(F32)
            top = min(conv_a, max(stop - first, 0))
            if top > 0:
                gw[first : first + top, lane] = ag_a[side, z, p, prow : prow + top, :].astype(F32)
            low = stop - first - conv_a
            if low > 0:
                gw[first + conv_a : stop, lane] = ag_b[side, p, z, :low, :].astype(F32)
        if stop > first:
            rows = pl.ds(first, stop - first)
            moves.append(pltpu.make_async_copy(gw.at[rows], gw_out.at[rows], sems.at[2 + j]))
            moves[-1].start()
    moves.append(pltpu.make_async_copy(gp, gp_out, sems.at[1]))
    moves[-1].start()
    for move in moves:
        move.wait()


def per_device(devices, batches, features, conv_weight, proj_weight, anchor_pixel, positive_pixel):
    rows_dev, cols, images, channels = features.shape
    group = conv_weight.shape[2]
    key_width = proj_weight.shape[1]
    anchors_dev = anchor_pixel.shape[0]
    chips = devices // 2
    inner = min(4, chips)
    layers = chips // inner
    pixels = rows_dev * cols
    both = 2 * pixels
    half = channels // 2
    taps = conv_weight.shape[0] * conv_weight.shape[1]
    blocks = half // LANES
    pieces = chips // blocks
    piece = -(-(taps * group) // pieces)
    piece = -(-piece // 8) * 8
    prow = channels // devices
    rows_a = (prow + piece) * 5 // 8 // 16 * 16
    rows_b = prow + piece - rows_a
    anchors_core = anchors_dev * chips
    anchor_count = anchors_core * 2 * images * batches
    gradient_scale = 1.0 / (SOFTMAX_TEMPER * anchor_count)
    tot_rows = anchors_core // LANES + 1
    padded = both + 2 * cols
    dma = pltpu.SemaphoreType.DMA
    vmem = pltpu.VMEM
    whole = pl.BlockSpec(memory_space=pltpu.VMEM)
    hbm = pl.BlockSpec(memory_space=pltpu.HBM)
    part = (chips, anchors_dev, LANES)
    scratch = {
        "xa": vmem((both, half), BF16),
        "w": vmem((taps, group, half), BF16),
        "proj": vmem((half, key_width), BF16),
        "anchor": vmem((1, anchors_dev), jnp.int32),
        "positive": vmem((1, anchors_dev), jnp.int32),
        "xh": vmem((2, cols, half), BF16),
        "slope_edge": vmem((2, cols, half), BF16),
        "slope_far": vmem((2, cols, half), BF16),
        "raw_edge": vmem((2, cols, key_width), BF16),
        "raw_far": vmem((2, cols, key_width), BF16),
        "xs": vmem((3, padded, half), BF16),
        "gs": vmem((3, padded, half), BF16),
        "wn": vmem((blocks, taps * LANES, LANES), BF16),
        "wt": vmem((blocks, LANES, taps * LANES), BF16),
        "at": vmem((blocks, taps * LANES, both), BF16),
        "mixed": vmem((both, half), BF16),
        "mixed_t": vmem((half, both), BF16),
        "slope": vmem((both, half), F32),
        "rks": vmem((both, key_width), F32),
        "rkr": vmem((both, key_width), F32),
        "posb": vmem((2, chips, 1, LANES), F32),
        "qall": vmem((2, *part), BF16),
        "pps": vmem(part, BF16),
        "ppr": vmem(part, BF16),
        "ws": vmem(part, BF16),
        "wr": vmem(part, BF16),
        "totb": vmem((chips, tot_rows, LANES), F32),
        "tfin": vmem((2, tot_rows, LANES), F32),
        "gq": vmem((2, anchors_dev, LANES), F32),
        "gm": vmem((both, half), BF16),
        "gp": vmem((both, half), BF16),
        "gr": vmem((both, key_width), BF16),
        "back": vmem((both, half), BF16),
        "l2a_s": vmem((inner, layers, rows_a, LANES), BF16),
        "l2a_r": vmem((inner, layers, rows_a, LANES), BF16),
        "l2b_s": vmem((layers, inner, rows_b, LANES), BF16),
        "l2b_r": vmem((layers, inner, rows_b, LANES), BF16),
        "l3a_s": vmem((layers, rows_a, LANES), BF16),
        "l3a_r": vmem((layers, rows_a, LANES), BF16),
        "l3b_s": vmem((inner, rows_b, LANES), BF16),
        "l3b_r": vmem((inner, rows_b, LANES), BF16),
        "xf": vmem((pixels, channels), BF16),
        "load": dma((6,)),
    }
    chunks_a = 2 * layers * (inner - 1) + 2 * (layers - 1) + chips
    chunks_b = 2 * inner * (layers - 1) + 2 * (inner - 1) + chips
    sent_rows = 2 * pixels * half // LANES + 2 * both + 2 * anchors_dev
    sent_rows += (4 * chips - 3) * anchors_dev + chunks_a * rows_a
    scratch["main_all"] = vmem((sent_rows, LANES), BF16)
    scratch["rest_all"] = vmem((chunks_b, rows_b, LANES), BF16)
    for name in ("main", "rest", "pos", "posp", "tot", "totp"):
        scratch[name + "_send"] = dma
    singles = ("xp", "rk", "pos", "posp", "q", "qp", "pp", "tot", "totp", "wp", "gqp")
    for name in (*singles, "l2b", "l3a", "l3b", "out", "ap", "bp"):
        scratch[name + "_recv"] = dma
    for name, count in (("xh", 4), ("sh", 2), ("gh", 2)):
        scratch[name + "_send"] = dma((count,))
        scratch[name + "_recv"] = dma((count,))
    for name, count in (("l2a", layers), ("af", layers), ("an", layers), ("bn", inner), ("bf", inner)):
        scratch[name + "_recv"] = dma((count,))
    names = ["x_hbm", "w_hbm", "proj_hbm", "anchor_hbm", "positive_hbm"]
    names += ["out", "ag_a", "ag_b", "loss", *scratch]
    sums = (
        jax.ShapeDtypeStruct((pixels, channels), BF16),
        jax.ShapeDtypeStruct((2, layers, inner, rows_a, LANES), BF16),
        jax.ShapeDtypeStruct((2, inner, layers, rows_b, LANES), BF16),
        jax.ShapeDtypeStruct((1, 1), F32),
    )
    parts = pl.pallas_call(
        functools.partial(
            kernel,
            names,
            devices,
            gradient_scale,
            (cols, group, pieces, piece, prow, inner, anchor_count),
        ),
        out_shape=sums,
        in_specs=[hbm] * 5,
        out_specs=(whole,) * 4,
        scratch_shapes=list(scratch.values()),
        compiler_params=pltpu.CompilerParams(
            collective_id=0, has_side_effects=True, vmem_limit_bytes=26000 * 1024
        ),
    )(
        in_hbm(features.reshape(pixels, channels)),
        in_hbm(conv_weight.reshape(taps, group, channels)),
        in_hbm(proj_weight),
        in_hbm(anchor_pixel.reshape(1, anchors_dev)),
        in_hbm(positive_pixel.reshape(1, anchors_dev)),
    )
    grad_features, grad_conv, grad_proj, loss = pl.pallas_call(
        functools.partial(finish, (2 * blocks, inner, pieces, piece, prow)),
        out_shape=(
            jax.ShapeDtypeStruct((pixels, channels), BF16),
            jax.ShapeDtypeStruct((taps * group, channels), F32),
            jax.ShapeDtypeStruct((channels, key_width), F32),
            jax.ShapeDtypeStruct((1, 1), F32),
        ),
        in_specs=[whole] * 4,
        out_specs=(hbm,) * 4,
        scratch_shapes=[
            vmem((taps * group, channels), F32),
            vmem((channels, key_width), F32),
            dma((3 + pieces,)),
        ],
        compiler_params=pltpu.CompilerParams(vmem_limit_bytes=16000 * 1024),
    )(*parts)
    grad_conv = grad_conv.reshape(conv_weight.shape)
    loss_value = loss.reshape(())
    if batches > 1:
        grad_conv, grad_proj, loss_value = lax.psum((grad_conv, grad_proj, loss_value), "batch")
    return (grad_features.reshape(features.shape), grad_conv, grad_proj, loss_value)


def solution(mesh):
    placed = (P("wide", None, "batch", None), P(), P(), P("wide", "batch"), P("wide", "batch"))
    return jax.shard_map(
        functools.partial(per_device, mesh.shape["wide"], mesh.shape["batch"]),
        mesh=mesh,
        in_specs=placed,
        out_specs=(P("wide", None, "batch", None), P(), P(), P()),
        check_vma=False,
    )
```

```python
import functools

import jax
import jax.numpy as jnp
from jax import lax
from jax.experimental import pallas as pl
from jax.experimental.pallas import tpu as pltpu
from jax.sharding import PartitionSpec as P

SOFTMAX_TEMPER = 0.1
EPSILON = 1e-06
LANES = 128
F32 = jnp.float32
BF16 = jnp.bfloat16
MESH = pl.DeviceIdType.MESH

NN = (((1,), (0,)), ((), ()))
NT = (((1,), (1,)), ((), ()))
TN = (((0,), (0,)), ((), ()))


def mm(a, b, dims, precision=None):
    return lax.dot_general(a, b, dims, preferred_element_type=F32, precision=precision)


def in_hbm(array):
    return pltpu.with_memory_space_constraint(array, pltpu.HBM)


def iota(shape, dim):
    return lax.broadcasted_iota(jnp.int32, shape, dim)


def store_shifted(dst, rows, start, values, cols, lane=slice(None)):
    wide = values.astype(F32)
    count = wide.shape[0]
    col = iota(wide.shape, 0) % cols
    dst[1, start : start + rows, lane] = values
    left = jnp.where(col == 0, 0.0, pltpu.roll(wide, 1, 0))
    dst[0, start : start + rows, lane] = left.astype(BF16)
    right = jnp.where(col == cols - 1, 0.0, pltpu.roll(wide, count - 1, 0))
    dst[2, start : start + rows, lane] = right.astype(BF16)


def kernel(names, devices, gradient_scale, geometry, *refs):
    r = dict(zip(names, refs, strict=True))
    cols, group, pieces, piece, prow, inner, anchor_count = geometry
    x_hbm, out_ref, ag_a, ag_b = r["x_hbm"], r["out"], r["ag_a"], r["ag_b"]
    pixels = x_hbm.shape[0]
    channels = x_hbm.shape[1]
    half = channels // 2
    blocks = half // LANES
    per_block = LANES // group
    anchors_dev = r["anchor"].shape[1]
    chips = devices // 2
    both = 2 * pixels
    anchors_core = chips * anchors_dev
    me = lax.axis_index("wide")
    core = lax.rem(me, 2)
    chip = me // 2
    other = 1 - core
    partner = chip * 2 + other
    place = lax.rem(chip, inner)
    layer = chip // inner
    layers = chips // inner
    span = pieces // inner
    conv_a = ag_a.shape[3] - prow
    barrier = pltpu.get_barrier_semaphore()

    def turn(count, start, body):
        def step(k, carry):
            body(lax.rem(start + k, count))
            return carry

        lax.fori_loop(1, count, step, 0)

    def away(k, count, own):
        down = count - 1 - k
        down = down - (down <= own).astype(jnp.int32)
        up = k + (k >= own).astype(jnp.int32)
        return jnp.where(2 * own < count, down, up)

    def farthest(count, own, body):
        def step(k, carry):
            body(away(k, count, own))
            return carry

        lax.fori_loop(0, count - 1, step, 0)

    def nearest(count, own, body):
        farthest_last = count - 2

        def step(k, carry):
            body(away(farthest_last - k, count, own))
            return carry

        lax.fori_loop(0, count - 1, step, 0)

    def across(body):
        body(inner - 1 - place)
        body(place + 1 - 2 * lax.rem(place, 2))
        body(place + 2 - 4 * (place // 2))

    def rise(count, start, body):
        def step(k, carry):
            body(k + (k >= start).astype(jnp.int32))
            return carry

        lax.fori_loop(0, count - 1, step, 0)

    def other_chips(body):
        def layer_step(k, carry):
            z = jnp.where(layer < layers // 2, layers - 1 - k, k)

            def step(j, carry):
                t = z * inner + lax.rem(place + inner - 1 - j, inner)

                @pl.when(t != chip)
                def _():
                    body(t)

                return carry

            return lax.fori_loop(0, inner, step, carry, unroll=True)

        lax.fori_loop(0, layers, layer_step, 0)

    def near_id(target):
        return (layer * inner + target) * 2 + core

    def far_id(target):
        return (target * inner + place) * 2 + core

    def remote(src, dst, name, target, at=None, sent=None):
        recv = r[name + "_recv"]
        send = r[name + "_send"]
        return pltpu.make_async_remote_copy(
            src_ref=src,
            dst_ref=dst,
            send_sem=send if sent is None else send.at[sent],
            recv_sem=recv if at is None else recv.at[at],
            device_id={"wide": target},
            device_id_type=MESH,
        )

    def to_chips(source, landing, name):
        other_chips(lambda t: remote(source(t), landing, name, t * 2 + core).start())

    def from_chips(buf, name):
        view = buf.at[pl.ds(0, chips - 1)]
        remote(view, view, name, partner).wait_recv()

    def sent_chips(buf, name):
        view = buf.at[pl.ds(0, chips - 1)]
        remote(view, view, name, partner).wait_send()

    def signal_entry(target):
        pl.semaphore_signal(barrier, inc=1, device_id={"wide": target}, device_id_type=MESH)

    has_prev = chip > 0
    has_next = chip < chips - 1
    previous = lax.rem(chip + chips - 1, chips)
    following = lax.rem(chip + 1, chips)
    my_half = pl.ds(pl.multiple_of(core * half, LANES), half)
    your_half = pl.ds(pl.multiple_of(other * half, LANES), half)
    my_pixels = pl.ds(pl.multiple_of(core * pixels, 16), pixels)

    loads = [
        pltpu.make_async_copy(src, dst, r["load"].at[n])
        for n, (src, dst) in enumerate(
            (
                (x_hbm, r["xf"]),
                (r["positive_hbm"], r["positive"]),
                (r["w_hbm"].at[:, :, my_half], r["w"]),
                (x_hbm.at[:, my_half], r["xa"].at[my_pixels]),
                (r["proj_hbm"].at[my_half], r["proj"]),
                (r["anchor_hbm"], r["anchor"]),
            )
        )
    ]
    for copy in loads:
        copy.start()

    @pl.when(has_prev)
    def _():
        signal_entry(previous * 2 + other)

    @pl.when(has_next)
    def _():
        signal_entry(following * 2 + other)

    signal_entry(partner)

    def greet(k, carry):
        signal_entry(lax.rem(chip + k, chips) * 2 + core)
        signal_entry(lax.rem(chip + chips - k, chips) * 2 + core)
        return carry

    lax.fori_loop(1, chips // 2, greet, 0)
    signal_entry(lax.rem(chip + chips // 2, chips) * 2 + core)
    loads[0].wait()
    xf = r["xf"]
    pl.semaphore_wait(barrier, chips + has_prev.astype(jnp.int32) + has_next.astype(jnp.int32))

    xh, xa, gp = r["xh"], r["xa"], r["gp"]

    wide = half // 2

    def x_edge(source, slot, target):
        return [
            remote(
                xf.at[pl.ds(source, cols), pl.ds(t * half + q * wide, wide)],
                xh.at[slot, :, pl.ds(q * wide, wide)],
                "xh",
                target * 2 + t,
                at=slot * 2 + q,
                sent=q * 2 + t,
            )
            for q in range(2)
            for t in range(2)
        ]

    up_edge = x_edge(0, 1, previous)
    down_edge = x_edge(pixels - cols, 0, following)
    sends_up = jnp.logical_and(core == 0, has_prev)
    sends_down = jnp.logical_and(core == 1, has_next)

    @pl.when(sends_up)
    def _():
        for copy in up_edge:
            copy.start()

    @pl.when(sends_down)
    def _():
        for copy in down_edge:
            copy.start()

    x_pair = remote(xf.at[:, your_half], xa.at[my_pixels], "xp", partner)
    x_pair.start()

    def edges(src, buf, name):
        up = remote(src.at[0], buf.at[1], name, previous * 2 + core, at=1, sent=0)
        down = remote(src.at[1], buf.at[0], name, following * 2 + core, at=0, sent=1)
        return up, down

    def edges_start(copies):
        for copy, present in zip(copies, (has_prev, has_next), strict=True):
            pl.when(present)(copy.start)

    def edges_sent(copies):
        for copy, present in zip(copies, (has_prev, has_next), strict=True):
            pl.when(present)(copy.wait_send)

    def edges_wait(copies, buf):
        up, down = copies

        @pl.when(has_prev)
        def _():
            down.wait_recv()

        @pl.when(jnp.logical_not(has_prev))
        def _():
            buf[0] = jnp.zeros(buf.shape[1:], buf.dtype)

        @pl.when(has_next)
        def _():
            up.wait_recv()

        @pl.when(jnp.logical_not(has_next))
        def _():
            buf[1] = jnp.zeros(buf.shape[1:], buf.dtype)

    for copy in loads[1:]:
        copy.wait()
    posb = r["posb"]
    posb[core, chip, :, :anchors_dev] = r["positive"][...].astype(F32)
    posb[core, chip, :, anchors_dev : 2 * anchors_dev] = r["anchor"][...].astype(F32)
    posb[core, chip, :, 2 * anchors_dev :] = jnp.zeros((1, LANES - 2 * anchors_dev), F32)
    to_chips(lambda t: posb.at[core, chip], posb.at[core, chip], "pos")

    w_ref, wn, wt, at = r["w"], r["wn"], r["wt"], r["at"]
    tap_count = w_ref.shape[0]
    diagonal = iota((LANES, LANES), 0) // group == iota((LANES, LANES), 1) // group

    def build(b, carry):
        lane = pl.ds(pl.multiple_of(b * LANES, LANES), LANES)
        for tap in range(tap_count):
            slab = w_ref[tap, :, lane].astype(F32)
            full = jnp.where(diagonal, jnp.concatenate([slab] * per_block, axis=0), 0.0)
            full = full.astype(BF16)
            wn[b, tap * LANES : (tap + 1) * LANES, :] = full
            wt[b, :, tap * LANES : (tap + 1) * LANES] = full
        return carry

    lax.fori_loop(0, blocks, build, 0)
    xs, gs = r["xs"], r["gs"]
    x_pair.wait_recv()
    store_shifted(xs, both, cols, xa[...], cols)

    def diagonal_col(row, first):
        lane = iota((anchors_dev, LANES), 1)
        hit = lane == iota((anchors_dev, LANES), 0) + first
        return jnp.sum(jnp.where(hit, row, 0.0), axis=1, keepdims=True)

    def pick_of(row, owner):
        column = diagonal_col(row, anchors_dev) + (owner * pixels).astype(F32)
        return jnp.where(iota((anchors_dev, both), 1).astype(F32) == column, 1.0, 0.0)

    pick_own = pick_of(posb[core, chip], core)

    @pl.when(jnp.logical_not(has_prev))
    def _():
        xh[0] = jnp.zeros(xh.shape[1:], xh.dtype)

    @pl.when(jnp.logical_not(has_next))
    def _():
        xh[1] = jnp.zeros(xh.shape[1:], xh.dtype)

    def x_edges_wait(q):
        lane = slice(q * wide, (q + 1) * wide)
        for slot, present in ((0, has_prev), (1, has_next)):
            view = xh.at[slot, :, pl.ds(q * wide, wide)]
            copy = remote(view, view, "xh", partner, at=slot * 2 + q, sent=0)

            @pl.when(present)
            def _():
                copy.wait_recv()

        store_shifted(xs, cols, 0, xh[0, :, lane], cols, lane)
        store_shifted(xs, cols, cols + both, xh[1, :, lane], cols, lane)

    def windows(buf, lane, flip):
        parts = []
        for row in range(3):
            for col in range(3):
                rr, cc = (2 - row, 2 - col) if flip else (row, col)
                parts.append(buf[cc, rr * cols : rr * cols + both, lane])
        return jnp.concatenate(parts, axis=1)

    mixed, mixed_t, slope, proj_ref = r["mixed"], r["mixed_t"], r["slope"], r["proj"]

    def forward(b, carry):
        lane = pl.ds(pl.multiple_of(b * LANES, LANES), LANES)
        pre = mm(windows(xs, lane, False), wn[b], NN)
        sig = 1.0 / (1.0 + jnp.exp(-pre))
        mixed[:, lane] = (xa[:, lane].astype(F32) + pre * sig).astype(BF16)
        slope[:, lane] = sig * (1.0 + pre * (1.0 - sig))
        return carry

    for q in range(2):
        x_edges_wait(q)
        lax.fori_loop(q * blocks // 2, (q + 1) * blocks // 2, forward, 0, unroll=True)

    rks, rkr = r["rks"], r["rkr"]
    rks[...] = mm(mixed[...], proj_ref[...], NN)
    rk_pair = remote(rks, rkr, "rk", partner)
    rk_pair.start()
    from_chips(posb.at[core], "pos")
    pos_pair = remote(posb.at[core], posb.at[core], "posp", partner)
    pos_pair.start()
    rk_pair.wait_recv()
    raw_key = rks[...] + rkr[...]
    norm_key = jnp.sqrt(jnp.sum(raw_key * raw_key, axis=1, keepdims=True) + EPSILON)
    unit_key = raw_key / norm_key
    keys = unit_key.astype(BF16)
    qall = r["qall"]
    qall[core, chip] = mm(pick_own.astype(BF16), keys, NN).astype(BF16)
    to_chips(lambda t: qall.at[core, chip], qall.at[core, chip], "q")

    def hits(parity):
        own_lane = iota((chips, anchors_dev, LANES), 1) == iota((chips, anchors_dev, LANES), 2)
        pos_all = jnp.sum(jnp.where(own_lane, posb[parity], 0.0), axis=2, keepdims=True)
        pos_local = pos_all - (chip * both).astype(F32)
        hit3 = jnp.where(
            iota((chips, anchors_dev, both), 2).astype(F32) == pos_local, 1.0, 0.0
        )
        return hit3.reshape(anchors_core, both).astype(BF16)

    hit_own = hits(core)
    part_pos = mm(hit_own, keys, NN)
    pps, ppr = r["pps"], r["ppr"]
    pps[...] = part_pos.reshape(chips, anchors_dev, LANES).astype(BF16)
    ppr[chip] = pps[chip]

    def flip_over(b, carry):
        start = pl.multiple_of(b * LANES, LANES)
        lane = pl.ds(start, LANES)
        at[b] = windows(xs, lane, False).T
        mixed_t[lane, :] = mixed[:, lane].T
        return carry

    lax.fori_loop(0, blocks, flip_over, 0, unroll=True)
    to_chips(lambda t: pps.at[t], ppr.at[chip], "pp")
    slope_edge, slope_far = r["slope_edge"], r["slope_far"]
    slope_edge[0] = slope[:cols, :].astype(BF16)
    slope_edge[1] = slope[both - cols :, :].astype(BF16)
    slope_edges = edges(slope_edge, slope_far, "sh")
    edges_start(slope_edges)


    from_chips(qall.at[core], "q")
    q_pair = remote(qall.at[core], qall.at[core], "qp", partner)
    q_pair.start()
    queries = qall[core].reshape(anchors_core, LANES)
    exp_own = jnp.exp(mm(keys, queries, NT) / SOFTMAX_TEMPER)
    part_total = jnp.sum(exp_own, axis=0, keepdims=True)
    pos_sum = jnp.sum(
        jnp.sum(part_pos * queries.astype(F32), axis=1, keepdims=True), axis=0, keepdims=True
    )
    totb, tfin = r["totb"], r["tfin"]
    tot_rows = anchors_core // LANES
    for n in range(tot_rows):
        totb[chip, n : n + 1, :] = part_total[:, n * LANES : (n + 1) * LANES]
    totb[chip, tot_rows : tot_rows + 1, :] = jnp.broadcast_to(pos_sum, (1, LANES))
    to_chips(lambda t: totb.at[chip], totb.at[chip], "tot")
    part_weighted = mm(exp_own.astype(BF16), keys, TN)
    ws, wr = r["ws"], r["wr"]
    ws[...] = part_weighted.reshape(chips, anchors_dev, LANES).astype(BF16)
    to_chips(lambda t: ws.at[t], wr.at[chip], "wp")
    wr[chip] = ws[chip]
    pos_pair.wait_recv()
    hit_other = hits(other)
    pick_other = pick_of(posb[other, chip], other)

    q_pair.wait_recv()
    queries_other = qall[other].reshape(anchors_core, LANES)
    exp_other = jnp.exp(mm(keys, queries_other, NT) / SOFTMAX_TEMPER)
    pushed = mm(hit_own, queries, TN) + mm(hit_other, queries_other, TN)

    def whole_row(sums):
        return jnp.concatenate([sums[n : n + 1, :] for n in range(tot_rows)], axis=1)

    def loss_of(sums, row):
        return jnp.sum(jnp.log(row), axis=1, keepdims=True) - sums[
            tot_rows : tot_rows + 1, 0:1
        ] / SOFTMAX_TEMPER

    def pulled_by(exp_scores, row, asked):
        inverse = (1.0 / row).astype(BF16).astype(F32)
        return mm((exp_scores * inverse).astype(BF16), asked, NN)

    from_chips(totb, "tot")
    sums_own = jnp.sum(totb[...], axis=0)
    tfin[core] = sums_own
    tot_pair = remote(tfin.at[core], tfin.at[core], "totp", partner)
    tot_pair.start()
    row_own = whole_row(sums_own)
    mine = iota((anchors_dev, anchors_core), 1) == chip * anchors_dev + iota(
        (anchors_dev, anchors_core), 0
    )
    own_total = jnp.sum(jnp.where(mine, row_own, 0.0), axis=1, keepdims=True)
    gq = r["gq"]
    from_chips(ppr, "pp")
    from_chips(wr, "wp")
    weighted = jnp.sum(wr[...].astype(F32), axis=0)
    pos_key = jnp.sum(ppr[...].astype(F32), axis=0)
    gq[core] = (weighted / own_total - pos_key) * gradient_scale
    gq_pair = remote(gq.at[core], gq.at[core], "gqp", partner)
    gq_pair.start()
    pulled = pulled_by(exp_own, row_own, queries)
    tot_pair.wait_recv()
    sums_other = tfin[other]
    row_other = whole_row(sums_other)
    pulled = pulled + pulled_by(exp_other, row_other, queries_other)
    grad_key = gradient_scale * (pulled - pushed)
    gq_pair.wait_recv()
    grad_key = grad_key + mm(pick_own, gq[core], TN, lax.Precision.HIGHEST)
    grad_key = grad_key + mm(pick_other, gq[other], TN, lax.Precision.HIGHEST)
    along = jnp.sum(grad_key * unit_key, axis=1, keepdims=True)
    grad_raw = ((grad_key - unit_key * along) / norm_key).astype(BF16)
    grad_mixed = mm(grad_raw, proj_ref[...], NT).astype(BF16)
    gm, gr = r["gm"], r["gr"]
    gm[...] = grad_mixed
    gr[...] = grad_raw
    gp[...] = (grad_mixed.astype(F32) * slope[...]).astype(BF16)

    raw_edge, raw_far = r["raw_edge"], r["raw_far"]
    raw_edge[0] = grad_raw[:cols]
    raw_edge[1] = grad_raw[both - cols :]
    raw_edges = edges(raw_edge, raw_far, "gh")
    l2a_s, l2a_r, l2b_s, l2b_r = r["l2a_s"], r["l2a_r"], r["l2b_s"], r["l2b_r"]
    l3a_s, l3a_r, l3b_s, l3b_r = r["l3a_s"], r["l3a_r"], r["l3b_s"], r["l3b_r"]
    lane_group = iota((group, LANES), 1) // group
    own_block = layer // span

    def block_at(k):
        return jnp.where(k == blocks - 1, own_block, away(k, blocks, own_block))


    def weight_grad(k, carry):
        b = block_at(k)
        lane = pl.ds(pl.multiple_of(b * LANES, LANES), LANES)
        proj_part = mm(mixed_t[lane, :], gr[...], NN)
        full = mm(at[b], gp[:, lane], NN)
        taps = []
        for tap in range(tap_count):
            folded = jnp.zeros((group, LANES), F32)
            for g in range(per_block):
                first = tap * LANES + g * group
                folded = jnp.where(lane_group == g, full[first : first + group], folded)
            taps.append(folded)
        short = pieces * piece - tap_count * group
        if short:
            taps.append(jnp.zeros((short, LANES), F32))
        conv = jnp.concatenate(taps, axis=0)
        for j in range(pieces):
            z, p = b * span + j // inner, j % inner
            top = j * piece
            l2a_s[p, z, :prow, :] = proj_part[j * prow : (j + 1) * prow].astype(BF16)
            l2a_s[p, z, prow:, :] = conv[top : top + conv_a].astype(BF16)
            l2b_s[z, p] = conv[top + conv_a : top + piece].astype(BF16)
        for j in range(span):
            z = b * span + j
            across(
                lambda t: remote(
                    l2a_s.at[t, z], l2a_r.at[place, z], "l2a", near_id(t), at=z
                ).start(),
            )
            l2a_r[place, z] = l2a_s[place, z]

            @pl.when(z != layer)
            def _():
                remote(l2b_s.at[z], l2b_r.at[layer], "l2b", far_id(z)).start()

        return carry

    lax.fori_loop(0, blocks, weight_grad, 0)
    edges_start(raw_edges)
    r["loss"][...] = (loss_of(sums_own, row_own) + loss_of(sums_other, row_other)) / anchor_count
    l2b_r[layer] = l2b_s[layer]
    store_shifted(gs, both, cols, gp[...], cols)

    def near_summed(k, carry):
        z = block_at(k // span) * span + lax.rem(k, span)
        view = l2a_r.at[pl.ds(0, inner - 1), z]
        remote(view, view, "l2a", partner, at=z).wait_recv()
        l3a_s[z] = jnp.sum(l2a_r[:, z].astype(F32), axis=0).astype(BF16)

        @pl.when(z != layer)
        def _():
            remote(l3a_s.at[z], l3a_r.at[layer], "l3a", far_id(z)).start()

        return carry

    lax.fori_loop(0, layers, near_summed, 0)
    l3a_r[layer] = l3a_s[layer]
    view = l2b_r.at[pl.ds(0, layers - 1)]
    remote(view, view, "l2b", partner).wait_recv()
    for p in range(inner):
        l3b_s[p] = jnp.sum(l2b_r[:, p].astype(F32), axis=0).astype(BF16)
    turn(
        inner,
        place,
        lambda t: remote(l3b_s.at[t], l3b_r.at[place], "l3b", near_id(t)).start(),
    )
    l3b_r[place] = l3b_s[place]

    view = l3a_r.at[pl.ds(0, layers - 1)]
    remote(view, view, "l3a", partner).wait_recv()
    ag_a[core, layer, place] = jnp.sum(l3a_r[...].astype(F32), axis=0).astype(BF16)

    def a_copy(z, at, name, target):
        chunk = ag_a.at[core, z, place]
        return remote(chunk, chunk, name, target, at=at)

    def b_copy(p, at, name, target):
        chunk = ag_b.at[core, p, layer]
        return remote(chunk, chunk, name, target, at=at)

    farthest(layers, layer, lambda t: a_copy(layer, layer, "af", far_id(t)).start())

    view = l3b_r.at[pl.ds(0, inner - 1)]
    remote(view, view, "l3b", partner).wait_recv()
    ag_b[core, place, layer] = jnp.sum(l3b_r[...].astype(F32), axis=0).astype(BF16)
    rise(inner, place, lambda t: b_copy(place, place, "bn", near_id(t)).start())
    rise(inner, place, lambda t: a_copy(layer, layer, "an", near_id(t)).start())
    farthest(layers, layer, lambda t: b_copy(place, place, "bf", far_id(t)).start())

    edges_wait(slope_edges, slope_far)
    edges_wait(raw_edges, raw_far)
    for slot in range(2):
        edge = mm(raw_far[slot], proj_ref[...], NT).astype(BF16).astype(F32)
        edge = (edge * slope_far[slot].astype(F32)).astype(BF16)
        store_shifted(gs, cols, slot * (cols + both), edge, cols)
    back_all = r["back"]

    def backward(b, carry):
        lane = pl.ds(pl.multiple_of(b * LANES, LANES), LANES)
        back = mm(windows(gs, lane, True), wt[b], NT).astype(BF16)
        back_all[:, lane] = (back.astype(F32) + gm[:, lane].astype(F32)).astype(BF16)
        return carry

    lax.fori_loop(0, blocks, backward, 0, unroll=True)
    out_pair = remote(
        back_all.at[pl.ds(pl.multiple_of(other * pixels, 16), pixels)],
        out_ref.at[:, my_half],
        "out",
        partner,
    )
    out_pair.start()
    out_ref[:, my_half] = back_all[my_pixels, :]

    def a_arrived(z):
        chunk = ag_a.at[core, z, place]
        remote(chunk, chunk, "af", partner, at=z).wait_recv()
        rise(inner, place, lambda t: a_copy(z, z, "an", near_id(t)).start())

    def b_arrived(p):
        chunk = ag_b.at[core, p, layer]
        remote(chunk, chunk, "bn", partner, at=p).wait_recv()
        farthest(layers, layer, lambda t: b_copy(p, p, "bf", far_id(t)).start())

    nearest(layers, layer, a_arrived)
    rise(inner, place, b_arrived)

    def a_whole(k, carry):
        z = jnp.where(k == 0, layer, away(layers - 1 - k, layers, layer))
        view = ag_a.at[core, z, pl.ds(0, inner - 1)]
        remote(view, view, "an", partner, at=z).wait_recv()
        remote(ag_a.at[core, z], ag_a.at[core, z], "ap", partner).start()
        return carry

    def b_whole(k, carry):
        p = lax.rem(place + k, inner)
        view = ag_b.at[core, p, pl.ds(0, layers - 1)]
        remote(view, view, "bf", partner, at=p).wait_recv()
        remote(ag_b.at[core, p], ag_b.at[core, p], "bp", partner).start()
        return carry

    lax.fori_loop(0, layers, a_whole, 0)
    lax.fori_loop(0, inner, b_whole, 0)

    @pl.when(sends_up)
    def _():
        for copy in up_edge:
            copy.wait_send()

    @pl.when(sends_down)
    def _():
        for copy in down_edge:
            copy.wait_send()

    edges_sent(slope_edges)
    edges_sent(raw_edges)

    for copy in (x_pair, rk_pair, pos_pair, q_pair, tot_pair, gq_pair):
        copy.wait_send()
    sent_chips(posb.at[core], "pos")
    sent_chips(qall.at[core], "q")
    sent_chips(pps, "pp")
    sent_chips(totb, "tot")
    sent_chips(ws, "wp")

    def sent(view, name, at=None):
        remote(view, view, name, partner, at=at).wait_send()

    sent(l2a_s.at[pl.ds(0, inner - 1)], "l2a", 0)
    sent(l2b_s.at[pl.ds(0, layers - 1)], "l2b")
    sent(l3a_s.at[pl.ds(0, layers - 1)], "l3a")
    sent(l3b_s.at[pl.ds(0, inner - 1)], "l3b")
    sent(ag_a.at[core, pl.ds(0, layers - 1), 0], "af", 0)
    sent(ag_a.at[core, :, pl.ds(0, inner - 1)], "an", 0)
    sent(ag_b.at[core, pl.ds(0, inner - 1), 0], "bn", 0)
    sent(ag_b.at[core, :, pl.ds(0, layers - 1)], "bf", 0)
    out_pair.wait()
    sent(ag_a.at[core], "ap")
    sent(ag_b.at[core], "bp")
    remote(ag_a.at[other], ag_a.at[other], "ap", partner).wait_recv()
    remote(ag_b.at[other], ag_b.at[other], "bp", partner).wait_recv()


def finish(geometry, gf_ref, ag_a, ag_b, loss_ref, gf_out, gw_out, gp_out, loss_out, gw, gp, sems):
    blocks, inner, pieces, piece, prow = geometry
    _, layers, _, rows_a, _ = ag_a.shape
    chips = layers * inner
    moves = [pltpu.make_async_copy(gf_ref, gf_out, sems.at[0])]
    moves[0].start()
    moves.append(pltpu.make_async_copy(loss_ref, loss_out, sems.at[2 + pieces]))
    moves[-1].start()
    height = gw_out.shape[0]
    conv_a = rows_a - prow
    for j in range(pieces):
        first = j * piece
        stop = min(height, first + piece)
        for b in range(blocks):
            side, i = b // (blocks // 2), b % (blocks // 2) * pieces + j
            lane = slice(b * LANES, (b + 1) * LANES)
            z, p = i // inner, i % inner
            first_p = (side * chips + i) * prow
            gp[first_p : first_p + prow, :] = ag_a[side, z, p, :prow, :].astype(F32)
            top = min(conv_a, max(stop - first, 0))
            if top > 0:
                gw[first : first + top, lane] = ag_a[side, z, p, prow : prow + top, :].astype(F32)
            low = stop - first - conv_a
            if low > 0:
                gw[first + conv_a : stop, lane] = ag_b[side, p, z, :low, :].astype(F32)
        if stop > first:
            rows = pl.ds(first, stop - first)
            moves.append(pltpu.make_async_copy(gw.at[rows], gw_out.at[rows], sems.at[2 + j]))
            moves[-1].start()
    moves.append(pltpu.make_async_copy(gp, gp_out, sems.at[1]))
    moves[-1].start()
    for move in moves:
        move.wait()


def per_device(devices, batches, features, conv_weight, proj_weight, anchor_pixel, positive_pixel):
    rows_dev, cols, images, channels = features.shape
    group = conv_weight.shape[2]
    key_width = proj_weight.shape[1]
    anchors_dev = anchor_pixel.shape[0]
    chips = devices // 2
    inner = min(4, chips)
    layers = chips // inner
    pixels = rows_dev * cols
    both = 2 * pixels
    half = channels // 2
    taps = conv_weight.shape[0] * conv_weight.shape[1]
    blocks = half // LANES
    pieces = chips // blocks
    piece = -(-(taps * group) // pieces)
    piece = -(-piece // 8) * 8
    prow = channels // devices
    rows_a = (prow + piece) * 5 // 8 // 16 * 16
    rows_b = prow + piece - rows_a
    anchors_core = anchors_dev * chips
    anchor_count = anchors_core * 2 * images * batches
    gradient_scale = 1.0 / (SOFTMAX_TEMPER * anchor_count)
    tot_rows = anchors_core // LANES + 1
    padded = both + 2 * cols
    dma = pltpu.SemaphoreType.DMA
    vmem = pltpu.VMEM
    whole = pl.BlockSpec(memory_space=pltpu.VMEM)
    hbm = pl.BlockSpec(memory_space=pltpu.HBM)
    part = (chips, anchors_dev, LANES)
    scratch = {
        "xa": vmem((both, half), BF16),
        "w": vmem((taps, group, half), BF16),
        "proj": vmem((half, key_width), BF16),
        "anchor": vmem((1, anchors_dev), jnp.int32),
        "positive": vmem((1, anchors_dev), jnp.int32),
        "xh": vmem((2, cols, half), BF16),
        "slope_edge": vmem((2, cols, half), BF16),
        "slope_far": vmem((2, cols, half), BF16),
        "raw_edge": vmem((2, cols, key_width), BF16),
        "raw_far": vmem((2, cols, key_width), BF16),
        "xs": vmem((3, padded, half), BF16),
        "gs": vmem((3, padded, half), BF16),
        "wn": vmem((blocks, taps * LANES, LANES), BF16),
        "wt": vmem((blocks, LANES, taps * LANES), BF16),
        "at": vmem((blocks, taps * LANES, both), BF16),
        "mixed": vmem((both, half), BF16),
        "mixed_t": vmem((half, both), BF16),
        "slope": vmem((both, half), F32),
        "rks": vmem((both, key_width), F32),
        "rkr": vmem((both, key_width), F32),
        "posb": vmem((2, chips, 1, LANES), F32),
        "qall": vmem((2, *part), BF16),
        "pps": vmem(part, BF16),
        "ppr": vmem(part, BF16),
        "ws": vmem(part, BF16),
        "wr": vmem(part, BF16),
        "totb": vmem((chips, tot_rows, LANES), F32),
        "tfin": vmem((2, tot_rows, LANES), F32),
        "gq": vmem((2, anchors_dev, LANES), F32),
        "gm": vmem((both, half), BF16),
        "gp": vmem((both, half), BF16),
        "gr": vmem((both, key_width), BF16),
        "back": vmem((both, half), BF16),
        "l2a_s": vmem((inner, layers, rows_a, LANES), BF16),
        "l2a_r": vmem((inner, layers, rows_a, LANES), BF16),
        "l2b_s": vmem((layers, inner, rows_b, LANES), BF16),
        "l2b_r": vmem((layers, inner, rows_b, LANES), BF16),
        "l3a_s": vmem((layers, rows_a, LANES), BF16),
        "l3a_r": vmem((layers, rows_a, LANES), BF16),
        "l3b_s": vmem((inner, rows_b, LANES), BF16),
        "l3b_r": vmem((inner, rows_b, LANES), BF16),
        "xf": vmem((pixels, channels), BF16),
        "load": dma((6,)),
    }
    singles = ("xp", "rk", "pos", "posp", "q", "qp", "pp", "tot", "totp", "wp", "gqp")
    for name in (*singles, "l2b", "l3a", "l3b", "out", "ap", "bp"):
        scratch[name + "_send"] = dma
        scratch[name + "_recv"] = dma
    for name, count in (("xh", 4), ("sh", 2), ("gh", 2)):
        scratch[name + "_send"] = dma((count,))
        scratch[name + "_recv"] = dma((count,))
    for name, count in (("l2a", layers), ("af", layers), ("an", layers), ("bn", inner), ("bf", inner)):
        scratch[name + "_send"] = dma
        scratch[name + "_recv"] = dma((count,))
    names = ["x_hbm", "w_hbm", "proj_hbm", "anchor_hbm", "positive_hbm"]
    names += ["out", "ag_a", "ag_b", "loss", *scratch]
    sums = (
        jax.ShapeDtypeStruct((pixels, channels), BF16),
        jax.ShapeDtypeStruct((2, layers, inner, rows_a, LANES), BF16),
        jax.ShapeDtypeStruct((2, inner, layers, rows_b, LANES), BF16),
        jax.ShapeDtypeStruct((1, 1), F32),
    )
    parts = pl.pallas_call(
        functools.partial(
            kernel,
            names,
            devices,
            gradient_scale,
            (cols, group, pieces, piece, prow, inner, anchor_count),
        ),
        out_shape=sums,
        in_specs=[hbm] * 5,
        out_specs=(whole,) * 4,
        scratch_shapes=list(scratch.values()),
        compiler_params=pltpu.CompilerParams(
            collective_id=0, has_side_effects=True, vmem_limit_bytes=26000 * 1024
        ),
    )(
        in_hbm(features.reshape(pixels, channels)),
        in_hbm(conv_weight.reshape(taps, group, channels)),
        in_hbm(proj_weight),
        in_hbm(anchor_pixel.reshape(1, anchors_dev)),
        in_hbm(positive_pixel.reshape(1, anchors_dev)),
    )
    grad_features, grad_conv, grad_proj, loss = pl.pallas_call(
        functools.partial(finish, (2 * blocks, inner, pieces, piece, prow)),
        out_shape=(
            jax.ShapeDtypeStruct((pixels, channels), BF16),
            jax.ShapeDtypeStruct((taps * group, channels), F32),
            jax.ShapeDtypeStruct((channels, key_width), F32),
            jax.ShapeDtypeStruct((1, 1), F32),
        ),
        in_specs=[whole] * 4,
        out_specs=(hbm,) * 4,
        scratch_shapes=[
            vmem((taps * group, channels), F32),
            vmem((channels, key_width), F32),
            dma((3 + pieces,)),
        ],
        compiler_params=pltpu.CompilerParams(vmem_limit_bytes=16000 * 1024),
    )(*parts)
    grad_conv = grad_conv.reshape(conv_weight.shape)
    loss_value = loss.reshape(())
    if batches > 1:
        grad_conv, grad_proj, loss_value = lax.psum((grad_conv, grad_proj, loss_value), "batch")
    return (grad_features.reshape(features.shape), grad_conv, grad_proj, loss_value)


def solution(mesh):
    placed = (P("wide", None, "batch", None), P(), P(), P("wide", "batch"), P("wide", "batch"))
    return jax.shard_map(
        functools.partial(per_device, mesh.shape["wide"], mesh.shape["batch"]),
        mesh=mesh,
        in_specs=placed,
        out_specs=(P("wide", None, "batch", None), P(), P(), P()),
        check_vma=False,
    )
```
